32 devices in a mesh: dp: 4 (over y, x), ctx: 4 (over z), tensor: 2 (over core).
Axes of the slice: x: 2, y: 2, z: 4, core: 2. Of those that a mesh axis runs over, the one named last changes fastest.
Arguments:
- hidden: bfloat16 [4, 1024, 1024], P('dp', 'ctx'), may hold values from -6 to 6
- segment_ids: int32 [4, 1024], P('dp', 'ctx'), may hold values from 0 to 5, as said below
- cotangent: bfloat16 [4, 1024, 1024], P('dp', 'ctx'), may hold values from -6 to 6
- input_gain: float32 [1024], replicated, may hold values from 0.5 to 1.5
- gate_weight: bfloat16 [1024, 2048], P('dp', 'tensor'), may hold values from -0.1875 to 0.1875
- value_weight: bfloat16 [1024, 2048], P('dp', 'tensor'), may hold values from -0.1875 to 0.1875
- state_weight: bfloat16 [1024, 256], P('dp'), may hold values from -0.1875 to 0.1875
- step_weight: bfloat16 [1024, 32], P('dp', 'tensor'), may hold values from -0.1875 to 0.1875
- conv_weight: float32 [4, 2304], replicated, may hold values from -3 to 3
- conv_bias: float32 [2304], replicated, may hold values from -3 to 3
- step_bias: float32 [32], replicated, may hold values from -4 to -1
- decay_log: float32 [32], replicated, may hold values from -6.5 to -1.5
- skip_gain: float32 [32], replicated, may hold values from 0.5 to 1.5
- mixer_gain: float32 [2048], replicated, may hold values from 0.5 to 1.5
- out_weight: bfloat16 [2048, 1024], P('tensor', 'dp'), may hold values from -0.125 to 0.125
Outputs:
- output: bfloat16 [4, 1024, 1024], P('dp', 'ctx')
- grad_hidden: float32 [4, 1024, 1024], P('dp', 'ctx')
- grad_input_gain: float32 [1024], replicated
- grad_gate_weight: float32 [1024, 2048], P('dp', 'tensor')
- grad_value_weight: float32 [1024, 2048], P('dp', 'tensor')
- grad_state_weight: float32 [1024, 256], P('dp')
- grad_step_weight: float32 [1024, 32], P('dp', 'tensor')
- grad_conv_weight: float32 [4, 2304], replicated
- grad_conv_bias: float32 [2304], replicated
- grad_step_bias: float32 [32], replicated
- grad_decay_log: float32 [32], replicated
- grad_skip_gain: float32 [32], replicated
- grad_mixer_gain: float32 [2048], replicated
- grad_out_weight: float32 [2048, 1024], P('tensor', 'dp')
The draws below stay inside these ranges and needn't reach their ends.
Inputs may be any that keep to these rules, and one draw needn't show every extreme that they name: `segment_ids`: within each sequence the ids start at 0, never fall and rise by one at each new document. Every document has 200 to 512 tokens, except the last one of a sequence, which may be cut short by the sequence's end. The first document of the first sequence has exactly 512 tokens; every document of the last sequence has exactly 200 tokens (the final one possibly cut short).
All inputs are finite; a program needn't handle non-finite values.
Results may differ from the reference program's by a relative error of at most 0.014.
Values may be sent and summed in bfloat16 or wider, within the bound.
A program may use at most 192 MiB of HBM per device.

```python
from functools import partial
import jax
import jax.numpy as jnp
from jax import lax

D = 1024
NH = 32
HD = 64
NS = 128
CW = 4
GROUP = 128
DOC_MIN = 200
DI = 2048
SEQ = 1024
DOC_MAX = 512
SEQS = 4


def draw_segment_ids(key, part):
    count = SEQ // DOC_MIN + 1
    lengths = jax.random.randint(jax.random.fold_in(key, 17), (SEQS, count), DOC_MIN, DOC_MAX + 1)
    lengths = lengths.at[0, 0].set(DOC_MAX)
    lengths = lengths.at[SEQS - 1, :].set(jnp.full((count,), DOC_MIN, jnp.int32))
    ends = jnp.cumsum(lengths, axis=1)
    position = jnp.arange(SEQ, dtype=jnp.int32)
    return jnp.sum((position[None, :, None] >= ends[:, None, :]).astype(jnp.int32), axis=2).astype(jnp.int32)


def block_scale(rng, extent, cuts, low, largest):
    def one(dim, shards_of):
        steps = jax.random.uniform(jax.random.fold_in(jax.random.fold_in(rng, 6), dim), (shards_of,), jnp.float32, low / len(cuts), largest / len(cuts))
        return jnp.repeat(jnp.exp(steps), extent[dim] // shards_of).reshape((-1,) + (1,) * (len(extent) - dim - 1))

    gain = one(*cuts[0])
    for cut in cuts[1:]:
        gain = gain * one(*cut)
    return gain


def scatter_about(own_key, extent, width, bound, cuts=(), kind=jnp.bfloat16):
    array = width * jax.random.normal(own_key, extent, jnp.float32)
    if cuts:
        array = array * block_scale(own_key, extent, cuts, -0.22, 0.18)
    return jnp.clip(array, -bound, bound).astype(kind)


def setup_inputs(seed: int = 0) -> dict:
    arg_keys = jax.random.split(jax.random.key(seed), 16)
    return {
        "hidden": scatter_about(arg_keys[0], (SEQS, SEQ, D), 1.0, 6.0, ((0, 4), (1, 4))),
        "segment_ids": draw_segment_ids(jax.random.fold_in(arg_keys[15], 71), 0),
        "cotangent": scatter_about(arg_keys[2], (SEQS, SEQ, D), 1.0, 6.0, ((0, 4), (1, 4))),
        "input_gain": jnp.clip(1.0 + 0.1 * jax.random.normal(arg_keys[3], (D,), jnp.float32), 0.5, 1.5),
        "gate_weight": scatter_about(arg_keys[4], (D, DI), D ** -0.5, 0.1875, ((0, 4), (1, 2))),
        "value_weight": scatter_about(arg_keys[5], (D, DI), D ** -0.5, 0.1875, ((0, 4), (1, 2))),
        "state_weight": scatter_about(arg_keys[6], (D, 2 * NS), D ** -0.5, 0.1875, ((0, 4),)),
        "step_weight": scatter_about(arg_keys[7], (D, NH), D ** -0.5, 0.1875, ((0, 4), (1, 2))),
        "conv_weight": scatter_about(arg_keys[8], (CW, DI + 2 * NS), CW ** -0.5, 3.0, (), jnp.float32),
        "conv_bias": scatter_about(arg_keys[9], (DI + 2 * NS,), 0.5, 3.0, (), jnp.float32),
        "step_bias": jnp.clip(jax.random.uniform(arg_keys[10], (NH,), jnp.float32, -4.0, -1.0), -4.0, -1.0),
        "decay_log": jnp.clip(jax.random.uniform(arg_keys[11], (NH,), jnp.float32, -6.5, -1.5), -6.5, -1.5),
        "skip_gain": jnp.clip(1.0 + 0.1 * jax.random.normal(arg_keys[12], (NH,), jnp.float32), 0.5, 1.5),
        "mixer_gain": jnp.clip(1.0 + 0.1 * jax.random.normal(arg_keys[13], (DI,), jnp.float32), 0.5, 1.5),
        "out_weight": scatter_about(arg_keys[14], (DI, D), DI ** -0.5, 0.125, ((0, 2), (1, 4))),
    }


epsilon = 1e-05
highest = lax.Precision.HIGHEST

def rms_scale(values, scaling):
    return values * lax.rsqrt(lax.optimization_barrier(jnp.mean(values * values, axis=-1, keepdims=True)) + epsilon) * scaling

def causal_conv(padded, padded_ids, segments, kernel, offset):
    reach = kernel.shape[0] - 1
    length = segments.shape[0]
    total = jnp.broadcast_to(offset[None, :], (length, offset.shape[0]))
    for lag in range(reach + 1):
        begin = reach - lag
        window = padded[begin:begin + length]
        same = (padded_ids[begin:begin + length] == segments).astype(jnp.float32)
        total = total + kernel[lag][None, :] * window * same[:, None]
    return total

def group_step(carry, item, rates):
    values, inputs_b, inputs_c, delta, segments, previous = item
    log_decay = delta * rates[None, :]
    running = jnp.cumsum(log_decay, axis=0)
    length = segments.shape[0]
    order = jnp.arange(length)
    allowed = (segments[:, None] == segments[None, :]) & (order[:, None] >= order[None, :])
    spread = running.T[:, :, None] - running.T[:, None, :]
    decay = jnp.where(allowed[None], jnp.exp(jnp.where(allowed[None], spread, 0.0)), 0.0)
    scores = jnp.dot(inputs_c, inputs_b.T, precision=highest)
    mixing = decay * scores[None] * delta.T[:, None, :]
    inner = jnp.einsum('hts,shp->thp', mixing, values, precision=highest)
    entry = jnp.exp(running) * (segments == previous).astype(jnp.float32)[:, None]
    carried = jnp.einsum('tn,hpn->thp', inputs_c, carry, precision=highest) * entry[:, :, None]
    tail = jnp.exp(running[-1][None, :] - running) * (segments == segments[-1]).astype(jnp.float32)[:, None] * delta
    fade = jnp.exp(running[-1]) * (segments[-1] == previous).astype(jnp.float32)
    update = jnp.einsum('sh,shp,sn->hpn', tail, values, inputs_b, precision=highest)
    return (carry * fade[:, None, None] + update, inner + carried)

def mixer(conv_input, raw_step, gate, kernel, offset, step_bias, decay_log, skip_gain, mixer_gain, segments):
    length = conv_input.shape[0]
    reach = kernel.shape[0] - 1
    padded = jnp.concatenate([jnp.zeros((reach, conv_input.shape[1]), jnp.float32), conv_input], 0)
    padded_ids = jnp.concatenate([jnp.full((reach,), -1, jnp.int32), segments])
    activated = jax.nn.silu(causal_conv(padded, padded_ids, segments, kernel, offset))
    inner_width = NH * HD
    values = activated[:, :inner_width].reshape(length, NH, HD)
    inputs_b = activated[:, inner_width:inner_width + NS]
    inputs_c = activated[:, inner_width + NS:]
    delta = jax.nn.softplus(raw_step + step_bias[None, :])
    rates = -jnp.exp(decay_log)
    count = length // GROUP
    previous = jnp.concatenate([(segments[0] - 1)[None], segments[GROUP - 1::GROUP][:count - 1]]).astype(jnp.int32)
    items = (values.reshape(count, GROUP, NH, HD), inputs_b.reshape(count, GROUP, NS), inputs_c.reshape(count, GROUP, NS), delta.reshape(count, GROUP, NH), segments.reshape(count, GROUP), previous)
    stepper = jax.checkpoint(partial(group_step, rates=rates))
    final, outputs = lax.scan(stepper, jnp.zeros((NH, HD, NS), jnp.float32), items)
    mixed = outputs.reshape(length, NH, HD) + skip_gain[None, :, None] * values
    mixed = mixed.reshape(length, inner_width)
    product = mixed * jax.nn.silu(gate)
    return rms_scale(product, mixer_gain)

def reference(hidden, segment_ids, cotangent, input_gain, gate_weight, value_weight, state_weight, step_weight, conv_weight, conv_bias, step_bias, decay_log, skip_gain, mixer_gain, out_weight):
    inner_width = NH * HD

    def one(totals, item):
        tokens, segments, cotangent_rows = item
        base = tokens.astype(jnp.float32)
        normed_full, norm_back = jax.vjp(rms_scale, base, input_gain)
        normed = normed_full.astype(jnp.bfloat16)
        gate = jnp.dot(normed, gate_weight, preferred_element_type=jnp.float32)
        value_pre = jnp.dot(normed, value_weight, preferred_element_type=jnp.float32).astype(jnp.bfloat16)
        state_pre = jnp.dot(normed, state_weight, preferred_element_type=jnp.float32).astype(jnp.bfloat16)
        raw_step = jnp.dot(normed, step_weight, preferred_element_type=jnp.float32)
        conv_input = jnp.concatenate([value_pre, state_pre], 1).astype(jnp.float32)
        gated_full, mixer_back = jax.vjp(partial(mixer, segments=segments), conv_input, raw_step, gate, conv_weight, conv_bias, step_bias, decay_log, skip_gain, mixer_gain)
        gated = gated_full.astype(jnp.bfloat16)
        result = (base + jnp.dot(gated, out_weight, preferred_element_type=jnp.float32)).astype(jnp.bfloat16)
        grad_gated = jnp.dot(cotangent_rows, out_weight.T, preferred_element_type=jnp.float32)
        grad_out = jnp.dot(gated.T, cotangent_rows, preferred_element_type=jnp.float32)
        grad_input, grad_raw, grad_gate, grad_kernel, grad_offset, grad_bias, grad_decay, grad_skip, grad_mgain = mixer_back(grad_gated)
        low_gate = grad_gate.astype(jnp.bfloat16)
        low_input = grad_input.astype(jnp.bfloat16)
        low_step = grad_raw.astype(jnp.bfloat16)
        grad_normed = jnp.dot(low_gate, gate_weight.T, preferred_element_type=jnp.float32) + jnp.dot(low_input[:, :inner_width], value_weight.T, preferred_element_type=jnp.float32) + jnp.dot(low_input[:, inner_width:], state_weight.T, preferred_element_type=jnp.float32) + jnp.dot(low_step, step_weight.T, preferred_element_type=jnp.float32)
        grad_base, grad_gain = norm_back(grad_normed)
        grad_tokens = cotangent_rows.astype(jnp.float32) + grad_base
        terms = (grad_gain, jnp.dot(normed.T, low_gate, preferred_element_type=jnp.float32), jnp.dot(normed.T, low_input[:, :inner_width], preferred_element_type=jnp.float32), jnp.dot(normed.T, low_input[:, inner_width:], preferred_element_type=jnp.float32), jnp.dot(normed.T, low_step, preferred_element_type=jnp.float32), grad_kernel, grad_offset, grad_bias, grad_decay, grad_skip, grad_mgain, grad_out)
        totals = tuple((left + right for left, right in zip(totals, terms)))
        return (totals, (result, grad_tokens))
    start = (jnp.zeros((D,), jnp.float32), jnp.zeros((D, inner_width), jnp.float32), jnp.zeros((D, inner_width), jnp.float32), jnp.zeros((D, 2 * NS), jnp.float32), jnp.zeros((D, NH), jnp.float32), jnp.zeros((CW, inner_width + 2 * NS), jnp.float32), jnp.zeros((inner_width + 2 * NS,), jnp.float32), jnp.zeros((NH,), jnp.float32), jnp.zeros((NH,), jnp.float32), jnp.zeros((NH,), jnp.float32), jnp.zeros((inner_width,), jnp.float32), jnp.zeros((inner_width, D), jnp.float32))
    totals, (results, grad_rows) = lax.scan(one, start, (hidden, segment_ids, cotangent))
    return (results, grad_rows, totals[0], totals[1], totals[2], totals[3], totals[4], totals[5], totals[6], totals[7], totals[8], totals[9], totals[10], totals[11])
```

```python
from functools import partial

import jax
import jax.numpy as jnp
from jax import lax
from jax.experimental import pallas as pl
from jax.experimental.pallas import tpu as pltpu
from jax.sharding import PartitionSpec as P

epsilon = 1e-05
highest = lax.Precision.HIGHEST
f32, bf16 = jnp.float32, jnp.bfloat16
MESH = pl.DeviceIdType.MESH
VM = pl.BlockSpec(memory_space=pltpu.VMEM)
ANY = pl.BlockSpec(memory_space=pl.ANY)
LIMIT = 56 * 1024 * 1024


def dot(a, b, ca=1, cb=0, precision=None):
    return lax.dot_general(
        a, b, (((ca,), (cb,)), ((), ())), precision=precision, preferred_element_type=f32
    )


def shifted(array, axis, by):
    size = lax.axis_size(axis)
    pairs = [(i, i + by) for i in range(size) if 0 <= i + by < size]
    return lax.ppermute(array, axis, pairs)


def chain_kernel(axis, by, chunks, local_ref, fade_ref, out_ref, landed, outgoing, send, recv):
    size = lax.axis_size(axis)
    me = lax.axis_index(axis)
    follower = lax.rem(me + by + size, size)
    leader = lax.rem(me - by + size, size)
    first, last = (0, size - 1) if by > 0 else (size - 1, 0)
    rows = local_ref.shape[0] // chunks
    barrier = pltpu.get_barrier_semaphore()

    @pl.when(me != first)
    def _():
        pl.semaphore_signal(barrier, inc=1, device_id={axis: leader}, device_id_type=MESH)

    @pl.when(me != last)
    def _():
        pl.semaphore_wait(barrier, 1)

    def copy(c):
        part = pl.ds(c * rows, rows)
        return pltpu.make_async_remote_copy(
            src_ref=outgoing.at[part],
            dst_ref=landed.at[part],
            send_sem=send.at[c],
            recv_sem=recv.at[c],
            device_id={axis: follower},
            device_id_type=MESH,
        )

    @pl.when(me == first)
    def _():
        landed[...] = jnp.zeros_like(landed)

    for c in range(chunks):
        part = pl.ds(c * rows, rows)

        @pl.when(me != first)
        def _():
            copy(c).wait_recv()

        @pl.when(me != last)
        def _():
            total = fade_ref[part, :] * landed[part, :].astype(f32) + local_ref[part, :].astype(f32)
            outgoing[part, :] = total.astype(outgoing.dtype)
            copy(c).start()

    out_ref[...] = landed[...]

    @pl.when(me != last)
    def _():
        for c in range(chunks):
            copy(c).wait_send()


def chain(local, fade, axis, by, ident, chunks=4):
    return pl.pallas_call(
        partial(chain_kernel, axis, by, chunks),
        out_shape=jax.ShapeDtypeStruct(local.shape, local.dtype),
        in_specs=[VM, VM],
        out_specs=VM,
        scratch_shapes=[
            pltpu.VMEM(local.shape, local.dtype),
            pltpu.VMEM(local.shape, local.dtype),
            pltpu.SemaphoreType.DMA((chunks,)),
            pltpu.SemaphoreType.DMA((chunks,)),
        ],
        compiler_params=pltpu.CompilerParams(collective_id=ident, has_side_effects=True),
        name="chain",
    )(local, fade)


def pair_kernel(axis, src_ref, out_ref, slots, send, recv):
    size = lax.axis_size(axis)
    me = lax.axis_index(axis)
    barrier = pltpu.get_barrier_semaphore()
    for k in range(1, size):
        pl.semaphore_signal(
            barrier, inc=1, device_id={axis: lax.rem(me + k, size)}, device_id_type=MESH
        )
    pl.semaphore_wait(barrier, size - 1)
    copies = []
    for k in range(1, size):
        copies.append(
            pltpu.make_async_remote_copy(
                src_ref=src_ref,
                dst_ref=slots.at[k - 1],
                send_sem=send.at[k - 1],
                recv_sem=recv.at[k - 1],
                device_id={axis: lax.rem(me + k, size)},
                device_id_type=MESH,
            )
        )
        copies[-1].start()
    for copy in copies:
        copy.wait()
    total = src_ref[...].astype(f32)
    for k in range(1, size):
        total = total + slots[k - 1].astype(f32)
    out_ref[...] = total


def pair_sum(array, axis, ident):
    size = lax.axis_size(axis)
    return pl.pallas_call(
        partial(pair_kernel, axis),
        out_shape=jax.ShapeDtypeStruct(array.shape, f32),
        in_specs=[VM],
        out_specs=VM,
        scratch_shapes=[
            pltpu.VMEM((size - 1,) + array.shape, array.dtype),
            pltpu.SemaphoreType.DMA((size - 1,)),
            pltpu.SemaphoreType.DMA((size - 1,)),
        ],
        compiler_params=pltpu.CompilerParams(
            collective_id=ident, has_side_effects=True, vmem_limit_bytes=LIMIT
        ),
        name="pair_sum",
    )(array)


def gather_kernel(axis, count, *refs):
    ins, outs = refs[:count], refs[count : 2 * count]
    local, send, recv = refs[2 * count :]
    me = lax.axis_index(axis)
    low, high = lax.rem(me, 2), me // 2
    side = high * 2 + (1 - low)
    other = (1 - high) * 2 + low
    corner = (1 - high) * 2 + (1 - low)
    barrier = pltpu.get_barrier_semaphore()
    for peer in (side, other):
        pl.semaphore_signal(barrier, inc=1, device_id={axis: peer}, device_id_type=MESH)
    own = []
    for a in range(count):
        own.append(pltpu.make_async_copy(ins[a], outs[a].at[me], local.at[a]))
        own[-1].start()
    pl.semaphore_wait(barrier, 2)

    def remote(a, src, dst, slot, peer):
        return pltpu.make_async_remote_copy(
            src_ref=src,
            dst_ref=dst,
            send_sem=send.at[a, slot],
            recv_sem=recv.at[a, slot],
            device_id={axis: peer},
            device_id_type=MESH,
        )

    direct = []
    for a in range(count):
        for slot, peer in ((0, side), (1, other)):
            direct.append(remote(a, ins[a], outs[a].at[me], slot, peer))
            direct[-1].start()
    relays = []
    for a in range(count):
        half = ins[a].shape[0] // 2
        lower, upper = pl.ds(0, half), pl.ds(half, half)
        remote(a, ins[a], outs[a].at[side], 0, side).wait_recv()
        relay = remote(a, outs[a].at[side, lower], outs[a].at[side, lower], 2, other)
        relay.start()
        relays.append(relay)
        remote(a, ins[a], outs[a].at[other], 1, other).wait_recv()
        relay = remote(a, outs[a].at[other, upper], outs[a].at[other, upper], 3, side)
        relay.start()
        relays.append(relay)
    for a in range(count):
        half = ins[a].shape[0] // 2
        lower, upper = pl.ds(0, half), pl.ds(half, half)
        remote(a, outs[a].at[corner, lower], outs[a].at[corner, lower], 2, other).wait_recv()
        remote(a, outs[a].at[corner, upper], outs[a].at[corner, upper], 3, side).wait_recv()
    for copy in direct + relays:
        copy.wait_send()
    for copy in own:
        copy.wait()


def gather(arrays, axis, ident):
    size = lax.axis_size(axis)
    if size != 4:
        return tuple(lax.all_gather(a, axis) for a in arrays)
    count = len(arrays)
    return pl.pallas_call(
        partial(gather_kernel, axis, count),
        out_shape=tuple(jax.ShapeDtypeStruct((size,) + a.shape, a.dtype) for a in arrays),
        in_specs=[VM] * count,
        out_specs=tuple([VM] * count),
        scratch_shapes=[
            pltpu.SemaphoreType.DMA((count,)),
            pltpu.SemaphoreType.DMA((count, 4)),
            pltpu.SemaphoreType.DMA((count, 4)),
        ],
        compiler_params=pltpu.CompilerParams(
            collective_id=ident, has_side_effects=True, vmem_limit_bytes=LIMIT
        ),
        name="gather",
    )(*arrays)


def sigmoid(v):
    return 1.0 / (1.0 + jnp.exp(-v))


def silu(v):
    return v / (1.0 + jnp.exp(-v))


def dsilu(v):
    s = sigmoid(v)
    return s * (1.0 + v * (1.0 - s))


def softplus(v):
    return jnp.maximum(v, 0.0) + jnp.log1p(jnp.exp(-jnp.abs(v)))


def spread_pair(first_lanes, table, pair):
    return jnp.where(first_lanes, table[:, 2 * pair : 2 * pair + 1], table[:, 2 * pair + 1 : 2 * pair + 2])


def lanes_first(length, head):
    return lax.broadcasted_iota(jnp.int32, (length, 2 * head), 1) < head


def negative_mask(segc, segr):
    length = segc.shape[0]
    row = lax.broadcasted_iota(jnp.int32, (length, length), 0)
    col = lax.broadcasted_iota(jnp.int32, (length, length), 1)
    return jnp.where((segc == segr) & (row >= col), 0.0, -1e30).astype(f32)


def tails(run, segc):
    length = segc.shape[0]
    return jnp.exp(run[length - 1 : length, :] - run) * (segc == segc[length - 1 : length]).astype(f32)


def local_kernel(
    width, head, cin, same, taps, offs, raw, bias, rate, segc, segr,
    tot, intra, xs, final, delta_out, run_out, runt_out, wide,
):
    length = segc.shape[0]
    total_width = cin.shape[1]
    states = (total_width - width) // 2
    wide[...] = cin[...].astype(f32)
    lags = taps.shape[0]
    pad = cin.shape[0] - length
    for c in range(total_width // 128):
        part = slice(c * 128, c * 128 + 128)
        acc = jnp.broadcast_to(offs[:, part], (length, 128))
        for j in range(lags):
            acc = acc + taps[j : j + 1, part] * (wide[pad - j : pad - j + length, part] * same[:, j : j + 1])
        tot[:, part] = acc
    delta = softplus(raw[...] + bias[...])
    delta_out[...] = delta
    row = lax.broadcasted_iota(jnp.int32, (length, length), 0)
    col = lax.broadcasted_iota(jnp.int32, (length, length), 1)
    below = (row >= col).astype(f32)
    decay = delta * rate[...]
    run = dot(below, decay, precision=highest)
    run_out[...] = run
    runt = run.T
    runt_out[...] = runt
    b = silu(tot[:, width : width + states]).astype(bf16)
    c = silu(tot[:, width + states :]).astype(bf16)
    scores = dot(c, b, 1, 1)
    negative = negative_mask(segc[...], segr[...])
    first = lanes_first(length, head)
    tail = tails(run, segc[...])
    for pair in range(width // (2 * head)):
        part = slice(pair * 2 * head, (pair + 1) * 2 * head)
        x = (silu(tot[:, part]) * spread_pair(first, delta, pair)).astype(bf16)
        xs[:, part] = x
        x32 = x.astype(f32)
        faded = (x32 * spread_pair(first, tail, pair)).astype(bf16)
        final[part, :] = dot(faded, b, 0, 0).astype(bf16)
        total = None
        for k in range(2):
            h = 2 * pair + k
            w = (jnp.exp(run[:, h : h + 1] - runt[h : h + 1, :] + negative) * scores).astype(bf16)
            xk = jnp.where(first if k == 0 else ~first, x32, 0.0).astype(bf16)
            term = dot(w, xk)
            total = term if total is None else total + term
        intra[:, part] = total


def entries(run, segc, before):
    return jnp.exp(run) * (segc == before).astype(f32)


def product_kernel(
    width, head, inner, ctot_ref, tot, intra, entering, run, segc, before, gate, gg, gain, skip, ysum, sums,
):
    length = segc.shape[0]
    first = lanes_first(length, head)
    c = silu(ctot_ref[...]).astype(bf16)
    entry = entries(run[...], segc[...], before[...])
    squares = jnp.zeros((length, 1), f32)
    project = jnp.zeros((length, 1), f32)
    for pair in range(width // (2 * head)):
        part = slice(pair * 2 * head, (pair + 1) * 2 * head)
        y = intra[:, part] + dot(c, entering[part, :], 1, 1) * spread_pair(first, entry, pair)
        ysum[:, part] = y
        mixed = y + spread_pair(first[:1], skip[...], pair) * silu(tot[:, part])
        product = mixed * silu(gate[:, part])
        squares = squares + jnp.sum(product * product, axis=1, keepdims=True)
        project = project + jnp.sum(gg[:, part] * gain[:, part] * product, axis=1, keepdims=True)
    lane = lax.broadcasted_iota(jnp.int32, sums.shape, 1)
    sums[...] = jnp.where(lane == 0, squares, jnp.where(lane == 1, project, 0.0))


def norm_kernel(
    width, head, inner, ctot_ref, tot, ysum, run, segc, before, gate, gg, gain, skip, sums,
    gated, low_gate, gm, grad_entering, grad_gain,
):
    length = segc.shape[0]
    first = lanes_first(length, head)
    c = silu(ctot_ref[...]).astype(bf16)
    entry = entries(run[...], segc[...], before[...])
    scale = lax.rsqrt(sums[:, 0:1] / inner + epsilon)
    project = scale * sums[:, 1:2] / inner
    for pair in range(width // (2 * head)):
        part = slice(pair * 2 * head, (pair + 1) * 2 * head)
        mixed = ysum[:, part] + spread_pair(first[:1], skip[...], pair) * silu(tot[:, part])
        z = gate[:, part]
        sg = sigmoid(z)
        act = z * sg
        unit = mixed * act * scale
        gated[:, part] = (unit * gain[:, part]).astype(bf16)
        g = gg[:, part]
        grad_gain[:, part] = jnp.sum(g * unit, axis=0, keepdims=True)
        gp = scale * (g * gain[:, part] - unit * project)
        gmix = gp * act
        low_gate[:, part] = (gp * mixed * sg * (1.0 + z * (1.0 - sg))).astype(bf16)
        gmb = gmix.astype(bf16)
        gm[:, part] = gmb
        scaled = (gmb.astype(f32) * spread_pair(first, entry, pair)).astype(bf16)
        grad_entering[part, :] = dot(scaled, c, 0, 0).astype(bf16)


def back_kernel(
    width, head, gm, xs, ysum, tot, cin, same, taps, raw, bias, rate, skip, delta_in, run_in, runt_in,
    segc, segr, before, entering, leaving,
    gpad, gtaps, goffs, graw, gheads, dtot, wide,
):
    length = segc.shape[0]
    heads = width // head
    total_width = tot.shape[1]
    states = (total_width - width) // 2
    first = lanes_first(length, head)
    run, runt, delta = run_in[...], runt_in[...], delta_in[...]
    negative = negative_mask(segc[...], segr[...])
    b = silu(tot[:, width : width + states]).astype(bf16)
    c = silu(tot[:, width + states :]).astype(bf16)
    scores = dot(c, b, 1, 1)
    tail = tails(run, segc[...])
    entry = entries(run, segc[...], before[...])
    dscores = jnp.zeros((length, length), f32)
    u = jnp.zeros((length, heads), f32)
    q = jnp.zeros((1, heads), f32)
    vdx = jnp.zeros((length, heads), f32)
    gv = jnp.zeros((1, heads), f32)
    ge = jnp.zeros((1, heads), f32)
    db = jnp.zeros((length, states), f32)
    dc = jnp.zeros((length, states), f32)
    chan = lax.broadcasted_iota(jnp.int32, (2 * head, heads), 0)
    which = lax.broadcasted_iota(jnp.int32, (2 * head, heads), 1)
    for pair in range(heads // 2):
        part = slice(pair * 2 * head, (pair + 1) * 2 * head)
        pick = (which == 2 * pair + (chan >= head).astype(jnp.int32)).astype(f32)
        x = xs[:, part]
        x32 = x.astype(f32)
        g = gm[:, part]
        g32 = g.astype(f32)
        tl = spread_pair(first, tail, pair)
        grad_f = leaving[part, :]
        late = dot(b, grad_f, 1, 1) * tl
        dx = late
        for k in range(2):
            h = 2 * pair + k
            lanes = first if k == 0 else ~first
            gk = jnp.where(lanes, g32, 0.0).astype(bf16)
            decay = jnp.exp(run[:, h : h + 1] - runt[h : h + 1, :] + negative)
            w = (decay * scores).astype(bf16)
            dscores = dscores + decay * dot(gk, x, 1, 1)
            dx = dx + dot(w, gk, 0, 0)
        raw_v = tot[:, part]
        sg = sigmoid(raw_v)
        v = raw_v * sg
        u = u + dot(g32 * ysum[:, part] - x32 * dx, pick, precision=highest)
        q = q + jnp.sum(dot(x32 * late, pick, precision=highest), axis=0, keepdims=True)
        vdx = vdx + dot(v * dx, pick, precision=highest)
        gv = gv + dot(jnp.sum(g32 * v, axis=0, keepdims=True), pick, precision=highest)
        per_row = jnp.sum(grad_f.astype(f32) * entering[part, :].astype(f32), axis=1, keepdims=True)
        ge = ge + jnp.sum(per_row * pick, axis=0, keepdims=True)
        dv = spread_pair(first, delta, pair) * dx + spread_pair(first[:1], skip[...], pair) * g32
        dtot[:, part] = dv * (sg * (1.0 + raw_v * (1.0 - sg)))
        db = db + dot((x32 * tl).astype(bf16), grad_f)
        dc = dc + dot((g32 * spread_pair(first, entry, pair)).astype(bf16), entering[part, :])
    dsb = dscores.astype(bf16)
    dc = dc + dot(dsb, b)
    db = db + dot(dsb, c, 0, 0)
    dtot[:, width : width + states] = db * dsilu(tot[:, width : width + states])
    dtot[:, width + states :] = dc * dsilu(tot[:, width + states :])
    row = lax.broadcasted_iota(jnp.int32, (length, length), 0)
    col = lax.broadcasted_iota(jnp.int32, (length, length), 1)
    above = (row <= col).astype(f32)
    last = slice(length - 1, length)
    dld = dot(above, u, precision=highest) + (q + entry[last, :] * ge)
    ddelta = dld * rate[...] + vdx
    gr = ddelta * sigmoid(raw[...] + bias[...])
    graw[...] = gr
    gheads[...] = jnp.zeros_like(gheads)
    gheads[0:1, :] = jnp.sum(gr, axis=0, keepdims=True)
    gheads[1:2, :] = jnp.sum(dld * delta, axis=0, keepdims=True) * rate[...]
    gheads[2:3, :] = gv
    wide[...] = cin[...].astype(f32)
    gpad[...] = jnp.zeros_like(gpad)
    lags = taps.shape[0]
    pad = cin.shape[0] - length
    for n in range(total_width // 128):
        part = slice(n * 128, n * 128 + 128)
        d = dtot[:, part]
        goffs[:, part] = jnp.sum(d, axis=0, keepdims=True)
        for j in range(lags):
            ds = d * same[:, j : j + 1]
            window = slice(pad - j, pad - j + length)
            gtaps[j : j + 1, part] = jnp.sum(ds * wide[window, part], axis=0, keepdims=True)
            gpad[window, part] = gpad[window, part] + ds * taps[j : j + 1, part]


def call(kernel, outs, args, scratch=(), name=None):
    return pl.pallas_call(
        kernel,
        out_shape=tuple(jax.ShapeDtypeStruct(s, d) for s, d in outs),
        in_specs=[VM] * len(args),
        out_specs=tuple([VM] * len(outs)),
        scratch_shapes=list(scratch),
        compiler_params=pltpu.CompilerParams(vmem_limit_bytes=LIMIT),
        name=name,
    )(*args)


def body(
    hidden,
    segment_ids,
    cotangent,
    input_gain,
    gate_weight,
    value_weight,
    state_weight,
    step_weight,
    conv_weight,
    conv_bias,
    step_bias,
    decay_log,
    skip_gain,
    mixer_gain,
    out_weight,
):
    tokens = hidden[0]
    wrapped = segment_ids[0] % 128
    cot = cotangent[0]
    length, width_in = tokens.shape
    shard = lax.axis_index("tensor")
    shards = lax.axis_size("tensor")
    lags = conv_weight.shape[0]
    reach = lags - 1
    dp = lax.axis_size("dp")
    width = gate_weight.shape[1]
    local_heads = step_weight.shape[1]
    head = width // local_heads
    inner = width * shards
    states = state_weight.shape[1] // 2
    ids_col = jnp.broadcast_to(wrapped[length - reach :].astype(bf16)[:, None], (reach, 128))
    edge = shifted(jnp.concatenate([tokens[length - reach :], ids_col], 1), "ctx", 1)
    narrow = jnp.concatenate(
        [state_weight, step_weight, jnp.zeros((state_weight.shape[0], 128 - local_heads), bf16)], 1
    )
    g_gate, g_value, g_narrow, g_out = gather(
        (gate_weight, value_weight, narrow, out_weight), "dp", 0
    )
    full_gate = g_gate.reshape(width_in, width)
    full_value = g_value.reshape(width_in, width)
    full_narrow = g_narrow.reshape(width_in, narrow.shape[1])
    full_out = jnp.concatenate([g_out[k] for k in range(dp)], 1)
    pad = 8
    base_ext = jnp.concatenate(
        [jnp.zeros((pad - reach, width_in), bf16), edge[:, :width_in], tokens], 0
    ).astype(f32)
    inv_ext = lax.rsqrt(jnp.mean(base_ext * base_ext, axis=-1, keepdims=True) + epsilon)
    normed_ext = (base_ext * inv_ext * input_gain).astype(bf16)
    normed = normed_ext[pad:]
    base = tokens.astype(f32)
    inv = inv_ext[pad:]
    gate = jnp.dot(normed, full_gate, preferred_element_type=f32)
    value_pre = jnp.dot(normed_ext, full_value, preferred_element_type=f32)
    rest_pre = jnp.dot(normed_ext, full_narrow, preferred_element_type=f32)
    cin = jnp.concatenate([value_pre.astype(bf16), rest_pre[:, : 2 * states].astype(bf16)], 1)
    raw_step = rest_pre[pad:, 2 * states : 2 * states + local_heads]
    grad_gated = jnp.dot(cot, full_out.T, preferred_element_type=f32)

    padded_ids = jnp.concatenate([edge[:, width_in].astype(jnp.int32), wrapped])
    before = padded_ids[reach - 1].astype(f32).reshape(1, 1)
    same = jnp.stack(
        [
            (padded_ids[reach - j : reach - j + length] == wrapped).astype(f32)
            for j in range(lags)
        ],
        1,
    )
    segc = wrapped.astype(f32)[:, None]
    segr = wrapped.astype(f32)[None, :]

    def local(array, size):
        return lax.dynamic_slice_in_dim(array, shard * size, size, array.ndim - 1)

    taps = jnp.concatenate([local(conv_weight, width), conv_weight[:, inner:]], 1)
    offs = jnp.concatenate([local(conv_bias, width), conv_bias[inner:]], 0)[None]
    bias = local(step_bias, local_heads)[None]
    rate = -jnp.exp(local(decay_log, local_heads))[None]
    skip = local(skip_gain, local_heads)[None]
    gain = local(mixer_gain, width)[None]
    total_width = width + 2 * states

    tot, intra, xs, final, delta, run, runt = call(
        partial(local_kernel, width, head),
        (
            ((length, total_width), f32),
            ((length, width), f32),
            ((length, width), bf16),
            ((width, states), bf16),
            ((length, local_heads), f32),
            ((length, local_heads), f32),
            ((local_heads, length), f32),
        ),
        (cin, same, taps, offs, raw_step, bias, rate, segc, segr),
        (pltpu.VMEM((length + pad, total_width), f32),),
        "mixer_local",
    )
    through = jnp.exp(run[length - 1]) * (segc[length - 1] == before[0]).astype(f32)
    fade = jnp.broadcast_to(jnp.repeat(through, head)[:, None], (width, 128))
    entering = chain(final, fade, "ctx", 1, 1)
    ctot = tot[:, width + states :]
    ysum, sums = call(
        partial(product_kernel, width, head, inner),
        (((length, width), f32), ((length, 128), f32)),
        (ctot, tot, intra, entering, run, segc, before, gate, grad_gated, gain, skip),
        (),
        "mixer_product",
    )
    sums = pair_sum(sums, "tensor", 2)
    gated, low_gate, gm, grad_entering, grad_mgain = call(
        partial(norm_kernel, width, head, inner),
        (
            ((length, width), bf16),
            ((length, width), bf16),
            ((length, width), bf16),
            ((width, states), bf16),
            ((1, width), f32),
        ),
        (ctot, tot, ysum, run, segc, before, gate, grad_gated, gain, skip, sums),
        (),
        "mixer_norm",
    )
    grad_out = jnp.dot(gated.T, cot, preferred_element_type=f32).astype(bf16)
    grad_gate_w = jnp.dot(normed.T, low_gate, preferred_element_type=f32).astype(bf16)
    out_piece = lax.psum_scatter(grad_out, "dp", scatter_dimension=1, tiled=True)
    gate_piece = lax.psum_scatter(grad_gate_w, "dp", scatter_dimension=0, tiled=True)
    leaving = chain(grad_entering, fade, "ctx", -1, 3)
    gpad, gtaps, goffs, graw, gheads = call(
        partial(back_kernel, width, head),
        (
            ((length + pad, total_width), f32),
            ((lags, total_width), f32),
            ((1, total_width), f32),
            ((length, local_heads), f32),
            ((8, local_heads), f32),
        ),
        (
            gm, xs, ysum, tot, cin, same, taps, raw_step, bias, rate, skip, delta, run, runt,
            segc, segr, before, entering, leaving,
        ),
        (pltpu.VMEM((length, total_width), f32), pltpu.VMEM((length + pad, total_width), f32)),
        "mixer_back",
    )
    edge_grad = shifted(gpad[pad - reach : pad], "ctx", -1)
    grad_input = jnp.concatenate(
        [gpad[pad : pad + length - 8], gpad[pad + length - 8 :] + jnp.pad(edge_grad, ((8 - reach, 0), (0, 0)))], 0
    )
    low_value = grad_input[:, :width].astype(bf16)
    low_rest = jnp.concatenate(
        [
            grad_input[:, width:].astype(bf16),
            graw.astype(bf16),
            jnp.zeros((length, 128 - local_heads), bf16),
        ],
        1,
    )
    low_tail = jnp.concatenate([low_value, low_rest], 1)
    grad_tail_w = jnp.dot(normed.T, low_tail, preferred_element_type=f32).astype(bf16)
    tail_piece = lax.psum_scatter(grad_tail_w, "dp", scatter_dimension=0, tiled=True)
    branch_out = jnp.dot(gated, full_out, preferred_element_type=f32).astype(bf16)
    normed_part = (
        jnp.dot(low_gate, full_gate.T, preferred_element_type=f32)
        + jnp.dot(low_value, full_value.T, preferred_element_type=f32)
        + jnp.dot(low_rest, full_narrow.T, preferred_element_type=f32)
    ).astype(bf16)
    both = pair_sum(jnp.concatenate([branch_out, normed_part], 0), "tensor", 4)
    result = (base + both[:length]).astype(bf16)
    gn = both[length:]
    grad_gain = jnp.sum(gn * base * inv, axis=0)
    gs = gn * input_gain
    grad_base = inv * (gs - base * (inv * inv) * jnp.mean(gs * base, axis=-1, keepdims=True))
    grad_tokens = cot.astype(f32) + grad_base

    out_sum = lax.psum(out_piece, "ctx").astype(f32)
    gate_sum = lax.psum(gate_piece, "ctx").astype(f32)
    tail_sum = lax.psum(tail_piece, "ctx")
    state_sum = pair_sum(tail_sum[:, width : width + 2 * states], "tensor", 5)

    mine = (shard == 0).astype(f32)

    def placed(array, size):
        spots = [jnp.where(shard == k, array, 0.0) for k in range(shards)]
        return jnp.concatenate(spots, -1)

    small = jnp.concatenate(
        [
            (grad_gain * mine)[None],
            jnp.concatenate([placed(gtaps[:, :width], width), gtaps[:, width:]], 1).reshape(1, -1),
            jnp.concatenate([placed(goffs[:, :width], width), goffs[:, width:]], 1),
            placed(grad_mgain, width),
            placed(gheads[0:1], local_heads),
            placed(gheads[1:2], local_heads),
            placed(gheads[2:3], local_heads),
        ],
        1,
    )
    sizes = [width_in, lags * (inner + 2 * states), inner + 2 * states, inner]
    sizes = sizes + [local_heads * shards] * 3
    totals = lax.psum(small, ("dp", "ctx", "tensor"))[0]
    parts, at = [], 0
    for size in sizes:
        parts.append(totals[at : at + size])
        at += size
    return (
        result[None],
        grad_tokens[None],
        parts[0],
        gate_sum,
        tail_sum[:, :width].astype(f32),
        state_sum,
        tail_sum[:, width + 2 * states : width + 2 * states + local_heads].astype(f32),
        parts[1].reshape(lags, inner + 2 * states),
        parts[2],
        parts[4],
        parts[5],
        parts[6],
        parts[3],
        out_sum,
    )


def rot(me, k, size):
    return lax.rem(me + k + size, size)


def remote(src, dst, send, recv, device):
    return pltpu.make_async_remote_copy(
        src_ref=src, dst_ref=dst, send_sem=send, recv_sem=recv, device_id=device, device_id_type=MESH
    )


def greet(barrier, device):
    pl.semaphore_signal(barrier, inc=1, device_id=device, device_id_type=MESH)


def spot(index, size):
    return pl.ds(pl.multiple_of(index * size, size), size)


def inside(index, size):
    return (index >= 0) & (index < size)


class Line:
    def __init__(self, own, at, send, recv, onward=None):
        self.own, self.at, self.send, self.recv, self.onward = own, at, send, recv, onward
        self.me, self.size = lax.axis_index("ctx"), lax.axis_size("ctx")

    def hop(self, w, s):
        way = (1, -1)[w]
        block = self.me - way * s
        src = self.own if s == 0 else self.at(block)
        return remote(src, self.at(block), self.send.at[w, s], self.recv.at[w, s], {"ctx": self.me + way})

    def start(self):
        for w, way in enumerate((1, -1)):
            @pl.when(inside(self.me + way, self.size))
            def _(w=w):
                self.hop(w, 0).start()

    def step(self, s):
        for w, way in enumerate((1, -1)):
            block = self.me - way * (s + 1)

            @pl.when(inside(block, self.size))
            def _(w=w, way=way, block=block):
                ref = self.at(block)
                remote(ref, ref, self.send.at[w, s], self.recv.at[w, s], {"ctx": self.me - way}).wait_recv()
                if s + 1 < self.size - 1:
                    @pl.when(inside(self.me + way, self.size))
                    def _():
                        self.hop(w, s + 1).start()
                if self.onward is not None:
                    self.onward(block, w, s).start()

    def finish(self):
        for s in range(self.size - 1):
            for w, way in enumerate((1, -1)):
                @pl.when(inside(self.me + way, self.size) & inside(self.me - way * s, self.size))
                def _(w=w, s=s):
                    self.hop(w, s).wait_send()

    def arrived(self):
        for s in range(self.size - 1):
            for w, way in enumerate((1, -1)):
                block = self.me - way * (s + 1)

                @pl.when(inside(block, self.size))
                def _(w=w, s=s, block=block):
                    self.onward(block, w, s).wait()


def greet_line(barrier):
    c, nc = lax.axis_index("ctx"), lax.axis_size("ctx")
    for way in (1, -1):
        @pl.when(inside(c + way, nc))
        def _(way=way):
            greet(barrier, {"ctx": c + way})


def line_peers():
    c, nc = lax.axis_index("ctx"), lax.axis_size("ctx")
    return (c > 0).astype(jnp.int32) + (c < nc - 1).astype(jnp.int32)


def collect_kernel(
    hid, cot, ids, wg, wv, ws, wst, wo, H, CF, IDS, WG, WV, WS, WST, WO, zs, zr, fs, fr, ds, dr,
):
    c, d, t = lax.axis_index("ctx"), lax.axis_index("dp"), lax.axis_index("tensor")
    nc, nd = lax.axis_size("ctx"), lax.axis_size("dp")
    half = hid.shape[0] // 2
    chans = WG.shape[2]
    wide = WST.shape[1] // nd
    barrier = pltpu.get_barrier_semaphore()
    greet(barrier, {"tensor": 1 - t})
    for k in range(1, nd):
        greet(barrier, {"dp": rot(d, k, nd)})
    greet_line(barrier)
    pl.semaphore_wait(barrier, nd + line_peers())

    def line(a, own, out):
        def at(block):
            return out.at[block, spot(t, half)]

        def onward(block, w, s):
            ref = at(block)
            return remote(ref, ref, fs.at[a, w, s], fr.at[a, w, s], {"tensor": 1 - t})

        return Line(own.at[spot(t, half)], at, zs.at[a], zr.at[a], onward)

    lines = [line(0, hid, H), line(1, cot, CF)]
    small = Line(ids, lambda block: IDS.at[block], zs.at[2], zr.at[2])
    small.start()
    lines[0].start()
    moves = (
        (wv.at[:, spot(c, chans)], WV.at[d]),
        (wg.at[:, spot(c, chans)], WG.at[d]),
        (ws, WS.at[d]),
        (wst, WST.at[:, spot(d, wide)]),
        (wo.at[spot(c, chans), :], WO.at[:, spot(d, wide)]),
    )
    sent = []
    for a, (src, dst) in enumerate(moves):
        for k in range(1, nd):
            sent.append(remote(src, dst, ds.at[a, k - 1], dr.at[a, k - 1], {"dp": rot(d, k, nd)}))
            sent[-1].start()
    lines[1].start()
    H[c] = hid[...]
    CF[c] = cot[...]
    IDS[c] = ids[...]
    WV[d] = wv[:, spot(c, chans)]
    WG[d] = wg[:, spot(c, chans)]
    WS[d] = ws[...]
    WST[:, spot(d, wide)] = wst[...]
    WO[:, spot(d, wide)] = wo[spot(c, chans), :]
    for s in range(nc - 1):
        small.step(s)
        for item in lines:
            item.step(s)
    landed = (
        lambda r: WV.at[r], lambda r: WG.at[r], lambda r: WS.at[r],
        lambda r: WST.at[:, spot(r, wide)], lambda r: WO.at[:, spot(r, wide)],
    )
    for a, at in enumerate(landed):
        for k in range(1, nd):
            ref = at(rot(d, -k, nd))
            remote(ref, ref, ds.at[a, k - 1], dr.at[a, k - 1], {"dp": rot(d, -k, nd)}).wait_recv()
    for copy in sent:
        copy.wait_send()
    small.finish()
    for item in lines:
        item.finish()
        item.arrived()


def chunk_masks(segp, at, length, lags):
    segc = segp[at : at + length, 0:1]
    return segc, [(segp[at - j : at - j + length, 0:1] == segc).astype(f32) for j in range(lags)]


def fades(through, pair, head, rows):
    low = lax.broadcasted_iota(jnp.int32, (rows, 1), 0) < head
    return jnp.where(low, through[:, 2 * pair : 2 * pair + 1], through[:, 2 * pair + 1 : 2 * pair + 2])


def forward_kernel(
    head, hid, cot, ids, wg, wv, ws, wst, wo, in_gain, cw, cb, mg, hp,
    normed, gate, gg, cin, tot, xs, ysum, ent, delta, run, runt, raw, sums, segp, taps, offs, gain, invs, state,
):
    c, t = lax.axis_index("ctx"), lax.axis_index("tensor")
    nc = lax.axis_size("ctx")
    chunks, _, length = ids.shape
    width = wg.shape[1]
    states = ws.shape[1] // 2
    pairs = width // (2 * head)
    lags = cw.shape[0]
    inner = mg.shape[1]
    pad = 8
    mine = spot(t * nc + c, width)
    taps[:, :width] = cw[:, mine]
    taps[:, width:] = cw[:, inner:]
    offs[:, :width] = cb[:, mine]
    offs[:, width:] = cb[:, inner:]
    gain[...] = mg[:, mine]
    segp[:pad, :] = jnp.full((pad, segp.shape[1]), -1.0, f32)
    for k in range(chunks):
        segp[pad + k * length : pad + (k + 1) * length, :] = ids[k].T
    cin[:pad, :] = jnp.zeros((pad, cin.shape[1]), f32)
    state[...] = jnp.zeros_like(state)
    sums[...] = jnp.zeros_like(sums)
    row = lax.broadcasted_iota(jnp.int32, (length, length), 0)
    col = lax.broadcasted_iota(jnp.int32, (length, length), 1)
    below = (row >= col).astype(f32)
    first = lanes_first(length, head)
    bias, rate, skip = hp[0:1, :], hp[1:2, :], hp[2:3, :]
    for k in range(chunks):
        rows = slice(k * length, (k + 1) * length)
        at = pad + k * length
        base = hid[rows, :].astype(f32)
        inv = lax.rsqrt(jnp.mean(base * base, axis=-1, keepdims=True) + epsilon)
        invs[rows, :] = inv
        nb = (base * inv * in_gain[...]).astype(bf16)
        normed[rows, :] = nb
        gate[rows, :] = dot(nb, wg[...])
        cin[at : at + length, :width] = dot(nb, wv[...]).astype(bf16).astype(f32)
        cin[at : at + length, width:] = dot(nb, ws[...]).astype(bf16).astype(f32)
        rawk = dot(nb, wst[...], 1, 1)
        raw[rows, :] = rawk
        gg[rows, :] = dot(cot[rows, :], wo[...], 1, 1)
        segc, same = chunk_masks(segp, at, length, lags)
        segr = ids[k, 0:1, :]
        before = segp[at - 1 : at, 0:1]
        for n in range(cin.shape[1] // 128):
            part = slice(n * 128, n * 128 + 128)
            acc = jnp.broadcast_to(offs[:, part], (length, 128))
            for j in range(lags):
                acc = acc + taps[j : j + 1, part] * (cin[at - j : at - j + length, part] * same[j])
            tot[rows, part] = acc
        dk = softplus(rawk + bias)
        delta[rows, :] = dk
        rk = dot(below, dk * rate, precision=highest)
        run[rows, :] = rk
        rkt = rk.T
        runt[k] = rkt
        b = silu(tot[rows, width : width + states]).astype(bf16)
        cc = silu(tot[rows, width + states :]).astype(bf16)
        scores = dot(cc, b, 1, 1)
        negative = negative_mask(segc, segr)
        tail = tails(rk, segc)
        entry = entries(rk, segc, before)
        through = entry[length - 1 : length, :]
        squares = jnp.zeros((length, 1), f32)
        project = jnp.zeros((length, 1), f32)
        for pair in range(pairs):
            part = slice(pair * 2 * head, (pair + 1) * 2 * head)
            values = silu(tot[rows, part])
            x = (values * spread_pair(first, dk, pair)).astype(bf16)
            xs[rows, part] = x
            x32 = x.astype(f32)
            faded = (x32 * spread_pair(first, tail, pair)).astype(bf16)
            old = state[part, :]
            entering = old.astype(bf16)
            ent[k, part, :] = entering
            state[part, :] = fades(through, pair, head, 2 * head) * old + dot(faded, b, 0, 0)
            y = dot(cc, entering, 1, 1) * spread_pair(first, entry, pair)
            for m in range(2):
                h = 2 * pair + m
                w = (jnp.exp(rk[:, h : h + 1] - rkt[h : h + 1, :] + negative) * scores).astype(bf16)
                xk = jnp.where(first if m == 0 else ~first, x32, 0.0).astype(bf16)
                y = y + dot(w, xk)
            ysum[rows, part] = y
            mixed = y + spread_pair(first[:1], skip, pair) * values
            product = mixed * silu(gate[rows, part])
            squares = squares + jnp.sum(product * product, axis=1, keepdims=True)
            project = project + jnp.sum(gg[rows, part] * gain[:, part] * product, axis=1, keepdims=True)
        lane = lax.broadcasted_iota(jnp.int32, (length, 128), 1)
        both = jnp.where(lane == 0, squares, jnp.where(lane == 1, project, 0.0))
        sums[2 * k : 2 * k + 2, :] = both.T[0:2, :]


def gate_kernel(
    head, inner, sums, tot, ysum, gate, gg, gain, hp, gated, low_gate, gm, grad_gain, slots, send, recv,
):
    c, t = lax.axis_index("ctx"), lax.axis_index("tensor")
    nc, nt = lax.axis_size("ctx"), lax.axis_size("tensor")
    total = nc * nt
    length = sums.shape[1]
    width = gate.shape[1]
    me = c * nt + t
    barrier = pltpu.get_barrier_semaphore()

    def peer(k):
        r = rot(me, k, total)
        return r, {"ctx": r // nt, "tensor": lax.rem(r, nt)}

    for k in range(1, total):
        greet(barrier, peer(k)[1])
    slots[me] = sums[...]
    pl.semaphore_wait(barrier, total - 1)
    sent = []
    for k in range(1, total):
        sent.append(remote(sums, slots.at[me], send.at[k - 1], recv.at[k - 1], peer(k)[1]))
        sent[-1].start()
    for k in range(1, total):
        r, device = peer(-k)
        remote(sums, slots.at[r], send.at[k - 1], recv.at[k - 1], device).wait_recv()
    added = slots[0]
    for r in range(1, total):
        added = added + slots[r]
    added = added.T
    first = lanes_first(length, head)
    skip = hp[2:3, :]
    grad_gain[...] = jnp.zeros_like(grad_gain)
    for k in range(gate.shape[0] // length):
        rows = slice(k * length, (k + 1) * length)
        scale = lax.rsqrt(added[:, 2 * k : 2 * k + 1] / inner + epsilon)
        project = scale * added[:, 2 * k + 1 : 2 * k + 2] / inner
        for pair in range(width // (2 * head)):
            part = slice(pair * 2 * head, (pair + 1) * 2 * head)
            mixed = ysum[rows, part] + spread_pair(first[:1], skip, pair) * silu(tot[rows, part])
            z = gate[rows, part]
            sg = sigmoid(z)
            act = z * sg
            unit = mixed * act * scale
            gated[rows, part] = (unit * gain[:, part]).astype(bf16)
            g = gg[rows, part]
            grad_gain[:, part] = grad_gain[:, part] + jnp.sum(g * unit, axis=0, keepdims=True)
            gp = scale * (g * gain[:, part] - unit * project)
            low_gate[rows, part] = (gp * mixed * sg * (1.0 + z * (1.0 - sg))).astype(bf16)
            gm[rows, part] = (gp * act).astype(bf16)
    for copy in sent:
        copy.wait_send()


def backward_kernel(
    head, gm, xs, ysum, tot, cin, segp, ids, taps, raw, hp, delta_in, run_in, runt_in, ent,
    low_value, low_state, low_step, gtaps, goffs, gheads, state, dtot, gpad,
):
    chunks, _, length = ids.shape
    width = gm.shape[1]
    heads = raw.shape[1]
    total_width = tot.shape[1]
    states = (total_width - width) // 2
    lags = taps.shape[0]
    pad = cin.shape[0] - tot.shape[0]
    first = lanes_first(length, head)
    bias, rate, skip = hp[0:1, :], hp[1:2, :], hp[2:3, :]
    chan = lax.broadcasted_iota(jnp.int32, (2 * head, heads), 0)
    which = lax.broadcasted_iota(jnp.int32, (2 * head, heads), 1)
    row = lax.broadcasted_iota(jnp.int32, (length, length), 0)
    col = lax.broadcasted_iota(jnp.int32, (length, length), 1)
    above = (row <= col).astype(f32)
    state[...] = jnp.zeros_like(state)
    gpad[...] = jnp.zeros_like(gpad)
    gtaps[...] = jnp.zeros_like(gtaps)
    goffs[...] = jnp.zeros_like(goffs)
    gheads[...] = jnp.zeros_like(gheads)
    for k in reversed(range(chunks)):
        rows = slice(k * length, (k + 1) * length)
        at = pad + k * length
        segc, same = chunk_masks(segp, at, length, lags)
        segr = ids[k, 0:1, :]
        before = segp[at - 1 : at, 0:1]
        run, runt, delta = run_in[rows, :], runt_in[k], delta_in[rows, :]
        negative = negative_mask(segc, segr)
        b = silu(tot[rows, width : width + states]).astype(bf16)
        c = silu(tot[rows, width + states :]).astype(bf16)
        scores = dot(c, b, 1, 1)
        tail = tails(run, segc)
        entry = entries(run, segc, before)
        through = entry[length - 1 : length, :]
        dscores = jnp.zeros((length, length), f32)
        u = jnp.zeros((length, heads), f32)
        q = jnp.zeros((1, heads), f32)
        vdx = jnp.zeros((length, heads), f32)
        gv = jnp.zeros((1, heads), f32)
        ge = jnp.zeros((1, heads), f32)
        db = jnp.zeros((length, states), f32)
        dc = jnp.zeros((length, states), f32)
        for pair in range(width // (2 * head)):
            part = slice(pair * 2 * head, (pair + 1) * 2 * head)
            pick = (which == 2 * pair + (chan >= head).astype(jnp.int32)).astype(f32)
            x = xs[rows, part]
            x32 = x.astype(f32)
            g32 = gm[rows, part].astype(f32)
            tl = spread_pair(first, tail, pair)
            grad_f32 = state[part, :]
            grad_f = grad_f32.astype(bf16)
            entering = ent[k, part, :]
            late = dot(b, grad_f, 1, 1) * tl
            dx = late
            for m in range(2):
                h = 2 * pair + m
                lanes = first if m == 0 else ~first
                gk = jnp.where(lanes, g32, 0.0).astype(bf16)
                decay = jnp.exp(run[:, h : h + 1] - runt[h : h + 1, :] + negative)
                w = (decay * scores).astype(bf16)
                dscores = dscores + decay * dot(gk, x, 1, 1)
                dx = dx + dot(w, gk, 0, 0)
            raw_v = tot[rows, part]
            sg = sigmoid(raw_v)
            v = raw_v * sg
            u = u + dot(g32 * ysum[rows, part] - x32 * dx, pick, precision=highest)
            q = q + dot(jnp.sum(x32 * late, axis=0, keepdims=True), pick, precision=highest)
            vdx = vdx + dot(v * dx, pick, precision=highest)
            gv = gv + dot(jnp.sum(g32 * v, axis=0, keepdims=True), pick, precision=highest)
            per_row = jnp.sum(grad_f32 * entering.astype(f32), axis=1, keepdims=True)
            ge = ge + jnp.sum(per_row * pick, axis=0, keepdims=True)
            dv = spread_pair(first, delta, pair) * dx + spread_pair(first[:1], skip, pair) * g32
            dtot[:, part] = dv * (sg * (1.0 + raw_v * (1.0 - sg)))
            db = db + dot((x32 * tl).astype(bf16), grad_f)
            scaled = (g32 * spread_pair(first, entry, pair)).astype(bf16)
            dc = dc + dot(scaled, entering)
            state[part, :] = fades(through, pair, head, 2 * head) * grad_f32 + dot(scaled, c, 0, 0)
        dsb = dscores.astype(bf16)
        dc = dc + dot(dsb, b)
        db = db + dot(dsb, c, 0, 0)
        dtot[:, width : width + states] = db * dsilu(tot[rows, width : width + states])
        dtot[:, width + states :] = dc * dsilu(tot[rows, width + states :])
        dld = dot(above, u, precision=highest) + (q + through * ge)
        ddelta = dld * rate + vdx
        gr = ddelta * sigmoid(raw[rows, :] + bias)
        low_step[rows, :] = gr.astype(bf16)
        gheads[0:1, :] = gheads[0:1, :] + jnp.sum(gr, axis=0, keepdims=True)
        gheads[1:2, :] = gheads[1:2, :] + jnp.sum(dld * delta, axis=0, keepdims=True) * rate
        gheads[2:3, :] = gheads[2:3, :] + gv
        for n in range(total_width // 128):
            part = slice(n * 128, n * 128 + 128)
            d = dtot[:, part]
            goffs[:, part] = goffs[:, part] + jnp.sum(d, axis=0, keepdims=True)
            for j in range(lags):
                ds = d * same[j]
                window = slice(at - j, at - j + length)
                gtaps[j : j + 1, part] = gtaps[j : j + 1, part] + jnp.sum(
                    ds * cin[window, part], axis=0, keepdims=True
                )
                gpad[window, part] = gpad[window, part] + ds * taps[j : j + 1, part]
        low_value[rows, :] = gpad[at : at + length, :width].astype(bf16)
        low_state[rows, :] = gpad[at : at + length, width:].astype(bf16)


def ranked(slots):
    total = slots[0].astype(f32)
    for r in range(1, slots.shape[0]):
        total = total + slots[r].astype(f32)
    return total


def tail_kernel(
    br, npart, gg, gv, go, gs, gst, small, hid, cot, in_gain,
    out, gh, dg, dv, do, dst, dstate, smalls,
    sib_b, sib_n, sib_s, stage_b, stage_n, slot_b, slot_n,
    slot_g, slot_v, slot_o, slot_t, slot_s, stage_s, all_s, slot_m, mid_m,
    ps, pr, qs, qr, zs, zr, ds, dr, ss, sr, ms, mr, es, er,
):
    c, d, t = lax.axis_index("ctx"), lax.axis_index("dp"), lax.axis_index("tensor")
    nc, nd, nt = lax.axis_size("ctx"), lax.axis_size("dp"), lax.axis_size("tensor")
    total = nc * nt
    me = c * nt + t
    half = br.shape[2]
    wide = slot_o.shape[2]
    sib = {"tensor": 1 - t}
    barrier = pltpu.get_barrier_semaphore()

    def peer(k):
        r = rot(me, k, total)
        return r, {"ctx": r // nt, "tensor": lax.rem(r, nt)}

    for k in range(1, nd):
        greet(barrier, {"dp": rot(d, k, nd)})
    for k in range(1, total):
        greet(barrier, peer(k)[1])
    pl.semaphore_wait(barrier, nd + total - 2)
    sent = []

    def go_(copy):
        copy.start()
        sent.append(copy)

    def swap(a, k, src, dst):
        return remote(src.at[k, 1 - t], dst.at[k], ps.at[a, k], pr.at[a, k], sib)

    for k in range(nd):
        go_(swap(2, k, gs, sib_s))
    for k in range(nc):
        go_(swap(0, k, br, sib_b))
        go_(swap(1, k, npart, sib_n))
    spread = (
        (lambda p: gg.at[p], slot_g),
        (lambda p: gv.at[p], slot_v),
        (lambda p: go.at[:, spot(p, wide)], slot_o),
        (lambda p: gst.at[:, spot(p, wide)], slot_t),
        (lambda p: small, slot_m),
    )
    for a, (src, slot) in enumerate(spread):
        for k in range(1, nd):
            p = rot(d, k, nd)
            go_(remote(src(p), slot.at[d], ds.at[a, k - 1], dr.at[a, k - 1], {"dp": p}))
    slot_g[d] = gg[d]
    slot_v[d] = gv[d]
    slot_o[d] = go[:, spot(d, wide)]
    slot_t[d] = gst[:, spot(d, wide)]
    slot_m[d] = small[...]

    for k in range(nd):
        swap(2, k, gs, sib_s).wait_recv()
        stage_s[k] = (gs[k, t].astype(f32) + sib_s[k].astype(f32)).astype(bf16)
    for k in range(1, nd):
        p = rot(d, k, nd)
        go_(remote(stage_s.at[p], slot_s.at[d], ss.at[k - 1], sr.at[k - 1], {"dp": p}))
    slot_s[d] = stage_s[d]

    def block_send(a, k, src, slot):
        p = rot(c, k, nc)
        return remote(src.at[p], slot.at[c], qs.at[a, k - 1], qr.at[a, k - 1], {"ctx": p})

    for a, (src, other, stage, slot) in enumerate(((br, sib_b, stage_b, slot_b), (npart, sib_n, stage_n, slot_n))):
        for k in range(nc):
            swap(a, k, src, other).wait_recv()
            stage[k] = (src[k, t].astype(f32) + other[k].astype(f32)).astype(bf16)
        for k in range(1, nc):
            go_(block_send(a, k, stage, slot))
        slot[c] = stage[c]

    def collected(a, slot):
        for k in range(1, nd):
            r = rot(d, -k, nd)
            remote(slot.at[r], slot.at[r], ds.at[a, k - 1], dr.at[a, k - 1], {"dp": r}).wait_recv()
        return ranked(slot)

    lines = []
    for a, (slot, place) in enumerate(((slot_g, dg), (slot_v, dv), (slot_o, do), (slot_t, dst))):
        place[c] = collected(a, slot).astype(bf16)
        lines.append(Line(place.at[c], lambda block, place=place: place.at[block], zs.at[a], zr.at[a]))
        lines[-1].start()
    mid_m[...] = collected(4, slot_m)
    smalls[me] = mid_m[...]
    for k in range(1, total):
        go_(remote(mid_m, smalls.at[me], ms.at[k - 1], mr.at[k - 1], peer(k)[1]))
    for k in range(1, nd):
        r = rot(d, -k, nd)
        remote(slot_s.at[r], slot_s.at[r], ss.at[k - 1], sr.at[k - 1], {"dp": r}).wait_recv()
    all_s[c] = ranked(slot_s).astype(bf16)
    line_s = Line(all_s.at[c], lambda block: all_s.at[block], zs.at[4], zr.at[4])
    line_s.start()
    lines.append(line_s)
    for s in range(nc - 1):
        for item in lines:
            item.step(s)
    dstate[t] = ranked(all_s)
    ends = [remote(dstate.at[t], dstate.at[t], es.at[0], er.at[0], sib)]
    ends[0].start()

    def blocks_in(a, slot):
        for k in range(1, nc):
            r = rot(c, -k, nc)
            remote(slot.at[r], slot.at[r], qs.at[a, k - 1], qr.at[a, k - 1], {"ctx": r}).wait_recv()
        return ranked(slot)

    rows = spot(t, half)
    base = hid[rows, :].astype(f32)
    out[t] = (base + blocks_in(0, slot_b)).astype(bf16)
    ends.append(remote(out.at[t], out.at[t], es.at[1], er.at[1], sib))
    ends[-1].start()
    gn = blocks_in(1, slot_n)
    inv = lax.rsqrt(jnp.mean(base * base, axis=-1, keepdims=True) + epsilon)
    gsx = gn * in_gain[...]
    grad = inv * (gsx - base * (inv * inv) * jnp.mean(gsx * base, axis=-1, keepdims=True))
    gh[t] = cot[rows, :].astype(f32) + grad
    ends.append(remote(gh.at[t], gh.at[t], es.at[2], er.at[2], sib))
    ends[-1].start()
    for k in range(1, total):
        r, device = peer(-k)
        remote(mid_m, smalls.at[r], ms.at[k - 1], mr.at[k - 1], device).wait_recv()
    for item in lines:
        item.finish()
    for copy in sent:
        copy.wait_send()
    for copy, ref, e in zip(ends, (dstate, out, gh), range(3)):
        copy.wait_send()
        remote(ref.at[1 - t], ref.at[1 - t], es.at[e], er.at[e], sib).wait_recv()


def sd(shape, kind):
    return jax.ShapeDtypeStruct(tuple(shape), kind)


def run_kernel(kernel, outs, args, scratch=(), name=None, ident=None):
    extra = {} if ident is None else dict(collective_id=ident, has_side_effects=True)
    return pl.pallas_call(
        kernel,
        out_shape=tuple(sd(s, k) for s, k in outs),
        in_specs=[VM] * len(args),
        out_specs=tuple([VM] * len(outs)),
        scratch_shapes=list(scratch),
        compiler_params=pltpu.CompilerParams(vmem_limit_bytes=LIMIT, **extra),
        name=name,
    )(*args)


def sems(*shape):
    return pltpu.SemaphoreType.DMA(shape)


def spread_body(
    hidden, segment_ids, cotangent, input_gain, gate_weight, value_weight, state_weight, step_weight,
    conv_weight, conv_bias, step_bias, decay_log, skip_gain, mixer_gain, out_weight,
):
    tokens, cot = hidden[0], cotangent[0]
    length, D = tokens.shape
    c, t = lax.axis_index("ctx"), lax.axis_index("tensor")
    nc, nd, nt = lax.axis_size("ctx"), lax.axis_size("dp"), lax.axis_size("tensor")
    width = gate_weight.shape[1] // nc
    inner = width * nc * nt
    heads_all = step_bias.shape[0]
    heads = heads_all // (nc * nt)
    hpad = 16 * ((heads + 15) // 16)
    head = width // heads
    states = state_weight.shape[1] // 2
    W = width + 2 * states
    T = length * nc
    rows = D // nd
    lags = conv_weight.shape[0]
    ids = jnp.broadcast_to(segment_ids.astype(f32), (8, length))
    stept = lax.dynamic_slice_in_dim(step_weight, c * heads, heads, 1).T
    stept = jnp.pad(stept, ((0, hpad - heads), (0, 0)))
    hp = jnp.stack([step_bias, -jnp.exp(decay_log), skip_gain] + [jnp.zeros_like(step_bias)] * 5)
    hp = lax.dynamic_slice_in_dim(hp, (t * nc + c) * heads, heads, 1)
    hp = jnp.pad(hp, ((0, 0), (0, hpad - heads)))
    gain_in = input_gain[None]

    H, CF, IDS, WG, WV, WS, WST, WO = run_kernel(
        collect_kernel,
        (
            ((nc, length, D), bf16), ((nc, length, D), bf16), ((nc, 8, length), f32),
            ((nd, rows, width), bf16), ((nd, rows, width), bf16), ((nd, rows, 2 * states), bf16),
            ((hpad, D), bf16), ((width, D), bf16),
        ),
        (tokens, cot, ids, gate_weight, value_weight, state_weight, stept, out_weight),
        (
            sems(3, 2, nc - 1), sems(3, 2, nc - 1), sems(2, 2, nc - 1), sems(2, 2, nc - 1),
            sems(5, nd - 1), sems(5, nd - 1),
        ),
        "collect",
        0,
    )
    H, CF = H.reshape(T, D), CF.reshape(T, D)
    WG, WV, WS = WG.reshape(D, width), WV.reshape(D, width), WS.reshape(D, 2 * states)
    srows = 8 * ((2 * nc + 7) // 8)
    (normed, gate, gg, cin, tot, xs, ysum, ent, delta, run, runt, raw, sums, segp, taps, offs, gain, invs) = run_kernel(
        partial(forward_kernel, head),
        (
            ((T, D), bf16), ((T, width), f32), ((T, width), f32), ((T + 8, W), f32), ((T, W), f32),
            ((T, width), bf16), ((T, width), f32), ((nc, width, states), bf16), ((T, hpad), f32),
            ((T, hpad), f32), ((nc, hpad, length), f32), ((T, hpad), f32), ((srows, length), f32),
            ((T + 8, 8), f32), ((lags, W), f32), ((1, W), f32), ((1, width), f32), ((T, 1), f32),
        ),
        (H, CF, IDS, WG, WV, WS, WST, WO, gain_in, conv_weight, conv_bias[None], mixer_gain[None], hp),
        (pltpu.VMEM((width, states), f32),),
        "forward",
    )
    total = nc * nt
    gated, low_gate, gm, grad_mgain = run_kernel(
        partial(gate_kernel, head, inner),
        (((T, width), bf16), ((T, width), bf16), ((T, width), bf16), ((1, width), f32)),
        (sums, tot, ysum, gate, gg, gain, hp),
        (pltpu.VMEM((total, srows, length), f32), sems(total - 1), sems(total - 1)),
        "gating",
        1,
    )
    low_value, low_state, low_step, gtaps, goffs, gheads = run_kernel(
        partial(backward_kernel, head),
        (
            ((T, width), bf16), ((T, 2 * states), bf16), ((T, hpad), bf16), ((lags, W), f32), ((1, W), f32),
            ((8, hpad), f32),
        ),
        (gm, xs, ysum, tot, cin, segp, IDS, taps, raw, hp, delta, run, runt, ent),
        (pltpu.VMEM((width, states), f32), pltpu.VMEM((length, W), f32), pltpu.VMEM((T + 8, W), f32)),
        "backward",
    )
    go = dot(gated, CF, 0, 0).astype(bf16)
    gG = dot(normed, low_gate, 0, 0).astype(bf16)
    br = dot(gated, WO).astype(bf16)
    gV = dot(normed, low_value, 0, 0).astype(bf16)
    gS = dot(normed, low_state, 0, 0).astype(bf16)
    gT = dot(low_step, normed, 0, 0).astype(bf16)
    npart = dot(low_gate, WG, 1, 1) + dot(low_value, WV, 1, 1) + dot(low_state, WS, 1, 1) + dot(low_step, WST)
    grad_gain = jnp.sum(npart * (H.astype(f32) * invs), axis=0)
    npart = npart.astype(bf16)
    small = jnp.concatenate(
        [
            gtaps[:, :width].reshape(-1), goffs[0, :width], grad_mgain[0],
            gtaps[:, width:].reshape(-1), goffs[0, width:], grad_gain, gheads[:3, :heads].reshape(-1),
        ]
    )
    used = small.shape[0]
    srow = 8 * ((used + 1023) // 1024)
    small = jnp.pad(small, (0, srow * 128 - used)).reshape(srow, 128)
    half = length // 2
    shalf = rows // 2
    out, gh, dg, dv, do, dst, dstate, smalls = run_kernel(
        tail_kernel,
        (
            ((2, half, D), bf16), ((2, half, D), f32), ((nc, rows, width), bf16), ((nc, rows, width), bf16),
            ((nc, width, rows), bf16), ((nc, hpad, rows), bf16), ((2, shalf, 2 * states), f32),
            ((total, srow, 128), f32),
        ),
        (
            br.reshape(nc, 2, half, D), npart.reshape(nc, 2, half, D), gG.reshape(nd, rows, width),
            gV.reshape(nd, rows, width), go, gS.reshape(nd, 2, shalf, 2 * states), gT, small, tokens, cot, gain_in,
        ),
        (
            pltpu.VMEM((nc, half, D), bf16), pltpu.VMEM((nc, half, D), bf16),
            pltpu.VMEM((nd, shalf, 2 * states), bf16),
            pltpu.VMEM((nc, half, D), bf16), pltpu.VMEM((nc, half, D), bf16),
            pltpu.VMEM((nc, half, D), bf16), pltpu.VMEM((nc, half, D), bf16),
            pltpu.VMEM((nd, rows, width), bf16), pltpu.VMEM((nd, rows, width), bf16),
            pltpu.VMEM((nd, width, rows), bf16), pltpu.VMEM((nd, hpad, rows), bf16),
            pltpu.VMEM((nd, shalf, 2 * states), bf16), pltpu.VMEM((nd, shalf, 2 * states), bf16),
            pltpu.VMEM((nc, shalf, 2 * states), bf16),
            pltpu.VMEM((nd, srow, 128), f32), pltpu.VMEM((srow, 128), f32),
            sems(3, max(nc, nd)), sems(3, max(nc, nd)), sems(2, nc - 1), sems(2, nc - 1),
            sems(5, 2, nc - 1), sems(5, 2, nc - 1), sems(5, nd - 1), sems(5, nd - 1),
            sems(nd - 1), sems(nd - 1), sems(total - 1), sems(total - 1), sems(3), sems(3),
        ),
        "tail",
        2,
    )
    flat = smalls.reshape(total, srow * 128)[:, :used]
    shared = jnp.sum(flat, axis=0)
    own = jnp.swapaxes(flat.reshape(nc, nt, used), 0, 1).reshape(total, used)
    at = 0
    got = {}
    for name, size, mine in (
        ("taps", lags * width, True), ("offs", width, True), ("gain", width, True),
        ("staps", lags * 2 * states, False), ("soffs", 2 * states, False), ("in", D, False),
        ("heads", 3 * heads, True),
    ):
        got[name] = (own if mine else shared)[..., at : at + size]
        at += size
    g_taps = jnp.swapaxes(got["taps"].reshape(total, lags, width), 0, 1).reshape(lags, inner)
    g_heads = jnp.swapaxes(got["heads"].reshape(total, 3, heads), 0, 1).reshape(3, heads_all)
    return (
        out.reshape(1, length, D),
        gh.reshape(1, length, D),
        got["in"],
        jnp.swapaxes(dg, 0, 1).reshape(rows, nc * width).astype(f32),
        jnp.swapaxes(dv, 0, 1).reshape(rows, nc * width).astype(f32),
        dstate.reshape(rows, 2 * states),
        jnp.transpose(dst[:, :heads, :], (2, 0, 1)).reshape(rows, nc * heads).astype(f32),
        jnp.concatenate([g_taps, got["staps"].reshape(lags, 2 * states)], 1),
        jnp.concatenate([got["offs"].reshape(-1), got["soffs"]]),
        g_heads[0],
        g_heads[1],
        g_heads[2],
        got["gain"].reshape(-1),
        do.reshape(nc * width, rows).astype(f32),
    )


def fits(mesh, args):
    nc, nd, nt = mesh.shape["ctx"], mesh.shape["dp"], mesh.shape["tensor"]
    hidden, gate_weight, state_weight, step_bias = args[0], args[4], args[6], args[10]
    seqs, tokens, D = hidden.shape
    inner, heads = gate_weight.shape[1], step_bias.shape[0]
    groups = nc * nt
    if nt != 2 or seqs != nd or heads % (2 * groups) or inner % (128 * groups):
        return False
    length = tokens // nc
    return tokens * (D + inner // groups) <= 2 << 20 and length % 128 == 0 and D % (128 * nd) == 0


def solution(mesh):
    in_specs = (
        P("dp", "ctx", None),
        P("dp", "ctx"),
        P("dp", "ctx", None),
        P(),
        P("dp", "tensor"),
        P("dp", "tensor"),
        P("dp", None),
        P("dp", "tensor"),
        P(),
        P(),
        P(),
        P(),
        P(),
        P(),
        P("tensor", "dp"),
    )
    out_specs = (
        P("dp", "ctx", None),
        P("dp", "ctx", None),
        P(),
        P("dp", "tensor"),
        P("dp", "tensor"),
        P("dp", None),
        P("dp", "tensor"),
        P(),
        P(),
        P(),
        P(),
        P(),
        P(),
        P("tensor", "dp"),
    )

    def whole(*args):
        chosen = spread_body if fits(mesh, args) else body
        return jax.shard_map(chosen, mesh=mesh, in_specs=in_specs, out_specs=out_specs, check_vma=False)(*args)

    return whole
```

```python
from functools import partial

import jax
import jax.numpy as jnp
from jax import lax
from jax.experimental import pallas as pl
from jax.experimental.pallas import tpu as pltpu
from jax.sharding import PartitionSpec as P

epsilon = 1e-05
highest = lax.Precision.HIGHEST
f32, bf16 = jnp.float32, jnp.bfloat16
MESH = pl.DeviceIdType.MESH
VM = pl.BlockSpec(memory_space=pltpu.VMEM)
ANY = pl.BlockSpec(memory_space=pl.ANY)
LIMIT = 56 * 1024 * 1024


def dot(a, b, ca=1, cb=0, precision=None):
    return lax.dot_general(
        a, b, (((ca,), (cb,)), ((), ())), precision=precision, preferred_element_type=f32
    )


def shifted(array, axis, by):
    size = lax.axis_size(axis)
    pairs = [(i, i + by) for i in range(size) if 0 <= i + by < size]
    return lax.ppermute(array, axis, pairs)


def chain_kernel(axis, by, chunks, local_ref, fade_ref, out_ref, landed, outgoing, send, recv):
    size = lax.axis_size(axis)
    me = lax.axis_index(axis)
    follower = lax.rem(me + by + size, size)
    leader = lax.rem(me - by + size, size)
    first, last = (0, size - 1) if by > 0 else (size - 1, 0)
    rows = local_ref.shape[0] // chunks
    barrier = pltpu.get_barrier_semaphore()

    @pl.when(me != first)
    def _():
        pl.semaphore_signal(barrier, inc=1, device_id={axis: leader}, device_id_type=MESH)

    @pl.when(me != last)
    def _():
        pl.semaphore_wait(barrier, 1)

    def copy(c):
        part = pl.ds(c * rows, rows)
        return pltpu.make_async_remote_copy(
            src_ref=outgoing.at[part],
            dst_ref=landed.at[part],
            send_sem=send.at[c],
            recv_sem=recv.at[c],
            device_id={axis: follower},
            device_id_type=MESH,
        )

    @pl.when(me == first)
    def _():
        landed[...] = jnp.zeros_like(landed)

    for c in range(chunks):
        part = pl.ds(c * rows, rows)

        @pl.when(me != first)
        def _():
            copy(c).wait_recv()

        @pl.when(me != last)
        def _():
            total = fade_ref[part, :] * landed[part, :].astype(f32) + local_ref[part, :].astype(f32)
            outgoing[part, :] = total.astype(outgoing.dtype)
            copy(c).start()

    out_ref[...] = landed[...]

    @pl.when(me != last)
    def _():
        for c in range(chunks):
            copy(c).wait_send()


def chain(local, fade, axis, by, ident, chunks=4):
    return pl.pallas_call(
        partial(chain_kernel, axis, by, chunks),
        out_shape=jax.ShapeDtypeStruct(local.shape, local.dtype),
        in_specs=[VM, VM],
        out_specs=VM,
        scratch_shapes=[
            pltpu.VMEM(local.shape, local.dtype),
            pltpu.VMEM(local.shape, local.dtype),
            pltpu.SemaphoreType.DMA((chunks,)),
            pltpu.SemaphoreType.DMA((chunks,)),
        ],
        compiler_params=pltpu.CompilerParams(collective_id=ident, has_side_effects=True),
        name="chain",
    )(local, fade)


def pair_kernel(axis, src_ref, out_ref, slots, send, recv):
    size = lax.axis_size(axis)
    me = lax.axis_index(axis)
    barrier = pltpu.get_barrier_semaphore()
    for k in range(1, size):
        pl.semaphore_signal(
            barrier, inc=1, device_id={axis: lax.rem(me + k, size)}, device_id_type=MESH
        )
    pl.semaphore_wait(barrier, size - 1)
    copies = []
    for k in range(1, size):
        copies.append(
            pltpu.make_async_remote_copy(
                src_ref=src_ref,
                dst_ref=slots.at[k - 1],
                send_sem=send.at[k - 1],
                recv_sem=recv.at[k - 1],
                device_id={axis: lax.rem(me + k, size)},
                device_id_type=MESH,
            )
        )
        copies[-1].start()
    for copy in copies:
        copy.wait()
    total = src_ref[...].astype(f32)
    for k in range(1, size):
        total = total + slots[k - 1].astype(f32)
    out_ref[...] = total


def pair_sum(array, axis, ident):
    size = lax.axis_size(axis)
    return pl.pallas_call(
        partial(pair_kernel, axis),
        out_shape=jax.ShapeDtypeStruct(array.shape, f32),
        in_specs=[VM],
        out_specs=VM,
        scratch_shapes=[
            pltpu.VMEM((size - 1,) + array.shape, array.dtype),
            pltpu.SemaphoreType.DMA((size - 1,)),
            pltpu.SemaphoreType.DMA((size - 1,)),
        ],
        compiler_params=pltpu.CompilerParams(
            collective_id=ident, has_side_effects=True, vmem_limit_bytes=LIMIT
        ),
        name="pair_sum",
    )(array)


def gather_kernel(axis, count, *refs):
    ins, outs = refs[:count], refs[count : 2 * count]
    local, send, recv = refs[2 * count :]
    me = lax.axis_index(axis)
    low, high = lax.rem(me, 2), me // 2
    side = high * 2 + (1 - low)
    other = (1 - high) * 2 + low
    corner = (1 - high) * 2 + (1 - low)
    barrier = pltpu.get_barrier_semaphore()
    for peer in (side, other):
        pl.semaphore_signal(barrier, inc=1, device_id={axis: peer}, device_id_type=MESH)
    own = []
    for a in range(count):
        own.append(pltpu.make_async_copy(ins[a], outs[a].at[me], local.at[a]))
        own[-1].start()
    pl.semaphore_wait(barrier, 2)

    def remote(a, src, dst, slot, peer):
        return pltpu.make_async_remote_copy(
            src_ref=src,
            dst_ref=dst,
            send_sem=send.at[a, slot],
            recv_sem=recv.at[a, slot],
            device_id={axis: peer},
            device_id_type=MESH,
        )

    direct = []
    for a in range(count):
        for slot, peer in ((0, side), (1, other)):
            direct.append(remote(a, ins[a], outs[a].at[me], slot, peer))
            direct[-1].start()
    relays = []
    for a in range(count):
        half = ins[a].shape[0] // 2
        lower, upper = pl.ds(0, half), pl.ds(half, half)
        remote(a, ins[a], outs[a].at[side], 0, side).wait_recv()
        relay = remote(a, outs[a].at[side, lower], outs[a].at[side, lower], 2, other)
        relay.start()
        relays.append(relay)
        remote(a, ins[a], outs[a].at[other], 1, other).wait_recv()
        relay = remote(a, outs[a].at[other, upper], outs[a].at[other, upper], 3, side)
        relay.start()
        relays.append(relay)
    for a in range(count):
        half = ins[a].shape[0] // 2
        lower, upper = pl.ds(0, half), pl.ds(half, half)
        remote(a, outs[a].at[corner, lower], outs[a].at[corner, lower], 2, other).wait_recv()
        remote(a, outs[a].at[corner, upper], outs[a].at[corner, upper], 3, side).wait_recv()
    for copy in direct + relays:
        copy.wait_send()
    for copy in own:
        copy.wait()


def gather(arrays, axis, ident):
    size = lax.axis_size(axis)
    if size != 4:
        return tuple(lax.all_gather(a, axis) for a in arrays)
    count = len(arrays)
    return pl.pallas_call(
        partial(gather_kernel, axis, count),
        out_shape=tuple(jax.ShapeDtypeStruct((size,) + a.shape, a.dtype) for a in arrays),
        in_specs=[VM] * count,
        out_specs=tuple([VM] * count),
        scratch_shapes=[
            pltpu.SemaphoreType.DMA((count,)),
            pltpu.SemaphoreType.DMA((count, 4)),
            pltpu.SemaphoreType.DMA((count, 4)),
        ],
        compiler_params=pltpu.CompilerParams(
            collective_id=ident, has_side_effects=True, vmem_limit_bytes=LIMIT
        ),
        name="gather",
    )(*arrays)


def sigmoid(v):
    return 1.0 / (1.0 + jnp.exp(-v))


def silu(v):
    return v / (1.0 + jnp.exp(-v))


def dsilu(v):
    s = sigmoid(v)
    return s * (1.0 + v * (1.0 - s))


def softplus(v):
    return jnp.maximum(v, 0.0) + jnp.log1p(jnp.exp(-jnp.abs(v)))


def spread_pair(first_lanes, table, pair):
    return jnp.where(first_lanes, table[:, 2 * pair : 2 * pair + 1], table[:, 2 * pair + 1 : 2 * pair + 2])


def lanes_first(length, head):
    return lax.broadcasted_iota(jnp.int32, (length, 2 * head), 1) < head


def negative_mask(segc, segr):
    length = segc.shape[0]
    row = lax.broadcasted_iota(jnp.int32, (length, length), 0)
    col = lax.broadcasted_iota(jnp.int32, (length, length), 1)
    return jnp.where((segc == segr) & (row >= col), 0.0, -1e30).astype(f32)


def tails(run, segc):
    length = segc.shape[0]
    return jnp.exp(run[length - 1 : length, :] - run) * (segc == segc[length - 1 : length]).astype(f32)


def local_kernel(
    width, head, cin, same, taps, offs, raw, bias, rate, segc, segr,
    tot, intra, xs, final, delta_out, run_out, runt_out, wide,
):
    length = segc.shape[0]
    total_width = cin.shape[1]
    states = (total_width - width) // 2
    wide[...] = cin[...].astype(f32)
    lags = taps.shape[0]
    pad = cin.shape[0] - length
    for c in range(total_width // 128):
        part = slice(c * 128, c * 128 + 128)
        acc = jnp.broadcast_to(offs[:, part], (length, 128))
        for j in range(lags):
            acc = acc + taps[j : j + 1, part] * (wide[pad - j : pad - j + length, part] * same[:, j : j + 1])
        tot[:, part] = acc
    delta = softplus(raw[...] + bias[...])
    delta_out[...] = delta
    row = lax.broadcasted_iota(jnp.int32, (length, length), 0)
    col = lax.broadcasted_iota(jnp.int32, (length, length), 1)
    below = (row >= col).astype(f32)
    decay = delta * rate[...]
    run = dot(below, decay, precision=highest)
    run_out[...] = run
    runt = run.T
    runt_out[...] = runt
    b = silu(tot[:, width : width + states]).astype(bf16)
    c = silu(tot[:, width + states :]).astype(bf16)
    scores = dot(c, b, 1, 1)
    negative = negative_mask(segc[...], segr[...])
    first = lanes_first(length, head)
    tail = tails(run, segc[...])
    for pair in range(width // (2 * head)):
        part = slice(pair * 2 * head, (pair + 1) * 2 * head)
        x = (silu(tot[:, part]) * spread_pair(first, delta, pair)).astype(bf16)
        xs[:, part] = x
        x32 = x.astype(f32)
        faded = (x32 * spread_pair(first, tail, pair)).astype(bf16)
        final[part, :] = dot(faded, b, 0, 0).astype(bf16)
        total = None
        for k in range(2):
            h = 2 * pair + k
            w = (jnp.exp(run[:, h : h + 1] - runt[h : h + 1, :] + negative) * scores).astype(bf16)
            xk = jnp.where(first if k == 0 else ~first, x32, 0.0).astype(bf16)
            term = dot(w, xk)
            total = term if total is None else total + term
        intra[:, part] = total


def entries(run, segc, before):
    return jnp.exp(run) * (segc == before).astype(f32)


def product_kernel(
    width, head, inner, ctot_ref, tot, intra, entering, run, segc, before, gate, gg, gain, skip, ysum, sums,
):
    length = segc.shape[0]
    first = lanes_first(length, head)
    c = silu(ctot_ref[...]).astype(bf16)
    entry = entries(run[...], segc[...], before[...])
    squares = jnp.zeros((length, 1), f32)
    project = jnp.zeros((length, 1), f32)
    for pair in range(width // (2 * head)):
        part = slice(pair * 2 * head, (pair + 1) * 2 * head)
        y = intra[:, part] + dot(c, entering[part, :], 1, 1) * spread_pair(first, entry, pair)
        ysum[:, part] = y
        mixed = y + spread_pair(first[:1], skip[...], pair) * silu(tot[:, part])
        product = mixed * silu(gate[:, part])
        squares = squares + jnp.sum(product * product, axis=1, keepdims=True)
        project = project + jnp.sum(gg[:, part] * gain[:, part] * product, axis=1, keepdims=True)
    lane = lax.broadcasted_iota(jnp.int32, sums.shape, 1)
    sums[...] = jnp.where(lane == 0, squares, jnp.where(lane == 1, project, 0.0))


def norm_kernel(
    width, head, inner, ctot_ref, tot, ysum, run, segc, before, gate, gg, gain, skip, sums,
    gated, low_gate, gm, grad_entering, grad_gain,
):
    length = segc.shape[0]
    first = lanes_first(length, head)
    c = silu(ctot_ref[...]).astype(bf16)
    entry = entries(run[...], segc[...], before[...])
    scale = lax.rsqrt(sums[:, 0:1] / inner + epsilon)
    project = scale * sums[:, 1:2] / inner
    for pair in range(width // (2 * head)):
        part = slice(pair * 2 * head, (pair + 1) * 2 * head)
        mixed = ysum[:, part] + spread_pair(first[:1], skip[...], pair) * silu(tot[:, part])
        z = gate[:, part]
        sg = sigmoid(z)
        act = z * sg
        unit = mixed * act * scale
        gated[:, part] = (unit * gain[:, part]).astype(bf16)
        g = gg[:, part]
        grad_gain[:, part] = jnp.sum(g * unit, axis=0, keepdims=True)
        gp = scale * (g * gain[:, part] - unit * project)
        gmix = gp * act
        low_gate[:, part] = (gp * mixed * sg * (1.0 + z * (1.0 - sg))).astype(bf16)
        gmb = gmix.astype(bf16)
        gm[:, part] = gmb
        scaled = (gmb.astype(f32) * spread_pair(first, entry, pair)).astype(bf16)
        grad_entering[part, :] = dot(scaled, c, 0, 0).astype(bf16)


def back_kernel(
    width, head, gm, xs, ysum, tot, cin, same, taps, raw, bias, rate, skip, delta_in, run_in, runt_in,
    segc, segr, before, entering, leaving,
    gpad, gtaps, goffs, graw, gheads, dtot, wide,
):
    length = segc.shape[0]
    heads = width // head
    total_width = tot.shape[1]
    states = (total_width - width) // 2
    first = lanes_first(length, head)
    run, runt, delta = run_in[...], runt_in[...], delta_in[...]
    negative = negative_mask(segc[...], segr[...])
    b = silu(tot[:, width : width + states]).astype(bf16)
    c = silu(tot[:, width + states :]).astype(bf16)
    scores = dot(c, b, 1, 1)
    tail = tails(run, segc[...])
    entry = entries(run, segc[...], before[...])
    dscores = jnp.zeros((length, length), f32)
    u = jnp.zeros((length, heads), f32)
    q = jnp.zeros((1, heads), f32)
    vdx = jnp.zeros((length, heads), f32)
    gv = jnp.zeros((1, heads), f32)
    ge = jnp.zeros((1, heads), f32)
    db = jnp.zeros((length, states), f32)
    dc = jnp.zeros((length, states), f32)
    chan = lax.broadcasted_iota(jnp.int32, (2 * head, heads), 0)
    which = lax.broadcasted_iota(jnp.int32, (2 * head, heads), 1)
    for pair in range(heads // 2):
        part = slice(pair * 2 * head, (pair + 1) * 2 * head)
        pick = (which == 2 * pair + (chan >= head).astype(jnp.int32)).astype(f32)
        x = xs[:, part]
        x32 = x.astype(f32)
        g = gm[:, part]
        g32 = g.astype(f32)
        tl = spread_pair(first, tail, pair)
        grad_f = leaving[part, :]
        late = dot(b, grad_f, 1, 1) * tl
        dx = late
        for k in range(2):
            h = 2 * pair + k
            lanes = first if k == 0 else ~first
            gk = jnp.where(lanes, g32, 0.0).astype(bf16)
            decay = jnp.exp(run[:, h : h + 1] - runt[h : h + 1, :] + negative)
            w = (decay * scores).astype(bf16)
            dscores = dscores + decay * dot(gk, x, 1, 1)
            dx = dx + dot(w, gk, 0, 0)
        raw_v = tot[:, part]
        sg = sigmoid(raw_v)
        v = raw_v * sg
        u = u + dot(g32 * ysum[:, part] - x32 * dx, pick, precision=highest)
        q = q + jnp.sum(dot(x32 * late, pick, precision=highest), axis=0, keepdims=True)
        vdx = vdx + dot(v * dx, pick, precision=highest)
        gv = gv + dot(jnp.sum(g32 * v, axis=0, keepdims=True), pick, precision=highest)
        per_row = jnp.sum(grad_f.astype(f32) * entering[part, :].astype(f32), axis=1, keepdims=True)
        ge = ge + jnp.sum(per_row * pick, axis=0, keepdims=True)
        dv = spread_pair(first, delta, pair) * dx + spread_pair(first[:1], skip[...], pair) * g32
        dtot[:, part] = dv * (sg * (1.0 + raw_v * (1.0 - sg)))
        db = db + dot((x32 * tl).astype(bf16), grad_f)
        dc = dc + dot((g32 * spread_pair(first, entry, pair)).astype(bf16), entering[part, :])
    dsb = dscores.astype(bf16)
    dc = dc + dot(dsb, b)
    db = db + dot(dsb, c, 0, 0)
    dtot[:, width : width + states] = db * dsilu(tot[:, width : width + states])
    dtot[:, width + states :] = dc * dsilu(tot[:, width + states :])
    row = lax.broadcasted_iota(jnp.int32, (length, length), 0)
    col = lax.broadcasted_iota(jnp.int32, (length, length), 1)
    above = (row <= col).astype(f32)
    last = slice(length - 1, length)
    dld = dot(above, u, precision=highest) + (q + entry[last, :] * ge)
    ddelta = dld * rate[...] + vdx
    gr = ddelta * sigmoid(raw[...] + bias[...])
    graw[...] = gr
    gheads[...] = jnp.zeros_like(gheads)
    gheads[0:1, :] = jnp.sum(gr, axis=0, keepdims=True)
    gheads[1:2, :] = jnp.sum(dld * delta, axis=0, keepdims=True) * rate[...]
    gheads[2:3, :] = gv
    wide[...] = cin[...].astype(f32)
    gpad[...] = jnp.zeros_like(gpad)
    lags = taps.shape[0]
    pad = cin.shape[0] - length
    for n in range(total_width // 128):
        part = slice(n * 128, n * 128 + 128)
        d = dtot[:, part]
        goffs[:, part] = jnp.sum(d, axis=0, keepdims=True)
        for j in range(lags):
            ds = d * same[:, j : j + 1]
            window = slice(pad - j, pad - j + length)
            gtaps[j : j + 1, part] = jnp.sum(ds * wide[window, part], axis=0, keepdims=True)
            gpad[window, part] = gpad[window, part] + ds * taps[j : j + 1, part]


def call(kernel, outs, args, scratch=(), name=None):
    return pl.pallas_call(
        kernel,
        out_shape=tuple(jax.ShapeDtypeStruct(s, d) for s, d in outs),
        in_specs=[VM] * len(args),
        out_specs=tuple([VM] * len(outs)),
        scratch_shapes=list(scratch),
        compiler_params=pltpu.CompilerParams(vmem_limit_bytes=LIMIT),
        name=name,
    )(*args)


def body(
    hidden,
    segment_ids,
    cotangent,
    input_gain,
    gate_weight,
    value_weight,
    state_weight,
    step_weight,
    conv_weight,
    conv_bias,
    step_bias,
    decay_log,
    skip_gain,
    mixer_gain,
    out_weight,
):
    tokens = hidden[0]
    wrapped = segment_ids[0] % 128
    cot = cotangent[0]
    length, width_in = tokens.shape
    shard = lax.axis_index("tensor")
    shards = lax.axis_size("tensor")
    lags = conv_weight.shape[0]
    reach = lags - 1
    dp = lax.axis_size("dp")
    width = gate_weight.shape[1]
    local_heads = step_weight.shape[1]
    head = width // local_heads
    inner = width * shards
    states = state_weight.shape[1] // 2
    ids_col = jnp.broadcast_to(wrapped[length - reach :].astype(bf16)[:, None], (reach, 128))
    edge = shifted(jnp.concatenate([tokens[length - reach :], ids_col], 1), "ctx", 1)
    narrow = jnp.concatenate(
        [state_weight, step_weight, jnp.zeros((state_weight.shape[0], 128 - local_heads), bf16)], 1
    )
    g_gate, g_value, g_narrow, g_out = gather(
        (gate_weight, value_weight, narrow, out_weight), "dp", 0
    )
    full_gate = g_gate.reshape(width_in, width)
    full_value = g_value.reshape(width_in, width)
    full_narrow = g_narrow.reshape(width_in, narrow.shape[1])
    full_out = jnp.concatenate([g_out[k] for k in range(dp)], 1)
    pad = 8
    base_ext = jnp.concatenate(
        [jnp.zeros((pad - reach, width_in), bf16), edge[:, :width_in], tokens], 0
    ).astype(f32)
    inv_ext = lax.rsqrt(jnp.mean(base_ext * base_ext, axis=-1, keepdims=True) + epsilon)
    normed_ext = (base_ext * inv_ext * input_gain).astype(bf16)
    normed = normed_ext[pad:]
    base = tokens.astype(f32)
    inv = inv_ext[pad:]
    gate = jnp.dot(normed, full_gate, preferred_element_type=f32)
    value_pre = jnp.dot(normed_ext, full_value, preferred_element_type=f32)
    rest_pre = jnp.dot(normed_ext, full_narrow, preferred_element_type=f32)
    cin = jnp.concatenate([value_pre.astype(bf16), rest_pre[:, : 2 * states].astype(bf16)], 1)
    raw_step = rest_pre[pad:, 2 * states : 2 * states + local_heads]
    grad_gated = jnp.dot(cot, full_out.T, preferred_element_type=f32)

    padded_ids = jnp.concatenate([edge[:, width_in].astype(jnp.int32), wrapped])
    before = padded_ids[reach - 1].astype(f32).reshape(1, 1)
    same = jnp.stack(
        [
            (padded_ids[reach - j : reach - j + length] == wrapped).astype(f32)
            for j in range(lags)
        ],
        1,
    )
    segc = wrapped.astype(f32)[:, None]
    segr = wrapped.astype(f32)[None, :]

    def local(array, size):
        return lax.dynamic_slice_in_dim(array, shard * size, size, array.ndim - 1)

    taps = jnp.concatenate([local(conv_weight, width), conv_weight[:, inner:]], 1)
    offs = jnp.concatenate([local(conv_bias, width), conv_bias[inner:]], 0)[None]
    bias = local(step_bias, local_heads)[None]
    rate = -jnp.exp(local(decay_log, local_heads))[None]
    skip = local(skip_gain, local_heads)[None]
    gain = local(mixer_gain, width)[None]
    total_width = width + 2 * states

    tot, intra, xs, final, delta, run, runt = call(
        partial(local_kernel, width, head),
        (
            ((length, total_width), f32),
            ((length, width), f32),
            ((length, width), bf16),
            ((width, states), bf16),
            ((length, local_heads), f32),
            ((length, local_heads), f32),
            ((local_heads, length), f32),
        ),
        (cin, same, taps, offs, raw_step, bias, rate, segc, segr),
        (pltpu.VMEM((length + pad, total_width), f32),),
        "mixer_local",
    )
    through = jnp.exp(run[length - 1]) * (segc[length - 1] == before[0]).astype(f32)
    fade = jnp.broadcast_to(jnp.repeat(through, head)[:, None], (width, 128))
    entering = chain(final, fade, "ctx", 1, 1)
    ctot = tot[:, width + states :]
    ysum, sums = call(
        partial(product_kernel, width, head, inner),
        (((length, width), f32), ((length, 128), f32)),
        (ctot, tot, intra, entering, run, segc, before, gate, grad_gated, gain, skip),
        (),
        "mixer_product",
    )
    sums = pair_sum(sums, "tensor", 2)
    gated, low_gate, gm, grad_entering, grad_mgain = call(
        partial(norm_kernel, width, head, inner),
        (
            ((length, width), bf16),
            ((length, width), bf16),
            ((length, width), bf16),
            ((width, states), bf16),
            ((1, width), f32),
        ),
        (ctot, tot, ysum, run, segc, before, gate, grad_gated, gain, skip, sums),
        (),
        "mixer_norm",
    )
    grad_out = jnp.dot(gated.T, cot, preferred_element_type=f32).astype(bf16)
    grad_gate_w = jnp.dot(normed.T, low_gate, preferred_element_type=f32).astype(bf16)
    out_piece = lax.psum_scatter(grad_out, "dp", scatter_dimension=1, tiled=True)
    gate_piece = lax.psum_scatter(grad_gate_w, "dp", scatter_dimension=0, tiled=True)
    leaving = chain(grad_entering, fade, "ctx", -1, 3)
    gpad, gtaps, goffs, graw, gheads = call(
        partial(back_kernel, width, head),
        (
            ((length + pad, total_width), f32),
            ((lags, total_width), f32),
            ((1, total_width), f32),
            ((length, local_heads), f32),
            ((8, local_heads), f32),
        ),
        (
            gm, xs, ysum, tot, cin, same, taps, raw_step, bias, rate, skip, delta, run, runt,
            segc, segr, before, entering, leaving,
        ),
        (pltpu.VMEM((length, total_width), f32), pltpu.VMEM((length + pad, total_width), f32)),
        "mixer_back",
    )
    edge_grad = shifted(gpad[pad - reach : pad], "ctx", -1)
    grad_input = jnp.concatenate(
        [gpad[pad : pad + length - 8], gpad[pad + length - 8 :] + jnp.pad(edge_grad, ((8 - reach, 0), (0, 0)))], 0
    )
    low_value = grad_input[:, :width].astype(bf16)
    low_rest = jnp.concatenate(
        [
            grad_input[:, width:].astype(bf16),
            graw.astype(bf16),
            jnp.zeros((length, 128 - local_heads), bf16),
        ],
        1,
    )
    low_tail = jnp.concatenate([low_value, low_rest], 1)
    grad_tail_w = jnp.dot(normed.T, low_tail, preferred_element_type=f32).astype(bf16)
    tail_piece = lax.psum_scatter(grad_tail_w, "dp", scatter_dimension=0, tiled=True)
    branch_out = jnp.dot(gated, full_out, preferred_element_type=f32).astype(bf16)
    normed_part = (
        jnp.dot(low_gate, full_gate.T, preferred_element_type=f32)
        + jnp.dot(low_value, full_value.T, preferred_element_type=f32)
        + jnp.dot(low_rest, full_narrow.T, preferred_element_type=f32)
    ).astype(bf16)
    both = pair_sum(jnp.concatenate([branch_out, normed_part], 0), "tensor", 4)
    result = (base + both[:length]).astype(bf16)
    gn = both[length:]
    grad_gain = jnp.sum(gn * base * inv, axis=0)
    gs = gn * input_gain
    grad_base = inv * (gs - base * (inv * inv) * jnp.mean(gs * base, axis=-1, keepdims=True))
    grad_tokens = cot.astype(f32) + grad_base

    out_sum = lax.psum(out_piece, "ctx").astype(f32)
    gate_sum = lax.psum(gate_piece, "ctx").astype(f32)
    tail_sum = lax.psum(tail_piece, "ctx")
    state_sum = pair_sum(tail_sum[:, width : width + 2 * states], "tensor", 5)

    mine = (shard == 0).astype(f32)

    def placed(array, size):
        spots = [jnp.where(shard == k, array, 0.0) for k in range(shards)]
        return jnp.concatenate(spots, -1)

    small = jnp.concatenate(
        [
            (grad_gain * mine)[None],
            jnp.concatenate([placed(gtaps[:, :width], width), gtaps[:, width:]], 1).reshape(1, -1),
            jnp.concatenate([placed(goffs[:, :width], width), goffs[:, width:]], 1),
            placed(grad_mgain, width),
            placed(gheads[0:1], local_heads),
            placed(gheads[1:2], local_heads),
            placed(gheads[2:3], local_heads),
        ],
        1,
    )
    sizes = [width_in, lags * (inner + 2 * states), inner + 2 * states, inner]
    sizes = sizes + [local_heads * shards] * 3
    totals = lax.psum(small, ("dp", "ctx", "tensor"))[0]
    parts, at = [], 0
    for size in sizes:
        parts.append(totals[at : at + size])
        at += size
    return (
        result[None],
        grad_tokens[None],
        parts[0],
        gate_sum,
        tail_sum[:, :width].astype(f32),
        state_sum,
        tail_sum[:, width + 2 * states : width + 2 * states + local_heads].astype(f32),
        parts[1].reshape(lags, inner + 2 * states),
        parts[2],
        parts[4],
        parts[5],
        parts[6],
        parts[3],
        out_sum,
    )


def rot(me, k, size):
    return lax.rem(me + k + size, size)


def remote(src, dst, send, recv, device):
    return pltpu.make_async_remote_copy(
        src_ref=src, dst_ref=dst, send_sem=send, recv_sem=recv, device_id=device, device_id_type=MESH
    )


def greet(barrier, device):
    pl.semaphore_signal(barrier, inc=1, device_id=device, device_id_type=MESH)


def spot(index, size):
    return pl.ds(pl.multiple_of(index * size, size), size)


def inside(index, size):
    return (index >= 0) & (index < size)


class Line:
    def __init__(self, own, at, send, recv, onward=None):
        self.own, self.at, self.send, self.recv, self.onward = own, at, send, recv, onward
        self.me, self.size = lax.axis_index("ctx"), lax.axis_size("ctx")

    def hop(self, w, s):
        way = (1, -1)[w]
        block = self.me - way * s
        src = self.own if s == 0 else self.at(block)
        return remote(src, self.at(block), self.send.at[w, s], self.recv.at[w, s], {"ctx": self.me + way})

    def start(self):
        for w, way in enumerate((1, -1)):
            @pl.when(inside(self.me + way, self.size))
            def _(w=w):
                self.hop(w, 0).start()

    def step(self, s):
        for w, way in enumerate((1, -1)):
            block = self.me - way * (s + 1)

            @pl.when(inside(block, self.size))
            def _(w=w, way=way, block=block):
                ref = self.at(block)
                remote(ref, ref, self.send.at[w, s], self.recv.at[w, s], {"ctx": self.me - way}).wait_recv()
                if s + 1 < self.size - 1:
                    @pl.when(inside(self.me + way, self.size))
                    def _():
                        self.hop(w, s + 1).start()
                if self.onward is not None:
                    self.onward(block, w, s).start()

    def finish(self):
        for s in range(self.size - 1):
            for w, way in enumerate((1, -1)):
                @pl.when(inside(self.me + way, self.size) & inside(self.me - way * s, self.size))
                def _(w=w, s=s):
                    self.hop(w, s).wait_send()

    def arrived(self):
        for s in range(self.size - 1):
            for w, way in enumerate((1, -1)):
                block = self.me - way * (s + 1)

                @pl.when(inside(block, self.size))
                def _(w=w, s=s, block=block):
                    self.onward(block, w, s).wait()


def greet_line(barrier):
    c, nc = lax.axis_index("ctx"), lax.axis_size("ctx")
    for way in (1, -1):
        @pl.when(inside(c + way, nc))
        def _(way=way):
            greet(barrier, {"ctx": c + way})


def line_peers():
    c, nc = lax.axis_index("ctx"), lax.axis_size("ctx")
    return (c > 0).astype(jnp.int32) + (c < nc - 1).astype(jnp.int32)


def collect_kernel(
    hid, cot, ids, wg, wv, ws, wst, wo, H, CF, IDS, WG, WV, WS, WST, WO, zs, zr, fs, fr, ds, dr,
):
    c, d, t = lax.axis_index("ctx"), lax.axis_index("dp"), lax.axis_index("tensor")
    nc, nd = lax.axis_size("ctx"), lax.axis_size("dp")
    half = hid.shape[0] // 2
    chans = WG.shape[2]
    wide = WST.shape[1] // nd
    barrier = pltpu.get_barrier_semaphore()
    greet(barrier, {"tensor": 1 - t})
    for k in range(1, nd):
        greet(barrier, {"dp": rot(d, k, nd)})
    greet_line(barrier)
    pl.semaphore_wait(barrier, nd + line_peers())

    def line(a, own, out):
        def at(block):
            return out.at[block, spot(t, half)]

        def onward(block, w, s):
            ref = at(block)
            return remote(ref, ref, fs.at[a, w, s], fr.at[a, w, s], {"tensor": 1 - t})

        return Line(own.at[spot(t, half)], at, zs.at[a], zr.at[a], onward)

    lines = [line(0, hid, H), line(1, cot, CF)]
    small = Line(ids, lambda block: IDS.at[block], zs.at[2], zr.at[2])
    small.start()
    lines[0].start()
    moves = (
        (wv.at[:, spot(c, chans)], WV.at[d]),
        (wg.at[:, spot(c, chans)], WG.at[d]),
        (ws, WS.at[d]),
        (wst, WST.at[:, spot(d, wide)]),
        (wo.at[spot(c, chans), :], WO.at[:, spot(d, wide)]),
    )
    sent = []
    for a, (src, dst) in enumerate(moves):
        for k in range(1, nd):
            sent.append(remote(src, dst, ds.at[a, k - 1], dr.at[a, k - 1], {"dp": rot(d, k, nd)}))
            sent[-1].start()
    lines[1].start()
    H[c] = hid[...]
    CF[c] = cot[...]
    IDS[c] = ids[...]
    WV[d] = wv[:, spot(c, chans)]
    WG[d] = wg[:, spot(c, chans)]
    WS[d] = ws[...]
    WST[:, spot(d, wide)] = wst[...]
    WO[:, spot(d, wide)] = wo[spot(c, chans), :]
    for s in range(nc - 1):
        small.step(s)
        for item in lines:
            item.step(s)
    landed = (
        lambda r: WV.at[r], lambda r: WG.at[r], lambda r: WS.at[r],
        lambda r: WST.at[:, spot(r, wide)], lambda r: WO.at[:, spot(r, wide)],
    )
    for a, at in enumerate(landed):
        for k in range(1, nd):
            ref = at(rot(d, -k, nd))
            remote(ref, ref, ds.at[a, k - 1], dr.at[a, k - 1], {"dp": rot(d, -k, nd)}).wait_recv()
    for copy in sent:
        copy.wait_send()
    small.finish()
    for item in lines:
        item.finish()
        item.arrived()


def chunk_masks(segp, at, length, lags):
    segc = segp[at : at + length, 0:1]
    return segc, [(segp[at - j : at - j + length, 0:1] == segc).astype(f32) for j in range(lags)]


def fades(through, pair, head, rows):
    low = lax.broadcasted_iota(jnp.int32, (rows, 1), 0) < head
    return jnp.where(low, through[:, 2 * pair : 2 * pair + 1], through[:, 2 * pair + 1 : 2 * pair + 2])


def forward_kernel(
    head, hid, cot, ids, wg, wv, ws, wst, wo, in_gain, cw, cb, mg, hp,
    normed, gate, gg, cin, tot, xs, ysum, ent, delta, run, runt, raw, sums, segp, taps, offs, gain, invs, state,
):
    c, t = lax.axis_index("ctx"), lax.axis_index("tensor")
    nc = lax.axis_size("ctx")
    chunks, _, length = ids.shape
    width = wg.shape[1]
    states = ws.shape[1] // 2
    pairs = width // (2 * head)
    lags = cw.shape[0]
    inner = mg.shape[1]
    pad = 8
    mine = spot(t * nc + c, width)
    taps[:, :width] = cw[:, mine]
    taps[:, width:] = cw[:, inner:]
    offs[:, :width] = cb[:, mine]
    offs[:, width:] = cb[:, inner:]
    gain[...] = mg[:, mine]
    segp[:pad, :] = jnp.full((pad, segp.shape[1]), -1.0, f32)
    for k in range(chunks):
        segp[pad + k * length : pad + (k + 1) * length, :] = ids[k].T
    cin[:pad, :] = jnp.zeros((pad, cin.shape[1]), f32)
    state[...] = jnp.zeros_like(state)
    sums[...] = jnp.zeros_like(sums)
    row = lax.broadcasted_iota(jnp.int32, (length, length), 0)
    col = lax.broadcasted_iota(jnp.int32, (length, length), 1)
    below = (row >= col).astype(f32)
    first = lanes_first(length, head)
    bias, rate, skip = hp[0:1, :], hp[1:2, :], hp[2:3, :]
    for k in range(chunks):
        rows = slice(k * length, (k + 1) * length)
        at = pad + k * length
        base = hid[rows, :].astype(f32)
        inv = lax.rsqrt(jnp.mean(base * base, axis=-1, keepdims=True) + epsilon)
        invs[rows, :] = inv
        nb = (base * inv * in_gain[...]).astype(bf16)
        normed[rows, :] = nb
        gate[rows, :] = dot(nb, wg[...])
        cin[at : at + length, :width] = dot(nb, wv[...]).astype(bf16).astype(f32)
        cin[at : at + length, width:] = dot(nb, ws[...]).astype(bf16).astype(f32)
        rawk = dot(nb, wst[...], 1, 1)
        raw[rows, :] = rawk
        gg[rows, :] = dot(cot[rows, :], wo[...], 1, 1)
        segc, same = chunk_masks(segp, at, length, lags)
        segr = ids[k, 0:1, :]
        before = segp[at - 1 : at, 0:1]
        for n in range(cin.shape[1] // 128):
            part = slice(n * 128, n * 128 + 128)
            acc = jnp.broadcast_to(offs[:, part], (length, 128))
            for j in range(lags):
                acc = acc + taps[j : j + 1, part] * (cin[at - j : at - j + length, part] * same[j])
            tot[rows, part] = acc
        dk = softplus(rawk + bias)
        delta[rows, :] = dk
        rk = dot(below, dk * rate, precision=highest)
        run[rows, :] = rk
        rkt = rk.T
        runt[k] = rkt
        b = silu(tot[rows, width : width + states]).astype(bf16)
        cc = silu(tot[rows, width + states :]).astype(bf16)
        scores = dot(cc, b, 1, 1)
        negative = negative_mask(segc, segr)
        tail = tails(rk, segc)
        entry = entries(rk, segc, before)
        through = entry[length - 1 : length, :]
        squares = jnp.zeros((length, 1), f32)
        project = jnp.zeros((length, 1), f32)
        for pair in range(pairs):
            part = slice(pair * 2 * head, (pair + 1) * 2 * head)
            values = silu(tot[rows, part])
            x = (values * spread_pair(first, dk, pair)).astype(bf16)
            xs[rows, part] = x
            x32 = x.astype(f32)
            faded = (x32 * spread_pair(first, tail, pair)).astype(bf16)
            old = state[part, :]
            entering = old.astype(bf16)
            ent[k, part, :] = entering
            state[part, :] = fades(through, pair, head, 2 * head) * old + dot(faded, b, 0, 0)
            y = dot(cc, entering, 1, 1) * spread_pair(first, entry, pair)
            for m in range(2):
                h = 2 * pair + m
                w = (jnp.exp(rk[:, h : h + 1] - rkt[h : h + 1, :] + negative) * scores).astype(bf16)
                xk = jnp.where(first if m == 0 else ~first, x32, 0.0).astype(bf16)
                y = y + dot(w, xk)
            ysum[rows, part] = y
            mixed = y + spread_pair(first[:1], skip, pair) * values
            product = mixed * silu(gate[rows, part])
            squares = squares + jnp.sum(product * product, axis=1, keepdims=True)
            project = project + jnp.sum(gg[rows, part] * gain[:, part] * product, axis=1, keepdims=True)
        lane = lax.broadcasted_iota(jnp.int32, (length, 128), 1)
        both = jnp.where(lane == 0, squares, jnp.where(lane == 1, project, 0.0))
        sums[2 * k : 2 * k + 2, :] = both.T[0:2, :]


def gate_kernel(
    head, inner, sums, tot, ysum, gate, gg, gain, hp, cf, wo, normed,
    low_gate, gm, grad_gain, br, go, gw, gated, slots, send, recv,
):
    c, t = lax.axis_index("ctx"), lax.axis_index("tensor")
    nc, nt = lax.axis_size("ctx"), lax.axis_size("tensor")
    total = nc * nt
    length = sums.shape[1]
    width = gate.shape[1]
    me = c * nt + t
    barrier = pltpu.get_barrier_semaphore()

    def peer(k):
        r = rot(me, k, total)
        return r, {"ctx": r // nt, "tensor": lax.rem(r, nt)}

    for k in range(1, total):
        greet(barrier, peer(k)[1])
    slots[me] = sums[...]
    pl.semaphore_wait(barrier, total - 1)
    sent = []
    for k in range(1, total):
        sent.append(remote(sums, slots.at[me], send.at[k - 1], recv.at[k - 1], peer(k)[1]))
        sent[-1].start()
    for k in range(1, total):
        r, device = peer(-k)
        remote(sums, slots.at[r], send.at[k - 1], recv.at[k - 1], device).wait_recv()
    added = slots[0]
    for r in range(1, total):
        added = added + slots[r]
    added = added.T
    first = lanes_first(length, head)
    skip = hp[2:3, :]
    grad_gain[...] = jnp.zeros_like(grad_gain)
    for k in range(gate.shape[0] // length):
        rows = slice(k * length, (k + 1) * length)
        scale = lax.rsqrt(added[:, 2 * k : 2 * k + 1] / inner + epsilon)
        project = scale * added[:, 2 * k + 1 : 2 * k + 2] / inner
        for pair in range(width // (2 * head)):
            part = slice(pair * 2 * head, (pair + 1) * 2 * head)
            mixed = ysum[rows, part] + spread_pair(first[:1], skip, pair) * silu(tot[rows, part])
            z = gate[rows, part]
            sg = sigmoid(z)
            act = z * sg
            unit = mixed * act * scale
            gated[rows, part] = (unit * gain[:, part]).astype(bf16)
            g = gg[rows, part]
            grad_gain[:, part] = grad_gain[:, part] + jnp.sum(g * unit, axis=0, keepdims=True)
            gp = scale * (g * gain[:, part] - unit * project)
            low_gate[rows, part] = (gp * mixed * sg * (1.0 + z * (1.0 - sg))).astype(bf16)
            gm[rows, part] = (gp * act).astype(bf16)
        branch = dot(gated[rows, :], wo[...]).astype(bf16)
        half = length // 2
        br[k, 0] = branch[:half]
        br[k, 1] = branch[half:]
    go[...] = dot(gated[...], cf[...], 0, 0).astype(bf16)
    gw[...] = dot(low_gate[...], normed[...], 0, 0).astype(bf16)
    for copy in sent:
        copy.wait_send()


def backward_chunk(
    k, head, gm, xs, ysum, tot, cin, segp, ids, taps, raw, hp, delta_in, run_in, runt_in, ent,
    low_value, low_state, low_step, small, gheads, state, dtot, gpad,
):
    length = ids.shape[2]
    width = gm.shape[1]
    heads = raw.shape[1]
    total_width = tot.shape[1]
    states = (total_width - width) // 2
    lags = taps.shape[0]
    pad = cin.shape[0] - tot.shape[0]
    first = lanes_first(length, head)
    bias, rate, skip = hp[0:1, :], hp[1:2, :], hp[2:3, :]
    chan = lax.broadcasted_iota(jnp.int32, (2 * head, heads), 0)
    which = lax.broadcasted_iota(jnp.int32, (2 * head, heads), 1)
    row = lax.broadcasted_iota(jnp.int32, (length, length), 0)
    col = lax.broadcasted_iota(jnp.int32, (length, length), 1)
    above = (row <= col).astype(f32)
    rows = slice(k * length, (k + 1) * length)
    at = pad + k * length
    segc, same = chunk_masks(segp, at, length, lags)
    segr = ids[k, 0:1, :]
    before = segp[at - 1 : at, 0:1]
    run, runt, delta = run_in[rows, :], runt_in[k], delta_in[rows, :]
    negative = negative_mask(segc, segr)
    b = silu(tot[rows, width : width + states]).astype(bf16)
    c = silu(tot[rows, width + states :]).astype(bf16)
    scores = dot(c, b, 1, 1)
    tail = tails(run, segc)
    entry = entries(run, segc, before)
    through = entry[length - 1 : length, :]
    dscores = jnp.zeros((length, length), f32)
    u = jnp.zeros((length, heads), f32)
    q = jnp.zeros((1, heads), f32)
    vdx = jnp.zeros((length, heads), f32)
    gv = jnp.zeros((1, heads), f32)
    ge = jnp.zeros((1, heads), f32)
    db = jnp.zeros((length, states), f32)
    dc = jnp.zeros((length, states), f32)
    for pair in range(width // (2 * head)):
        part = slice(pair * 2 * head, (pair + 1) * 2 * head)
        pick = (which == 2 * pair + (chan >= head).astype(jnp.int32)).astype(f32)
        x = xs[rows, part]
        x32 = x.astype(f32)
        g32 = gm[rows, part].astype(f32)
        tl = spread_pair(first, tail, pair)
        grad_f32 = state[part, :]
        grad_f = grad_f32.astype(bf16)
        entering = ent[k, part, :]
        late = dot(b, grad_f, 1, 1) * tl
        dx = late
        for m in range(2):
            h = 2 * pair + m
            lanes = first if m == 0 else ~first
            gk = jnp.where(lanes, g32, 0.0).astype(bf16)
            decay = jnp.exp(run[:, h : h + 1] - runt[h : h + 1, :] + negative)
            w = (decay * scores).astype(bf16)
            dscores = dscores + decay * dot(gk, x, 1, 1)
            dx = dx + dot(w, gk, 0, 0)
        raw_v = tot[rows, part]
        sg = sigmoid(raw_v)
        v = raw_v * sg
        u = u + dot(g32 * ysum[rows, part] - x32 * dx, pick, precision=highest)
        q = q + dot(jnp.sum(x32 * late, axis=0, keepdims=True), pick, precision=highest)
        vdx = vdx + dot(v * dx, pick, precision=highest)
        gv = gv + dot(jnp.sum(g32 * v, axis=0, keepdims=True), pick, precision=highest)
        per_row = jnp.sum(grad_f32 * entering.astype(f32), axis=1, keepdims=True)
        ge = ge + jnp.sum(per_row * pick, axis=0, keepdims=True)
        dv = spread_pair(first, delta, pair) * dx + spread_pair(first[:1], skip, pair) * g32
        dtot[:, part] = dv * (sg * (1.0 + raw_v * (1.0 - sg)))
        db = db + dot((x32 * tl).astype(bf16), grad_f)
        scaled = (g32 * spread_pair(first, entry, pair)).astype(bf16)
        dc = dc + dot(scaled, entering)
        state[part, :] = fades(through, pair, head, 2 * head) * grad_f32 + dot(scaled, c, 0, 0)
    dsb = dscores.astype(bf16)
    dc = dc + dot(dsb, b)
    db = db + dot(dsb, c, 0, 0)
    dtot[:, width : width + states] = db * dsilu(tot[rows, width : width + states])
    dtot[:, width + states :] = dc * dsilu(tot[rows, width + states :])
    dld = dot(above, u, precision=highest) + (q + through * ge)
    ddelta = dld * rate + vdx
    gr = ddelta * sigmoid(raw[rows, :] + bias)
    low_step[rows, :] = gr.astype(bf16)
    gheads[0:1, :] = gheads[0:1, :] + jnp.sum(gr, axis=0, keepdims=True)
    gheads[1:2, :] = gheads[1:2, :] + jnp.sum(dld * delta, axis=0, keepdims=True) * rate
    gheads[2:3, :] = gheads[2:3, :] + gv
    for n in range(total_width // 128):
        part = slice(n * 128, n * 128 + 128)
        d = dtot[:, part]
        small[lags : lags + 1, part] = small[lags : lags + 1, part] + jnp.sum(d, axis=0, keepdims=True)
        for j in range(lags):
            ds = d * same[j]
            window = slice(at - j, at - j + length)
            small[j : j + 1, part] = small[j : j + 1, part] + jnp.sum(ds * cin[window, part], axis=0, keepdims=True)
            gpad[window, part] = gpad[window, part] + ds * taps[j : j + 1, part]
    low_value[rows, :] = gpad[at : at + length, :width].astype(bf16)
    low_state[rows, :] = gpad[at : at + length, width:].astype(bf16)


def ranked(slots):
    total = slots[0].astype(f32)
    for r in range(1, slots.shape[0]):
        total = total + slots[r].astype(f32)
    return total


class Shed:
    def __init__(self, own, slot, stage, send, recv):
        self.own, self.slot, self.stage, self.send, self.recv = own, slot, stage, send, recv
        self.me, self.size = lax.axis_index("ctx"), lax.axis_size("ctx")

    def hop(self, w, b):
        way = (1, -1)[w]
        return remote(
            self.stage.at[w, b], self.slot.at[w, b], self.send.at[w, b], self.recv.at[w, b], {"ctx": self.me + way}
        )

    def step(self, i):
        far = self.size - 1 - i
        for w, way in enumerate((1, -1)):
            b = self.me + way * far
            fed = inside(self.me - way, self.size) & inside(b, self.size)

            @pl.when(fed)
            def _(w=w, b=b, way=way):
                ref = self.slot.at[w, b]
                remote(ref, ref, self.send.at[w, b], self.recv.at[w, b], {"ctx": self.me - way}).wait_recv()
                if far:
                    self.stage[w, b] = (self.own[b] + self.slot[w, b].astype(f32)).astype(bf16)
                    self.hop(w, b).start()

            if far:
                @pl.when(jnp.logical_not(inside(self.me - way, self.size)) & inside(b, self.size))
                def _(w=w, b=b):
                    self.stage[w, b] = self.own[b].astype(bf16)
                    self.hop(w, b).start()

    def result(self, ref):
        ref[...] = self.own[self.me]
        for w, way in enumerate((1, -1)):
            @pl.when(inside(self.me - way, self.size))
            def _(w=w):
                ref[...] = ref[...] + self.slot[w, self.me].astype(f32)

    def finish(self):
        for b in range(self.size):
            for w, way in enumerate((1, -1)):
                @pl.when((b - self.me) * way > 0)
                def _(w=w, b=b):
                    self.hop(w, b).wait_send()


def rest_kernel(
    head, br, gw, go, low_gate, gm, xs, ysum, tot, cin, segp, ids, taps, raw, hp, delta, run, runt, ent, grad_mgain,
    normed, tokens, invs, wg, wv, ws, wst, hid, cot, in_gain,
    out, gh, dg, dv, do, dst, dstate, smalls,
    low_value, low_state, low_step, small, gheads, state, dtot, gpad, gv, gs, gt, npart,
    sib_b, sib_n, sib_s, own_b, own_n, slot_b, slot_n, stage_b, stage_n,
    slot_g, slot_o, slot_v, slot_t, slot_m, slot_s, stage_s, all_s, acc,
    ps, pr, qs, qr, zs, zr, ds, dr, ss, sr, ms, mr, es, er,
):
    c, d, t = lax.axis_index("ctx"), lax.axis_index("dp"), lax.axis_index("tensor")
    nc, nd = lax.axis_size("ctx"), lax.axis_size("dp")
    length = ids.shape[2]
    half = br.shape[2]
    wide = slot_o.shape[2]
    sib = {"tensor": 1 - t}
    barrier = pltpu.get_barrier_semaphore()
    for k in range(1, nd):
        greet(barrier, {"dp": rot(d, k, nd)})
    greet(barrier, sib)
    greet_line(barrier)
    pl.semaphore_wait(barrier, nd + line_peers())
    sent = []

    def launch(copy):
        copy.start()
        sent.append(copy)

    def swap(a, k, src, dst):
        return remote(src.at[k, 1 - t], dst.at[k], ps.at[a, k], pr.at[a, k], sib)

    def scatter(a, src, slot):
        for k in range(1, nd):
            p = rot(d, k, nd)
            launch(remote(src(p), slot.at[d], ds.at[a, k - 1], dr.at[a, k - 1], {"dp": p}))

    def columns(ref):
        return lambda p: ref.at[:, spot(p, wide)]

    def collected(a, slot):
        for k in range(1, nd):
            r = rot(d, -k, nd)
            remote(slot.at[r], slot.at[r], ds.at[a, k - 1], dr.at[a, k - 1], {"dp": r}).wait_recv()
        return ranked(slot)

    def owned(a, src, other, own):
        for k in range(nc):
            swap(a, k, src, other).wait_recv()
            own[k] = src[k, t].astype(f32) + other[k].astype(f32)

    def place(a, ref, block):
        ref[c] = block.astype(bf16)
        line = Line(ref.at[c], lambda block: ref.at[block], zs.at[a], zr.at[a])
        line.start()
        return line

    for i in range((nc + 1) // 2):
        for k in sorted({i, nc - 1 - i}):
            launch(swap(0, k, br, sib_b))
    scatter(0, columns(gw), slot_g)
    scatter(1, columns(go), slot_o)
    slot_g[d] = gw[:, spot(d, wide)]
    slot_o[d] = go[:, spot(d, wide)]
    for ref in (state, gpad, small, gheads):
        ref[...] = jnp.zeros_like(ref)
    shed_b = Shed(own_b, slot_b, stage_b, qs.at[0], qr.at[0])
    shed_n = Shed(own_n, slot_n, stage_n, qs.at[1], qr.at[1])
    lines = []
    for i in range(nc):
        backward_chunk(
            nc - 1 - i, head, gm, xs, ysum, tot, cin, segp, ids, taps, raw, hp, delta, run, runt, ent,
            low_value, low_state, low_step, small, gheads, state, dtot, gpad,
        )
        if i == 0:
            owned(0, br, sib_b, own_b)
        shed_b.step(i)
        if i == nc // 2 - 1:
            lines.append(place(0, dg, collected(0, slot_g).T))
            lines.append(place(1, do, collected(1, slot_o)))
        if i > nc // 2 - 1:
            for item in lines:
                item.step(i - nc // 2)
    gs[...] = dot(low_state[...], normed[...], 0, 0).astype(bf16)
    side = wide // 2

    def cross(p):
        return remote(gs.at[:, spot(2 * p + 1 - t, side)], sib_s.at[p], ps.at[2, p], pr.at[2, p], sib)

    for p in range(nd):
        launch(cross(p))
    for k in range(nc):
        rows = slice(k * length, (k + 1) * length)
        part = dot(low_gate[rows, :], wg[...], 1, 1) + dot(low_value[rows, :], wv[...], 1, 1)
        part = part + dot(low_state[rows, :], ws[...], 1, 1) + dot(low_step[rows, :], wst[...])
        unit = tokens[rows, :].astype(f32) * invs[rows, :]
        gained = jnp.sum(part * unit, axis=0, keepdims=True)
        for m in range(gained.shape[1] // small.shape[1]):
            at = taps.shape[0] + 2 + m
            small[at : at + 1, :] = small[at : at + 1, :] + gained[:, m * small.shape[1] : (m + 1) * small.shape[1]]
        part = part.astype(bf16)
        npart[k, 0] = part[:half]
        npart[k, 1] = part[half:]
        launch(swap(1, k, npart, sib_n))
    gv[...] = dot(low_value[...], normed[...], 0, 0).astype(bf16)
    scatter(2, columns(gv), slot_v)
    gt[...] = dot(low_step[...], normed[...], 0, 0).astype(bf16)
    scatter(3, columns(gt), slot_t)
    small[taps.shape[0] + 1 : taps.shape[0] + 2, : gm.shape[1]] = grad_mgain[...]
    small[small.shape[0] - 8 :, : raw.shape[1]] = gheads[...]
    scatter(4, lambda p: small, slot_m)
    slot_v[d] = gv[:, spot(d, wide)]
    slot_t[d] = gt[:, spot(d, wide)]
    slot_m[d] = small[...]
    for s in range(nc - nc // 2, nc - 1):
        for item in lines:
            item.step(s)
    owned(1, npart, sib_n, own_n)
    shed_n.step(0)
    for p in range(nd):
        cross(p).wait_recv()
        stage_s[p] = (gs[:, spot(2 * p + t, side)].astype(f32) + sib_s[p].astype(f32)).astype(bf16)
    for k in range(1, nd):
        p = rot(d, k, nd)
        launch(remote(stage_s.at[p], slot_s.at[d], ss.at[k - 1], sr.at[k - 1], {"dp": p}))
    slot_s[d] = stage_s[d]
    late = [place(2, dv, collected(2, slot_v).T), place(3, dst, collected(3, slot_t))]
    smalls[c, t] = collected(4, slot_m)

    def onward(block, w, s):
        ref = smalls.at[block, t]
        return remote(ref, ref, ms.at[w, s], mr.at[w, s], sib)

    line_m = Line(smalls.at[c, t], lambda block: smalls.at[block, t], zs.at[4], zr.at[4], onward)
    line_m.start()
    ends = [(smalls.at[c, t], smalls.at[c, 1 - t], 3)]
    remote(smalls.at[c, t], smalls.at[c, t], es.at[3], er.at[3], sib).start()
    for k in range(1, nd):
        r = rot(d, -k, nd)
        remote(slot_s.at[r], slot_s.at[r], ss.at[k - 1], sr.at[k - 1], {"dp": r}).wait_recv()
    late.append(place(5, all_s, ranked(slot_s)))
    late.append(line_m)
    shed_n.step(1)

    def end(ref, e):
        ends.append((ref.at[t], ref.at[1 - t], e))
        remote(ref.at[t], ref.at[t], es.at[e], er.at[e], sib).start()

    rows = spot(t, half)
    base = hid[rows, :].astype(f32)
    shed_b.result(acc)
    out[t] = (base + acc[...]).astype(bf16)
    end(out, 1)
    for s in range(nc - 1):
        for item in late:
            item.step(s)
        if s + 2 < nc:
            shed_n.step(s + 2)
    dstate[t] = ranked(all_s).T
    end(dstate, 0)
    shed_n.result(acc)
    gn = acc[...]
    inv = lax.rsqrt(jnp.mean(base * base, axis=-1, keepdims=True) + epsilon)
    gsx = gn * in_gain[...]
    grad = inv * (gsx - base * (inv * inv) * jnp.mean(gsx * base, axis=-1, keepdims=True))
    gh[t] = cot[rows, :].astype(f32) + grad
    end(gh, 2)
    for item in lines + late + [shed_b, shed_n]:
        item.finish()
    line_m.arrived()
    for copy in sent:
        copy.wait_send()
    for mine, theirs, e in ends:
        remote(mine, mine, es.at[e], er.at[e], sib).wait_send()
        remote(theirs, theirs, es.at[e], er.at[e], sib).wait_recv()


def finish_kernel(
    heads, out_in, gh_in, dg, dv, do, dst, dstate, smalls,
    out, gh, g_in, g_gate, g_value, g_state, g_step, g_conv, g_offs, g_heads, g_gain, g_out,
):
    nc, nt = smalls.shape[0], smalls.shape[1]
    width = dg.shape[2]
    lags = g_conv.shape[0]
    inner = g_gain.shape[1]
    half = out_in.shape[1]
    side = dstate.shape[1]
    hpad = dst.shape[1]
    for m in range(2):
        out[m * half : (m + 1) * half, :] = out_in[m]
        gh[m * half : (m + 1) * half, :] = gh_in[m]
        g_state[m * side : (m + 1) * side, :] = dstate[m]
    shared, headed = None, jnp.zeros(g_heads.shape, f32)
    stepped = jnp.zeros(g_step.shape, f32)
    for k in range(nc):
        part = slice(k * width, (k + 1) * width)
        g_gate[:, part] = dg[k].astype(f32)
        g_value[:, part] = dv[k].astype(f32)
        g_out[part, :] = do[k].astype(f32)
        lane = lax.broadcasted_iota(jnp.int32, (hpad, g_step.shape[1]), 1)
        line = lax.broadcasted_iota(jnp.int32, (hpad, g_step.shape[1]), 0)
        pick = ((lane == line + k * heads) & (line < heads)).astype(f32)
        stepped = stepped + dot(dst[k].astype(f32), pick, 0, 0, precision=highest)
        for t in range(nt):
            mine = smalls[k, t]
            at = t * nc + k
            part = slice(at * width, (at + 1) * width)
            g_conv[:, part] = mine[:lags, :width]
            g_offs[:, part] = mine[lags : lags + 1, :width]
            g_gain[:, part] = mine[lags + 1 : lags + 2, :width]
            lane = lax.broadcasted_iota(jnp.int32, (hpad, g_heads.shape[1]), 1)
            line = lax.broadcasted_iota(jnp.int32, (hpad, g_heads.shape[1]), 0)
            pick = ((lane == line + at * heads) & (line < heads)).astype(f32)
            headed = headed + dot(mine[mine.shape[0] - 8 :, :hpad], pick, precision=highest)
            shared = mine if shared is None else shared + mine
    g_step[...] = stepped
    g_heads[...] = headed
    g_conv[:, inner:] = shared[:lags, width:]
    g_offs[:, inner:] = shared[lags : lags + 1, width:]
    wide = shared.shape[1]
    for m in range(g_in.shape[1] // wide):
        g_in[:, m * wide : (m + 1) * wide] = shared[lags + 2 + m : lags + 3 + m, :]


def sd(shape, kind):
    return jax.ShapeDtypeStruct(tuple(shape), kind)


def run_kernel(kernel, outs, args, scratch=(), name=None, ident=None):
    extra = {} if ident is None else dict(collective_id=ident, has_side_effects=True)
    return pl.pallas_call(
        kernel,
        out_shape=tuple(sd(s, k) for s, k in outs),
        in_specs=[VM] * len(args),
        out_specs=tuple([VM] * len(outs)),
        scratch_shapes=list(scratch),
        compiler_params=pltpu.CompilerParams(vmem_limit_bytes=LIMIT, **extra),
        name=name,
    )(*args)


def sems(*shape):
    return pltpu.SemaphoreType.DMA(shape)


def spread_body(
    hidden, segment_ids, cotangent, input_gain, gate_weight, value_weight, state_weight, step_weight,
    conv_weight, conv_bias, step_bias, decay_log, skip_gain, mixer_gain, out_weight,
):
    tokens, cot = hidden[0], cotangent[0]
    length, D = tokens.shape
    c, t = lax.axis_index("ctx"), lax.axis_index("tensor")
    nc, nd, nt = lax.axis_size("ctx"), lax.axis_size("dp"), lax.axis_size("tensor")
    width = gate_weight.shape[1] // nc
    inner = width * nc * nt
    heads_all = step_bias.shape[0]
    heads = heads_all // (nc * nt)
    hpad = 16 * ((heads + 15) // 16)
    head = width // heads
    states = state_weight.shape[1] // 2
    W = width + 2 * states
    T = length * nc
    rows = D // nd
    lags = conv_weight.shape[0]
    ids = jnp.broadcast_to(segment_ids.astype(f32), (8, length))
    stept = lax.dynamic_slice_in_dim(step_weight, c * heads, heads, 1).T
    stept = jnp.pad(stept, ((0, hpad - heads), (0, 0)))
    hp = jnp.stack([step_bias, -jnp.exp(decay_log), skip_gain] + [jnp.zeros_like(step_bias)] * 5)
    hp = lax.dynamic_slice_in_dim(hp, (t * nc + c) * heads, heads, 1)
    hp = jnp.pad(hp, ((0, 0), (0, hpad - heads)))
    gain_in = input_gain[None]

    H, CF, IDS, WG, WV, WS, WST, WO = run_kernel(
        collect_kernel,
        (
            ((nc, length, D), bf16), ((nc, length, D), bf16), ((nc, 8, length), f32),
            ((nd, rows, width), bf16), ((nd, rows, width), bf16), ((nd, rows, 2 * states), bf16),
            ((hpad, D), bf16), ((width, D), bf16),
        ),
        (tokens, cot, ids, gate_weight, value_weight, state_weight, stept, out_weight),
        (
            sems(3, 2, nc - 1), sems(3, 2, nc - 1), sems(2, 2, nc - 1), sems(2, 2, nc - 1),
            sems(5, nd - 1), sems(5, nd - 1),
        ),
        "collect",
        0,
    )
    H, CF = H.reshape(T, D), CF.reshape(T, D)
    WG, WV, WS = WG.reshape(D, width), WV.reshape(D, width), WS.reshape(D, 2 * states)
    srows = 8 * ((2 * nc + 7) // 8)
    (normed, gate, gg, cin, tot, xs, ysum, ent, delta, run, runt, raw, sums, segp, taps, offs, gain, invs) = run_kernel(
        partial(forward_kernel, head),
        (
            ((T, D), bf16), ((T, width), f32), ((T, width), f32), ((T + 8, W), f32), ((T, W), f32),
            ((T, width), bf16), ((T, width), f32), ((nc, width, states), bf16), ((T, hpad), f32),
            ((T, hpad), f32), ((nc, hpad, length), f32), ((T, hpad), f32), ((srows, length), f32),
            ((T + 8, 8), f32), ((lags, W), f32), ((1, W), f32), ((1, width), f32), ((T, 1), f32),
        ),
        (H, CF, IDS, WG, WV, WS, WST, WO, gain_in, conv_weight, conv_bias[None], mixer_gain[None], hp),
        (pltpu.VMEM((width, states), f32),),
        "forward",
    )
    total = nc * nt
    half = length // 2
    shalf = rows // 2
    low_gate, gm, grad_mgain, br, go, gw = run_kernel(
        partial(gate_kernel, head, inner),
        (
            ((T, width), bf16), ((T, width), bf16), ((1, width), f32), ((nc, 2, half, D), bf16),
            ((width, D), bf16), ((width, D), bf16),
        ),
        (sums, tot, ysum, gate, gg, gain, hp, CF, WO, normed),
        (
            pltpu.VMEM((T, width), bf16), pltpu.VMEM((total, srows, length), f32),
            sems(total - 1), sems(total - 1),
        ),
        "gating",
        1,
    )
    srow = 8 * ((lags + 2 + D // W + 7) // 8) + 8
    both = ((nc, half, D), bf16)

    def room(shape, kind):
        return pltpu.VMEM(shape, kind)

    out, gh, dg, dv, do, dst, dstate, smalls = run_kernel(
        partial(rest_kernel, head),
        (
            ((2, half, D), bf16), ((2, half, D), f32), ((nc, rows, width), bf16), ((nc, rows, width), bf16),
            ((nc, width, rows), bf16), ((nc, hpad, rows), bf16), ((2, shalf, 2 * states), f32),
            ((nc, nt, srow, W), f32),
        ),
        (
            br, gw, go, low_gate, gm, xs, ysum, tot, cin, segp, IDS, taps, raw, hp, delta, run, runt, ent, grad_mgain,
            normed, H, invs, WG, WV, WS, WST, tokens, cot, gain_in,
        ),
        (
            room((T, width), bf16), room((T, 2 * states), bf16), room((T, hpad), bf16), room((srow, W), f32),
            room((8, hpad), f32), room((width, states), f32), room((length, W), f32), room((T + 8, W), f32),
            room((width, D), bf16), room((2 * states, D), bf16), room((hpad, D), bf16), room((nc, 2, half, D), bf16),
            room(*both), room(*both), room((nd, 2 * states, shalf), bf16),
            room((nc, half, D), f32), room((nc, half, D), f32),
            room((2, nc, half, D), bf16), room((2, nc, half, D), bf16),
            room((2, nc, half, D), bf16), room((2, nc, half, D), bf16),
            room((nd, width, rows), bf16), room((nd, width, rows), bf16), room((nd, width, rows), bf16),
            room((nd, hpad, rows), bf16), room((nd, srow, W), f32), room((nd, 2 * states, shalf), bf16),
            room((nd, 2 * states, shalf), bf16), room((nc, 2 * states, shalf), bf16), room((half, D), f32),
            sems(3, max(nc, nd)), sems(3, max(nc, nd)), sems(2, 2, nc), sems(2, 2, nc),
            sems(6, 2, nc - 1), sems(6, 2, nc - 1), sems(5, nd - 1), sems(5, nd - 1),
            sems(nd - 1), sems(nd - 1), sems(2, nc - 1), sems(2, nc - 1), sems(4), sems(4),
        ),
        "rest",
        2,
    )
    outs = run_kernel(
        partial(finish_kernel, heads),
        (
            ((length, D), bf16), ((length, D), f32), ((1, D), f32), ((rows, nc * width), f32), ((rows, nc * width), f32),
            ((rows, 2 * states), f32), ((rows, nc * heads), f32), ((lags, inner + 2 * states), f32),
            ((1, inner + 2 * states), f32), ((8, heads_all), f32), ((1, inner), f32), ((nc * width, rows), f32),
        ),
        (out, gh, dg, dv, do, dst, dstate, smalls),
        (),
        "finish",
    )
    out, gh, g_in, g_gate, g_value, g_state, g_step, g_conv, g_offs, g_heads, g_gain, g_out = outs
    return (
        out[None], gh[None], g_in[0], g_gate, g_value, g_state, g_step, g_conv, g_offs[0],
        g_heads[0], g_heads[1], g_heads[2], g_gain[0], g_out,
    )


def fits(mesh, args):
    nc, nd, nt = mesh.shape["ctx"], mesh.shape["dp"], mesh.shape["tensor"]
    hidden, gate_weight, state_weight, step_bias = args[0], args[4], args[6], args[10]
    seqs, tokens, D = hidden.shape
    inner, heads = gate_weight.shape[1], step_bias.shape[0]
    groups = nc * nt
    if nt != 2 or seqs != nd or heads % (2 * groups) or inner % (128 * groups):
        return False
    length = tokens // nc
    states = state_weight.shape[1]
    if D % (256 * nd) or D % (inner // groups + states) or nc % 2:
        return False
    return tokens * (D + inner // groups) <= 2 << 20 and length % 128 == 0


def solution(mesh):
    in_specs = (
        P("dp", "ctx", None),
        P("dp", "ctx"),
        P("dp", "ctx", None),
        P(),
        P("dp", "tensor"),
        P("dp", "tensor"),
        P("dp", None),
        P("dp", "tensor"),
        P(),
        P(),
        P(),
        P(),
        P(),
        P(),
        P("tensor", "dp"),
    )
    out_specs = (
        P("dp", "ctx", None),
        P("dp", "ctx", None),
        P(),
        P("dp", "tensor"),
        P("dp", "tensor"),
        P("dp", None),
        P("dp", "tensor"),
        P(),
        P(),
        P(),
        P(),
        P(),
        P(),
        P("tensor", "dp"),
    )

    def whole(*args):
        chosen = spread_body if fits(mesh, args) else body
        return jax.shard_map(chosen, mesh=mesh, in_specs=in_specs, out_specs=out_specs, check_vma=False)(*args)

    return whole
```

```python
from functools import partial
from types import SimpleNamespace

import jax
import jax.numpy as jnp
from jax import lax
from jax.experimental import pallas as pl
from jax.experimental.pallas import tpu as pltpu
from jax.sharding import PartitionSpec as P

epsilon = 1e-05
highest = lax.Precision.HIGHEST
f32, bf16 = jnp.float32, jnp.bfloat16
MESH = pl.DeviceIdType.MESH
VM = pl.BlockSpec(memory_space=pltpu.VMEM)
ANY = pl.BlockSpec(memory_space=pl.ANY)
LIMIT = 56 * 1024 * 1024
FULL = 60 * 1024 * 1024
PARTS = 4


def dot(a, b, ca=1, cb=0, precision=None):
    return lax.dot_general(
        a, b, (((ca,), (cb,)), ((), ())), precision=precision, preferred_element_type=f32
    )


def shifted(array, axis, by):
    size = lax.axis_size(axis)
    pairs = [(i, i + by) for i in range(size) if 0 <= i + by < size]
    return lax.ppermute(array, axis, pairs)


def chain_kernel(axis, by, chunks, local_ref, fade_ref, out_ref, landed, outgoing, send, recv):
    size = lax.axis_size(axis)
    me = lax.axis_index(axis)
    follower = lax.rem(me + by + size, size)
    leader = lax.rem(me - by + size, size)
    first, last = (0, size - 1) if by > 0 else (size - 1, 0)
    rows = local_ref.shape[0] // chunks
    barrier = pltpu.get_barrier_semaphore()

    @pl.when(me != first)
    def _():
        pl.semaphore_signal(barrier, inc=1, device_id={axis: leader}, device_id_type=MESH)

    @pl.when(me != last)
    def _():
        pl.semaphore_wait(barrier, 1)

    def copy(c):
        part = pl.ds(c * rows, rows)
        return pltpu.make_async_remote_copy(
            src_ref=outgoing.at[part],
            dst_ref=landed.at[part],
            send_sem=send.at[c],
            recv_sem=recv.at[c],
            device_id={axis: follower},
            device_id_type=MESH,
        )

    @pl.when(me == first)
    def _():
        landed[...] = jnp.zeros_like(landed)

    for c in range(chunks):
        part = pl.ds(c * rows, rows)

        @pl.when(me != first)
        def _():
            copy(c).wait_recv()

        @pl.when(me != last)
        def _():
            total = fade_ref[part, :] * landed[part, :].astype(f32) + local_ref[part, :].astype(f32)
            outgoing[part, :] = total.astype(outgoing.dtype)
            copy(c).start()

    out_ref[...] = landed[...]

    @pl.when(me != last)
    def _():
        for c in range(chunks):
            copy(c).wait_send()


def chain(local, fade, axis, by, ident, chunks=4):
    return pl.pallas_call(
        partial(chain_kernel, axis, by, chunks),
        out_shape=jax.ShapeDtypeStruct(local.shape, local.dtype),
        in_specs=[VM, VM],
        out_specs=VM,
        scratch_shapes=[
            pltpu.VMEM(local.shape, local.dtype),
            pltpu.VMEM(local.shape, local.dtype),
            pltpu.SemaphoreType.DMA((chunks,)),
            pltpu.SemaphoreType.DMA((chunks,)),
        ],
        compiler_params=pltpu.CompilerParams(collective_id=ident, has_side_effects=True),
        name="chain",
    )(local, fade)


def pair_kernel(axis, src_ref, out_ref, slots, send, recv):
    size = lax.axis_size(axis)
    me = lax.axis_index(axis)
    barrier = pltpu.get_barrier_semaphore()
    for k in range(1, size):
        pl.semaphore_signal(
            barrier, inc=1, device_id={axis: lax.rem(me + k, size)}, device_id_type=MESH
        )
    pl.semaphore_wait(barrier, size - 1)
    copies = []
    for k in range(1, size):
        copies.append(
            pltpu.make_async_remote_copy(
                src_ref=src_ref,
                dst_ref=slots.at[k - 1],
                send_sem=send.at[k - 1],
                recv_sem=recv.at[k - 1],
                device_id={axis: lax.rem(me + k, size)},
                device_id_type=MESH,
            )
        )
        copies[-1].start()
    for copy in copies:
        copy.wait()
    total = src_ref[...].astype(f32)
    for k in range(1, size):
        total = total + slots[k - 1].astype(f32)
    out_ref[...] = total


def pair_sum(array, axis, ident):
    size = lax.axis_size(axis)
    return pl.pallas_call(
        partial(pair_kernel, axis),
        out_shape=jax.ShapeDtypeStruct(array.shape, f32),
        in_specs=[VM],
        out_specs=VM,
        scratch_shapes=[
            pltpu.VMEM((size - 1,) + array.shape, array.dtype),
            pltpu.SemaphoreType.DMA((size - 1,)),
            pltpu.SemaphoreType.DMA((size - 1,)),
        ],
        compiler_params=pltpu.CompilerParams(
            collective_id=ident, has_side_effects=True, vmem_limit_bytes=LIMIT
        ),
        name="pair_sum",
    )(array)


def gather_kernel(axis, count, *refs):
    ins, outs = refs[:count], refs[count : 2 * count]
    local, send, recv = refs[2 * count :]
    me = lax.axis_index(axis)
    low, high = lax.rem(me, 2), me // 2
    side = high * 2 + (1 - low)
    other = (1 - high) * 2 + low
    corner = (1 - high) * 2 + (1 - low)
    barrier = pltpu.get_barrier_semaphore()
    for peer in (side, other):
        pl.semaphore_signal(barrier, inc=1, device_id={axis: peer}, device_id_type=MESH)
    own = []
    for a in range(count):
        own.append(pltpu.make_async_copy(ins[a], outs[a].at[me], local.at[a]))
        own[-1].start()
    pl.semaphore_wait(barrier, 2)

    def remote(a, src, dst, slot, peer):
        return pltpu.make_async_remote_copy(
            src_ref=src,
            dst_ref=dst,
            send_sem=send.at[a, slot],
            recv_sem=recv.at[a, slot],
            device_id={axis: peer},
            device_id_type=MESH,
        )

    direct = []
    for a in range(count):
        for slot, peer in ((0, side), (1, other)):
            direct.append(remote(a, ins[a], outs[a].at[me], slot, peer))
            direct[-1].start()
    relays = []
    for a in range(count):
        half = ins[a].shape[0] // 2
        lower, upper = pl.ds(0, half), pl.ds(half, half)
        remote(a, ins[a], outs[a].at[side], 0, side).wait_recv()
        relay = remote(a, outs[a].at[side, lower], outs[a].at[side, lower], 2, other)
        relay.start()
        relays.append(relay)
        remote(a, ins[a], outs[a].at[other], 1, other).wait_recv()
        relay = remote(a, outs[a].at[other, upper], outs[a].at[other, upper], 3, side)
        relay.start()
        relays.append(relay)
    for a in range(count):
        half = ins[a].shape[0] // 2
        lower, upper = pl.ds(0, half), pl.ds(half, half)
        remote(a, outs[a].at[corner, lower], outs[a].at[corner, lower], 2, other).wait_recv()
        remote(a, outs[a].at[corner, upper], outs[a].at[corner, upper], 3, side).wait_recv()
    for copy in direct + relays:
        copy.wait_send()
    for copy in own:
        copy.wait()


def gather(arrays, axis, ident):
    size = lax.axis_size(axis)
    if size != 4:
        return tuple(lax.all_gather(a, axis) for a in arrays)
    count = len(arrays)
    return pl.pallas_call(
        partial(gather_kernel, axis, count),
        out_shape=tuple(jax.ShapeDtypeStruct((size,) + a.shape, a.dtype) for a in arrays),
        in_specs=[VM] * count,
        out_specs=tuple([VM] * count),
        scratch_shapes=[
            pltpu.SemaphoreType.DMA((count,)),
            pltpu.SemaphoreType.DMA((count, 4)),
            pltpu.SemaphoreType.DMA((count, 4)),
        ],
        compiler_params=pltpu.CompilerParams(
            collective_id=ident, has_side_effects=True, vmem_limit_bytes=LIMIT
        ),
        name="gather",
    )(*arrays)


def sigmoid(v):
    return 1.0 / (1.0 + jnp.exp(-v))


def silu(v):
    return v / (1.0 + jnp.exp(-v))


def dsilu(v):
    s = sigmoid(v)
    return s * (1.0 + v * (1.0 - s))


def softplus(v):
    return jnp.maximum(v, 0.0) + jnp.log1p(jnp.exp(-jnp.abs(v)))


def spread_pair(first_lanes, table, pair):
    return jnp.where(first_lanes, table[:, 2 * pair : 2 * pair + 1], table[:, 2 * pair + 1 : 2 * pair + 2])


def lanes_first(length, head):
    return lax.broadcasted_iota(jnp.int32, (length, 2 * head), 1) < head


def negative_mask(segc, segr):
    length = segc.shape[0]
    row = lax.broadcasted_iota(jnp.int32, (length, length), 0)
    col = lax.broadcasted_iota(jnp.int32, (length, length), 1)
    return jnp.where((segc == segr) & (row >= col), 0.0, -1e30).astype(f32)


def tails(run, segc):
    length = segc.shape[0]
    return jnp.exp(run[length - 1 : length, :] - run) * (segc == segc[length - 1 : length]).astype(f32)


def local_kernel(
    width, head, cin, same, taps, offs, raw, bias, rate, segc, segr,
    tot, intra, xs, final, delta_out, run_out, runt_out, wide,
):
    length = segc.shape[0]
    total_width = cin.shape[1]
    states = (total_width - width) // 2
    wide[...] = cin[...].astype(f32)
    lags = taps.shape[0]
    pad = cin.shape[0] - length
    for c in range(total_width // 128):
        part = slice(c * 128, c * 128 + 128)
        acc = jnp.broadcast_to(offs[:, part], (length, 128))
        for j in range(lags):
            acc = acc + taps[j : j + 1, part] * (wide[pad - j : pad - j + length, part] * same[:, j : j + 1])
        tot[:, part] = acc
    delta = softplus(raw[...] + bias[...])
    delta_out[...] = delta
    row = lax.broadcasted_iota(jnp.int32, (length, length), 0)
    col = lax.broadcasted_iota(jnp.int32, (length, length), 1)
    below = (row >= col).astype(f32)
    decay = delta * rate[...]
    run = dot(below, decay, precision=highest)
    run_out[...] = run
    runt = run.T
    runt_out[...] = runt
    b = silu(tot[:, width : width + states]).astype(bf16)
    c = silu(tot[:, width + states :]).astype(bf16)
    scores = dot(c, b, 1, 1)
    negative = negative_mask(segc[...], segr[...])
    first = lanes_first(length, head)
    tail = tails(run, segc[...])
    for pair in range(width // (2 * head)):
        part = slice(pair * 2 * head, (pair + 1) * 2 * head)
        x = (silu(tot[:, part]) * spread_pair(first, delta, pair)).astype(bf16)
        xs[:, part] = x
        x32 = x.astype(f32)
        faded = (x32 * spread_pair(first, tail, pair)).astype(bf16)
        final[part, :] = dot(faded, b, 0, 0).astype(bf16)
        total = None
        for k in range(2):
            h = 2 * pair + k
            w = (jnp.exp(run[:, h : h + 1] - runt[h : h + 1, :] + negative) * scores).astype(bf16)
            xk = jnp.where(first if k == 0 else ~first, x32, 0.0).astype(bf16)
            term = dot(w, xk)
            total = term if total is None else total + term
        intra[:, part] = total


def entries(run, segc, before):
    return jnp.exp(run) * (segc == before).astype(f32)


def product_kernel(
    width, head, inner, ctot_ref, tot, intra, entering, run, segc, before, gate, gg, gain, skip, ysum, sums,
):
    length = segc.shape[0]
    first = lanes_first(length, head)
    c = silu(ctot_ref[...]).astype(bf16)
    entry = entries(run[...], segc[...], before[...])
    squares = jnp.zeros((length, 1), f32)
    project = jnp.zeros((length, 1), f32)
    for pair in range(width // (2 * head)):
        part = slice(pair * 2 * head, (pair + 1) * 2 * head)
        y = intra[:, part] + dot(c, entering[part, :], 1, 1) * spread_pair(first, entry, pair)
        ysum[:, part] = y
        mixed = y + spread_pair(first[:1], skip[...], pair) * silu(tot[:, part])
        product = mixed * silu(gate[:, part])
        squares = squares + jnp.sum(product * product, axis=1, keepdims=True)
        project = project + jnp.sum(gg[:, part] * gain[:, part] * product, axis=1, keepdims=True)
    lane = lax.broadcasted_iota(jnp.int32, sums.shape, 1)
    sums[...] = jnp.where(lane == 0, squares, jnp.where(lane == 1, project, 0.0))


def norm_kernel(
    width, head, inner, ctot_ref, tot, ysum, run, segc, before, gate, gg, gain, skip, sums,
    gated, low_gate, gm, grad_entering, grad_gain,
):
    length = segc.shape[0]
    first = lanes_first(length, head)
    c = silu(ctot_ref[...]).astype(bf16)
    entry = entries(run[...], segc[...], before[...])
    scale = lax.rsqrt(sums[:, 0:1] / inner + epsilon)
    project = scale * sums[:, 1:2] / inner
    for pair in range(width // (2 * head)):
        part = slice(pair * 2 * head, (pair + 1) * 2 * head)
        mixed = ysum[:, part] + spread_pair(first[:1], skip[...], pair) * silu(tot[:, part])
        z = gate[:, part]
        sg = sigmoid(z)
        act = z * sg
        unit = mixed * act * scale
        gated[:, part] = (unit * gain[:, part]).astype(bf16)
        g = gg[:, part]
        grad_gain[:, part] = jnp.sum(g * unit, axis=0, keepdims=True)
        gp = scale * (g * gain[:, part] - unit * project)
        gmix = gp * act
        low_gate[:, part] = (gp * mixed * sg * (1.0 + z * (1.0 - sg))).astype(bf16)
        gmb = gmix.astype(bf16)
        gm[:, part] = gmb
        scaled = (gmb.astype(f32) * spread_pair(first, entry, pair)).astype(bf16)
        grad_entering[part, :] = dot(scaled, c, 0, 0).astype(bf16)


def back_kernel(
    width, head, gm, xs, ysum, tot, cin, same, taps, raw, bias, rate, skip, delta_in, run_in, runt_in,
    segc, segr, before, entering, leaving,
    gpad, gtaps, goffs, graw, gheads, dtot, wide,
):
    length = segc.shape[0]
    heads = width // head
    total_width = tot.shape[1]
    states = (total_width - width) // 2
    first = lanes_first(length, head)
    run, runt, delta = run_in[...], runt_in[...], delta_in[...]
    negative = negative_mask(segc[...], segr[...])
    b = silu(tot[:, width : width + states]).astype(bf16)
    c = silu(tot[:, width + states :]).astype(bf16)
    scores = dot(c, b, 1, 1)
    tail = tails(run, segc[...])
    entry = entries(run, segc[...], before[...])
    dscores = jnp.zeros((length, length), f32)
    u = jnp.zeros((length, heads), f32)
    q = jnp.zeros((1, heads), f32)
    vdx = jnp.zeros((length, heads), f32)
    gv = jnp.zeros((1, heads), f32)
    ge = jnp.zeros((1, heads), f32)
    db = jnp.zeros((length, states), f32)
    dc = jnp.zeros((length, states), f32)
    chan = lax.broadcasted_iota(jnp.int32, (2 * head, heads), 0)
    which = lax.broadcasted_iota(jnp.int32, (2 * head, heads), 1)
    for pair in range(heads // 2):
        part = slice(pair * 2 * head, (pair + 1) * 2 * head)
        pick = (which == 2 * pair + (chan >= head).astype(jnp.int32)).astype(f32)
        x = xs[:, part]
        x32 = x.astype(f32)
        g = gm[:, part]
        g32 = g.astype(f32)
        tl = spread_pair(first, tail, pair)
        grad_f = leaving[part, :]
        late = dot(b, grad_f, 1, 1) * tl
        dx = late
        for k in range(2):
            h = 2 * pair + k
            lanes = first if k == 0 else ~first
            gk = jnp.where(lanes, g32, 0.0).astype(bf16)
            decay = jnp.exp(run[:, h : h + 1] - runt[h : h + 1, :] + negative)
            w = (decay * scores).astype(bf16)
            dscores = dscores + decay * dot(gk, x, 1, 1)
            dx = dx + dot(w, gk, 0, 0)
        raw_v = tot[:, part]
        sg = sigmoid(raw_v)
        v = raw_v * sg
        u = u + dot(g32 * ysum[:, part] - x32 * dx, pick, precision=highest)
        q = q + jnp.sum(dot(x32 * late, pick, precision=highest), axis=0, keepdims=True)
        vdx = vdx + dot(v * dx, pick, precision=highest)
        gv = gv + dot(jnp.sum(g32 * v, axis=0, keepdims=True), pick, precision=highest)
        per_row = jnp.sum(grad_f.astype(f32) * entering[part, :].astype(f32), axis=1, keepdims=True)
        ge = ge + jnp.sum(per_row * pick, axis=0, keepdims=True)
        dv = spread_pair(first, delta, pair) * dx + spread_pair(first[:1], skip[...], pair) * g32
        dtot[:, part] = dv * (sg * (1.0 + raw_v * (1.0 - sg)))
        db = db + dot((x32 * tl).astype(bf16), grad_f)
        dc = dc + dot((g32 * spread_pair(first, entry, pair)).astype(bf16), entering[part, :])
    dsb = dscores.astype(bf16)
    dc = dc + dot(dsb, b)
    db = db + dot(dsb, c, 0, 0)
    dtot[:, width : width + states] = db * dsilu(tot[:, width : width + states])
    dtot[:, width + states :] = dc * dsilu(tot[:, width + states :])
    row = lax.broadcasted_iota(jnp.int32, (length, length), 0)
    col = lax.broadcasted_iota(jnp.int32, (length, length), 1)
    above = (row <= col).astype(f32)
    last = slice(length - 1, length)
    dld = dot(above, u, precision=highest) + (q + entry[last, :] * ge)
    ddelta = dld * rate[...] + vdx
    gr = ddelta * sigmoid(raw[...] + bias[...])
    graw[...] = gr
    gheads[...] = jnp.zeros_like(gheads)
    gheads[0:1, :] = jnp.sum(gr, axis=0, keepdims=True)
    gheads[1:2, :] = jnp.sum(dld * delta, axis=0, keepdims=True) * rate[...]
    gheads[2:3, :] = gv
    wide[...] = cin[...].astype(f32)
    gpad[...] = jnp.zeros_like(gpad)
    lags = taps.shape[0]
    pad = cin.shape[0] - length
    for n in range(total_width // 128):
        part = slice(n * 128, n * 128 + 128)
        d = dtot[:, part]
        goffs[:, part] = jnp.sum(d, axis=0, keepdims=True)
        for j in range(lags):
            ds = d * same[:, j : j + 1]
            window = slice(pad - j, pad - j + length)
            gtaps[j : j + 1, part] = jnp.sum(ds * wide[window, part], axis=0, keepdims=True)
            gpad[window, part] = gpad[window, part] + ds * taps[j : j + 1, part]


def call(kernel, outs, args, scratch=(), name=None):
    return pl.pallas_call(
        kernel,
        out_shape=tuple(jax.ShapeDtypeStruct(s, d) for s, d in outs),
        in_specs=[VM] * len(args),
        out_specs=tuple([VM] * len(outs)),
        scratch_shapes=list(scratch),
        compiler_params=pltpu.CompilerParams(vmem_limit_bytes=LIMIT),
        name=name,
    )(*args)


def body(
    hidden,
    segment_ids,
    cotangent,
    input_gain,
    gate_weight,
    value_weight,
    state_weight,
    step_weight,
    conv_weight,
    conv_bias,
    step_bias,
    decay_log,
    skip_gain,
    mixer_gain,
    out_weight,
):
    tokens = hidden[0]
    wrapped = segment_ids[0] % 128
    cot = cotangent[0]
    length, width_in = tokens.shape
    shard = lax.axis_index("tensor")
    shards = lax.axis_size("tensor")
    lags = conv_weight.shape[0]
    reach = lags - 1
    dp = lax.axis_size("dp")
    width = gate_weight.shape[1]
    local_heads = step_weight.shape[1]
    head = width // local_heads
    inner = width * shards
    states = state_weight.shape[1] // 2
    ids_col = jnp.broadcast_to(wrapped[length - reach :].astype(bf16)[:, None], (reach, 128))
    edge = shifted(jnp.concatenate([tokens[length - reach :], ids_col], 1), "ctx", 1)
    narrow = jnp.concatenate(
        [state_weight, step_weight, jnp.zeros((state_weight.shape[0], 128 - local_heads), bf16)], 1
    )
    g_gate, g_value, g_narrow, g_out = gather(
        (gate_weight, value_weight, narrow, out_weight), "dp", 0
    )
    full_gate = g_gate.reshape(width_in, width)
    full_value = g_value.reshape(width_in, width)
    full_narrow = g_narrow.reshape(width_in, narrow.shape[1])
    full_out = jnp.concatenate([g_out[k] for k in range(dp)], 1)
    pad = 8
    base_ext = jnp.concatenate(
        [jnp.zeros((pad - reach, width_in), bf16), edge[:, :width_in], tokens], 0
    ).astype(f32)
    inv_ext = lax.rsqrt(jnp.mean(base_ext * base_ext, axis=-1, keepdims=True) + epsilon)
    normed_ext = (base_ext * inv_ext * input_gain).astype(bf16)
    normed = normed_ext[pad:]
    base = tokens.astype(f32)
    inv = inv_ext[pad:]
    gate = jnp.dot(normed, full_gate, preferred_element_type=f32)
    value_pre = jnp.dot(normed_ext, full_value, preferred_element_type=f32)
    rest_pre = jnp.dot(normed_ext, full_narrow, preferred_element_type=f32)
    cin = jnp.concatenate([value_pre.astype(bf16), rest_pre[:, : 2 * states].astype(bf16)], 1)
    raw_step = rest_pre[pad:, 2 * states : 2 * states + local_heads]
    grad_gated = jnp.dot(cot, full_out.T, preferred_element_type=f32)

    padded_ids = jnp.concatenate([edge[:, width_in].astype(jnp.int32), wrapped])
    before = padded_ids[reach - 1].astype(f32).reshape(1, 1)
    same = jnp.stack(
        [
            (padded_ids[reach - j : reach - j + length] == wrapped).astype(f32)
            for j in range(lags)
        ],
        1,
    )
    segc = wrapped.astype(f32)[:, None]
    segr = wrapped.astype(f32)[None, :]

    def local(array, size):
        return lax.dynamic_slice_in_dim(array, shard * size, size, array.ndim - 1)

    taps = jnp.concatenate([local(conv_weight, width), conv_weight[:, inner:]], 1)
    offs = jnp.concatenate([local(conv_bias, width), conv_bias[inner:]], 0)[None]
    bias = local(step_bias, local_heads)[None]
    rate = -jnp.exp(local(decay_log, local_heads))[None]
    skip = local(skip_gain, local_heads)[None]
    gain = local(mixer_gain, width)[None]
    total_width = width + 2 * states

    tot, intra, xs, final, delta, run, runt = call(
        partial(local_kernel, width, head),
        (
            ((length, total_width), f32),
            ((length, width), f32),
            ((length, width), bf16),
            ((width, states), bf16),
            ((length, local_heads), f32),
            ((length, local_heads), f32),
            ((local_heads, length), f32),
        ),
        (cin, same, taps, offs, raw_step, bias, rate, segc, segr),
        (pltpu.VMEM((length + pad, total_width), f32),),
        "mixer_local",
    )
    through = jnp.exp(run[length - 1]) * (segc[length - 1] == before[0]).astype(f32)
    fade = jnp.broadcast_to(jnp.repeat(through, head)[:, None], (width, 128))
    entering = chain(final, fade, "ctx", 1, 1)
    ctot = tot[:, width + states :]
    ysum, sums = call(
        partial(product_kernel, width, head, inner),
        (((length, width), f32), ((length, 128), f32)),
        (ctot, tot, intra, entering, run, segc, before, gate, grad_gated, gain, skip),
        (),
        "mixer_product",
    )
    sums = pair_sum(sums, "tensor", 2)
    gated, low_gate, gm, grad_entering, grad_mgain = call(
        partial(norm_kernel, width, head, inner),
        (
            ((length, width), bf16),
            ((length, width), bf16),
            ((length, width), bf16),
            ((width, states), bf16),
            ((1, width), f32),
        ),
        (ctot, tot, ysum, run, segc, before, gate, grad_gated, gain, skip, sums),
        (),
        "mixer_norm",
    )
    grad_out = jnp.dot(gated.T, cot, preferred_element_type=f32).astype(bf16)
    grad_gate_w = jnp.dot(normed.T, low_gate, preferred_element_type=f32).astype(bf16)
    out_piece = lax.psum_scatter(grad_out, "dp", scatter_dimension=1, tiled=True)
    gate_piece = lax.psum_scatter(grad_gate_w, "dp", scatter_dimension=0, tiled=True)
    leaving = chain(grad_entering, fade, "ctx", -1, 3)
    gpad, gtaps, goffs, graw, gheads = call(
        partial(back_kernel, width, head),
        (
            ((length + pad, total_width), f32),
            ((lags, total_width), f32),
            ((1, total_width), f32),
            ((length, local_heads), f32),
            ((8, local_heads), f32),
        ),
        (
            gm, xs, ysum, tot, cin, same, taps, raw_step, bias, rate, skip, delta, run, runt,
            segc, segr, before, entering, leaving,
        ),
        (pltpu.VMEM((length, total_width), f32), pltpu.VMEM((length + pad, total_width), f32)),
        "mixer_back",
    )
    edge_grad = shifted(gpad[pad - reach : pad], "ctx", -1)
    grad_input = jnp.concatenate(
        [gpad[pad : pad + length - 8], gpad[pad + length - 8 :] + jnp.pad(edge_grad, ((8 - reach, 0), (0, 0)))], 0
    )
    low_value = grad_input[:, :width].astype(bf16)
    low_rest = jnp.concatenate(
        [
            grad_input[:, width:].astype(bf16),
            graw.astype(bf16),
            jnp.zeros((length, 128 - local_heads), bf16),
        ],
        1,
    )
    low_tail = jnp.concatenate([low_value, low_rest], 1)
    grad_tail_w = jnp.dot(normed.T, low_tail, preferred_element_type=f32).astype(bf16)
    tail_piece = lax.psum_scatter(grad_tail_w, "dp", scatter_dimension=0, tiled=True)
    branch_out = jnp.dot(gated, full_out, preferred_element_type=f32).astype(bf16)
    normed_part = (
        jnp.dot(low_gate, full_gate.T, preferred_element_type=f32)
        + jnp.dot(low_value, full_value.T, preferred_element_type=f32)
        + jnp.dot(low_rest, full_narrow.T, preferred_element_type=f32)
    ).astype(bf16)
    both = pair_sum(jnp.concatenate([branch_out, normed_part], 0), "tensor", 4)
    result = (base + both[:length]).astype(bf16)
    gn = both[length:]
    grad_gain = jnp.sum(gn * base * inv, axis=0)
    gs = gn * input_gain
    grad_base = inv * (gs - base * (inv * inv) * jnp.mean(gs * base, axis=-1, keepdims=True))
    grad_tokens = cot.astype(f32) + grad_base

    out_sum = lax.psum(out_piece, "ctx").astype(f32)
    gate_sum = lax.psum(gate_piece, "ctx").astype(f32)
    tail_sum = lax.psum(tail_piece, "ctx")
    state_sum = pair_sum(tail_sum[:, width : width + 2 * states], "tensor", 5)

    mine = (shard == 0).astype(f32)

    def placed(array, size):
        spots = [jnp.where(shard == k, array, 0.0) for k in range(shards)]
        return jnp.concatenate(spots, -1)

    small = jnp.concatenate(
        [
            (grad_gain * mine)[None],
            jnp.concatenate([placed(gtaps[:, :width], width), gtaps[:, width:]], 1).reshape(1, -1),
            jnp.concatenate([placed(goffs[:, :width], width), goffs[:, width:]], 1),
            placed(grad_mgain, width),
            placed(gheads[0:1], local_heads),
            placed(gheads[1:2], local_heads),
            placed(gheads[2:3], local_heads),
        ],
        1,
    )
    sizes = [width_in, lags * (inner + 2 * states), inner + 2 * states, inner]
    sizes = sizes + [local_heads * shards] * 3
    totals = lax.psum(small, ("dp", "ctx", "tensor"))[0]
    parts, at = [], 0
    for size in sizes:
        parts.append(totals[at : at + size])
        at += size
    return (
        result[None],
        grad_tokens[None],
        parts[0],
        gate_sum,
        tail_sum[:, :width].astype(f32),
        state_sum,
        tail_sum[:, width + 2 * states : width + 2 * states + local_heads].astype(f32),
        parts[1].reshape(lags, inner + 2 * states),
        parts[2],
        parts[4],
        parts[5],
        parts[6],
        parts[3],
        out_sum,
    )


def rot(me, k, size):
    return lax.rem(me + k + size, size)


def remote(src, dst, send, recv, device):
    return pltpu.make_async_remote_copy(
        src_ref=src, dst_ref=dst, send_sem=send, recv_sem=recv, device_id=device, device_id_type=MESH
    )


def greet(barrier, device):
    pl.semaphore_signal(barrier, inc=1, device_id=device, device_id_type=MESH)


def spot(index, size):
    return pl.ds(pl.multiple_of(index * size, size), size)


def inside(index, size):
    return (index >= 0) & (index < size)


class Line:
    def __init__(self, own, at, send, recv, onward=None):
        self.own, self.at, self.send, self.recv, self.onward = own, at, send, recv, onward
        self.me, self.size = lax.axis_index("ctx"), lax.axis_size("ctx")

    def hop(self, w, s):
        way = (1, -1)[w]
        block = self.me - way * s
        src = self.own if s == 0 else self.at(block)
        return remote(src, self.at(block), self.send.at[w, s], self.recv.at[w, s], {"ctx": self.me + way})

    def start(self):
        for w, way in enumerate((1, -1)):
            @pl.when(inside(self.me + way, self.size))
            def _(w=w):
                self.hop(w, 0).start()

    def step(self, s):
        for w, way in enumerate((1, -1)):
            block = self.me - way * (s + 1)

            @pl.when(inside(block, self.size))
            def _(w=w, way=way, block=block):
                ref = self.at(block)
                remote(ref, ref, self.send.at[w, s], self.recv.at[w, s], {"ctx": self.me - way}).wait_recv()
                if s + 1 < self.size - 1:
                    @pl.when(inside(self.me + way, self.size))
                    def _():
                        self.hop(w, s + 1).start()
                if self.onward is not None:
                    self.onward(block, w, s).start()

    def finish(self):
        for s in range(self.size - 1):
            for w, way in enumerate((1, -1)):
                @pl.when(inside(self.me + way, self.size) & inside(self.me - way * s, self.size))
                def _(w=w, s=s):
                    self.hop(w, s).wait_send()

    def arrived(self):
        for s in range(self.size - 1):
            for w, way in enumerate((1, -1)):
                block = self.me - way * (s + 1)

                @pl.when(inside(block, self.size))
                def _(w=w, s=s, block=block):
                    self.onward(block, w, s).wait()


def greet_line(barrier):
    c, nc = lax.axis_index("ctx"), lax.axis_size("ctx")
    for way in (1, -1):
        @pl.when(inside(c + way, nc))
        def _(way=way):
            greet(barrier, {"ctx": c + way})


class Cast:
    def __init__(self, ref, send, recv):
        self.ref, self.send, self.recv = ref, send, recv
        self.me, self.size = lax.axis_index("ctx"), lax.axis_size("ctx")

    def copy(self, block, k):
        ref = self.ref(block)
        return remote(ref, ref, self.send.at[k - 1], self.recv.at[k - 1], {"ctx": rot(self.me, k, self.size)})

    def start(self):
        for k in range(1, self.size):
            self.copy(self.me, k).start()

    def arrived(self):
        for k in range(1, self.size):
            self.copy(rot(self.me, -k, self.size), k).wait_recv()

    def finish(self):
        for k in range(1, self.size):
            self.copy(self.me, k).wait_send()


class Several:
    def __init__(self, items):
        self.items = items

    def start(self):
        for item in self.items:
            item.start()

    def step(self, i):
        for item in self.items:
            item.step(i)

    def finish(self):
        for item in self.items:
            item.finish()

    def arrived(self):
        for item in self.items:
            item.arrived()


def line_peers():
    c, nc = lax.axis_index("ctx"), lax.axis_size("ctx")
    return (c > 0).astype(jnp.int32) + (c < nc - 1).astype(jnp.int32)


def chunk_masks(segp, at, length, lags):
    segc = segp[at : at + length, 0:1]
    return segc, [(segp[at - j : at - j + length, 0:1] == segc).astype(f32) for j in range(lags)]


def fades(through, pair, head, rows):
    low = lax.broadcasted_iota(jnp.int32, (rows, 1), 0) < head
    return jnp.where(low, through[:, 2 * pair : 2 * pair + 1], through[:, 2 * pair + 1 : 2 * pair + 2])


def scan_chunk(
    k, head, hid, ids, wv, ws, wst, in_gain, hp,
    normed, cin, tot, xs, ysum, ent, delta, run, runt, raw, segp, taps, offs, invs, state,
):
    length = ids.shape[2]
    width = wv.shape[1]
    states = ws.shape[1] // 2
    lags = taps.shape[0]
    pad = 8
    row = lax.broadcasted_iota(jnp.int32, (length, length), 0)
    col = lax.broadcasted_iota(jnp.int32, (length, length), 1)
    below = (row >= col).astype(f32)
    first = lanes_first(length, head)
    bias, rate = hp[0:1, :], hp[1:2, :]
    rows = slice(k * length, (k + 1) * length)
    at = pad + k * length
    base = hid[k].astype(f32)
    inv = lax.rsqrt(jnp.mean(base * base, axis=-1, keepdims=True) + epsilon)
    invs[rows, :] = inv
    nb = (base * inv * in_gain[...]).astype(bf16)
    normed[rows, :] = nb
    cin[at : at + length, :width] = dot(nb, wv[...]).astype(bf16).astype(f32)
    cin[at : at + length, width:] = dot(nb, ws[...]).astype(bf16).astype(f32)
    rawk = dot(nb, wst[...], 1, 1)
    raw[rows, :] = rawk
    segc, same = chunk_masks(segp, at, length, lags)
    segr = ids[k, 0:1, :]
    before = segp[at - 1 : at, 0:1]
    for n in range(cin.shape[1] // 128):
        part = slice(n * 128, n * 128 + 128)
        acc = jnp.broadcast_to(offs[:, part], (length, 128))
        for j in range(lags):
            acc = acc + taps[j : j + 1, part] * (cin[at - j : at - j + length, part] * same[j])
        tot[rows, part] = acc
    dk = softplus(rawk + bias)
    delta[rows, :] = dk
    rk = dot(below, dk * rate, precision=highest)
    run[rows, :] = rk
    rkt = rk.T
    runt[k] = rkt
    b = silu(tot[rows, width : width + states]).astype(bf16)
    cc = silu(tot[rows, width + states :]).astype(bf16)
    scores = dot(cc, b, 1, 1)
    negative = negative_mask(segc, segr)
    tail = tails(rk, segc)
    entry = entries(rk, segc, before)
    through = entry[length - 1 : length, :]
    for pair in range(width // (2 * head)):
        part = slice(pair * 2 * head, (pair + 1) * 2 * head)
        values = silu(tot[rows, part])
        x = (values * spread_pair(first, dk, pair)).astype(bf16)
        xs[rows, part] = x
        x32 = x.astype(f32)
        faded = (x32 * spread_pair(first, tail, pair)).astype(bf16)
        old = state[part, :]
        entering = old.astype(bf16)
        ent[k, part, :] = entering
        state[part, :] = fades(through, pair, head, 2 * head) * old + dot(faded, b, 0, 0)
        y = dot(cc, entering, 1, 1) * spread_pair(first, entry, pair)
        for m in range(2):
            h = 2 * pair + m
            w = (jnp.exp(rk[:, h : h + 1] - rkt[h : h + 1, :] + negative) * scores).astype(bf16)
            xk = jnp.where(first if m == 0 else ~first, x32, 0.0).astype(bf16)
            y = y + dot(w, xk)
        ysum[rows, part] = y


def product_chunk(k, head, length, cf, wo, normed, wg, hp, gain, tot, ysum, gate, gg, sums):
    first = lanes_first(length, head)
    skip = hp[2:3, :]
    rows = slice(k * length, (k + 1) * length)
    gate[rows, :] = dot(normed[rows, :], wg[...])
    gg[rows, :] = dot(cf[k], wo[...], 1, 1)
    squares = jnp.zeros((length, 1), f32)
    project = jnp.zeros((length, 1), f32)
    for pair in range(gate.shape[1] // (2 * head)):
        part = slice(pair * 2 * head, (pair + 1) * 2 * head)
        mixed = ysum[rows, part] + spread_pair(first[:1], skip, pair) * silu(tot[rows, part])
        product = mixed * silu(gate[rows, part])
        squares = squares + jnp.sum(product * product, axis=1, keepdims=True)
        project = project + jnp.sum(gg[rows, part] * gain[:, part] * product, axis=1, keepdims=True)
    lane = lax.broadcasted_iota(jnp.int32, (length, 128), 1)
    both = jnp.where(lane == 0, squares, jnp.where(lane == 1, project, 0.0))
    sums[2 * k : 2 * k + 2, :] = both.T[0:2, :]


def gate_chunk(k, head, inner, length, added, hp, gain, tot, ysum, gate, gg, wo, gated, low_gate, gm, mgain, br):
    first = lanes_first(length, head)
    skip = hp[2:3, :]
    rows = slice(k * length, (k + 1) * length)
    scale = lax.rsqrt(added[:, 2 * k : 2 * k + 1] / inner + epsilon)
    project = scale * added[:, 2 * k + 1 : 2 * k + 2] / inner
    for pair in range(gate.shape[1] // (2 * head)):
        part = slice(pair * 2 * head, (pair + 1) * 2 * head)
        mixed = ysum[rows, part] + spread_pair(first[:1], skip, pair) * silu(tot[rows, part])
        z = gate[rows, part]
        sg = sigmoid(z)
        act = z * sg
        unit = mixed * act * scale
        gated[rows, part] = (unit * gain[:, part]).astype(bf16)
        g = gg[rows, part]
        mgain[:, part] = mgain[:, part] + jnp.sum(g * unit, axis=0, keepdims=True)
        gp = scale * (g * gain[:, part] - unit * project)
        low_gate[rows, part] = (gp * mixed * sg * (1.0 + z * (1.0 - sg))).astype(bf16)
        gm[rows, part] = (gp * act).astype(bf16)
    branch = dot(gated[rows, :], wo[...]).astype(bf16)
    half = length // 2
    br[k, 0] = branch[:half]
    br[k, 1] = branch[half:]


def backward_chunk(
    k, head, gm, xs, ysum, tot, cin, segp, ids, taps, raw, hp, delta_in, run_in, runt_in, ent,
    low_value, low_state, low_step, small, gheads, state, dtot, gpad,
):
    length = ids.shape[2]
    width = gm.shape[1]
    heads = raw.shape[1]
    total_width = tot.shape[1]
    states = (total_width - width) // 2
    lags = taps.shape[0]
    pad = cin.shape[0] - tot.shape[0]
    first = lanes_first(length, head)
    bias, rate, skip = hp[0:1, :], hp[1:2, :], hp[2:3, :]
    chan = lax.broadcasted_iota(jnp.int32, (2 * head, heads), 0)
    which = lax.broadcasted_iota(jnp.int32, (2 * head, heads), 1)
    row = lax.broadcasted_iota(jnp.int32, (length, length), 0)
    col = lax.broadcasted_iota(jnp.int32, (length, length), 1)
    above = (row <= col).astype(f32)
    rows = slice(k * length, (k + 1) * length)
    at = pad + k * length
    segc, same = chunk_masks(segp, at, length, lags)
    segr = ids[k, 0:1, :]
    before = segp[at - 1 : at, 0:1]
    run, runt, delta = run_in[rows, :], runt_in[k], delta_in[rows, :]
    negative = negative_mask(segc, segr)
    b = silu(tot[rows, width : width + states]).astype(bf16)
    c = silu(tot[rows, width + states :]).astype(bf16)
    scores = dot(c, b, 1, 1)
    tail = tails(run, segc)
    entry = entries(run, segc, before)
    through = entry[length - 1 : length, :]
    dscores = jnp.zeros((length, length), f32)
    u = jnp.zeros((length, heads), f32)
    q = jnp.zeros((1, heads), f32)
    vdx = jnp.zeros((length, heads), f32)
    gv = jnp.zeros((1, heads), f32)
    ge = jnp.zeros((1, heads), f32)
    db = jnp.zeros((length, states), f32)
    dc = jnp.zeros((length, states), f32)
    for pair in range(width // (2 * head)):
        part = slice(pair * 2 * head, (pair + 1) * 2 * head)
        pick = (which == 2 * pair + (chan >= head).astype(jnp.int32)).astype(f32)
        x = xs[rows, part]
        x32 = x.astype(f32)
        g32 = gm[rows, part].astype(f32)
        tl = spread_pair(first, tail, pair)
        grad_f32 = state[part, :]
        grad_f = grad_f32.astype(bf16)
        entering = ent[k, part, :]
        late = dot(b, grad_f, 1, 1) * tl
        dx = late
        for m in range(2):
            h = 2 * pair + m
            lanes = first if m == 0 else ~first
            gk = jnp.where(lanes, g32, 0.0).astype(bf16)
            decay = jnp.exp(run[:, h : h + 1] - runt[h : h + 1, :] + negative)
            w = (decay * scores).astype(bf16)
            dscores = dscores + decay * dot(gk, x, 1, 1)
            dx = dx + dot(w, gk, 0, 0)
        raw_v = tot[rows, part]
        sg = sigmoid(raw_v)
        v = raw_v * sg
        u = u + dot(g32 * ysum[rows, part] - x32 * dx, pick, precision=highest)
        q = q + dot(jnp.sum(x32 * late, axis=0, keepdims=True), pick, precision=highest)
        vdx = vdx + dot(v * dx, pick, precision=highest)
        gv = gv + dot(jnp.sum(g32 * v, axis=0, keepdims=True), pick, precision=highest)
        per_row = jnp.sum(grad_f32 * entering.astype(f32), axis=1, keepdims=True)
        ge = ge + jnp.sum(per_row * pick, axis=0, keepdims=True)
        dv = spread_pair(first, delta, pair) * dx + spread_pair(first[:1], skip, pair) * g32
        dtot[:, part] = dv * (sg * (1.0 + raw_v * (1.0 - sg)))
        db = db + dot((x32 * tl).astype(bf16), grad_f)
        scaled = (g32 * spread_pair(first, entry, pair)).astype(bf16)
        dc = dc + dot(scaled, entering)
        state[part, :] = fades(through, pair, head, 2 * head) * grad_f32 + dot(scaled, c, 0, 0)
    dsb = dscores.astype(bf16)
    dc = dc + dot(dsb, b)
    db = db + dot(dsb, c, 0, 0)
    dtot[:, width : width + states] = db * dsilu(tot[rows, width : width + states])
    dtot[:, width + states :] = dc * dsilu(tot[rows, width + states :])
    dld = dot(above, u, precision=highest) + (q + through * ge)
    ddelta = dld * rate + vdx
    gr = ddelta * sigmoid(raw[rows, :] + bias)
    low_step[rows, :] = gr.astype(bf16)
    gheads[0:1, :] = gheads[0:1, :] + jnp.sum(gr, axis=0, keepdims=True)
    gheads[1:2, :] = gheads[1:2, :] + jnp.sum(dld * delta, axis=0, keepdims=True) * rate
    gheads[2:3, :] = gheads[2:3, :] + gv
    for n in range(total_width // 128):
        part = slice(n * 128, n * 128 + 128)
        d = dtot[:, part]
        small[lags : lags + 1, part] = small[lags : lags + 1, part] + jnp.sum(d, axis=0, keepdims=True)
        for j in range(lags):
            ds = d * same[j]
            window = slice(at - j, at - j + length)
            small[j : j + 1, part] = small[j : j + 1, part] + jnp.sum(ds * cin[window, part], axis=0, keepdims=True)
            gpad[window, part] = gpad[window, part] + ds * taps[j : j + 1, part]
    low_value[rows, :] = gpad[at : at + length, :width].astype(bf16)
    low_state[rows, :] = gpad[at : at + length, width:].astype(bf16)


def ranked(slots):
    total = slots[0].astype(f32)
    for r in range(1, slots.shape[0]):
        total = total + slots[r].astype(f32)
    return total


class Shed:
    def __init__(self, own, slot, stage, send, recv):
        self.own, self.slot, self.stage, self.send, self.recv = own, slot, stage, send, recv
        self.me, self.size = lax.axis_index("ctx"), lax.axis_size("ctx")

    def hop(self, w, b):
        way = (1, -1)[w]
        return remote(
            self.stage.at[w, b], self.slot.at[w, b], self.send.at[w, b], self.recv.at[w, b], {"ctx": self.me + way}
        )

    def step(self, i):
        far = self.size - 1 - i
        for w, way in enumerate((1, -1)):
            b = self.me + way * far
            fed = inside(self.me - way, self.size) & inside(b, self.size)

            @pl.when(fed)
            def _(w=w, b=b, way=way):
                ref = self.slot.at[w, b]
                remote(ref, ref, self.send.at[w, b], self.recv.at[w, b], {"ctx": self.me - way}).wait_recv()
                if far:
                    self.stage[w, b] = (self.own[b] + self.slot[w, b].astype(f32)).astype(bf16)
                    self.hop(w, b).start()

            if far:
                @pl.when(jnp.logical_not(inside(self.me - way, self.size)) & inside(b, self.size))
                def _(w=w, b=b):
                    self.stage[w, b] = self.own[b].astype(bf16)
                    self.hop(w, b).start()

    def result(self, ref):
        ref[...] = self.own[self.me]
        for w, way in enumerate((1, -1)):
            @pl.when(inside(self.me - way, self.size))
            def _(w=w):
                ref[...] = ref[...] + self.slot[w, self.me].astype(f32)

    def finish(self):
        for b in range(self.size):
            for w, way in enumerate((1, -1)):
                @pl.when((b - self.me) * way > 0)
                def _(w=w, b=b):
                    self.hop(w, b).wait_send()


def whole_kernel(heads, head, inner, names, *refs):
    r = SimpleNamespace(**dict(zip(names, refs)))
    hid, cot, seg, wg, wv, ws, sw, wo = (r.hid, r.cot, r.seg, r.wg, r.wv, r.ws, r.sw, r.wo)
    H, CF, ids, WG, WV, WS, wst, WO = (r.H, r.CF, r.IDS, r.WG, r.WV, r.WS, r.WST, r.WO)
    in_gain, cw, cb, mg = (r.in_gain, r.cw, r.cb, r.mg)
    out, gh, dg, dv, do, dst, dstate, smalls = (r.out, r.gh, r.dg, r.dv, r.do, r.dst, r.dstate, r.smalls)
    hp, taps, offs, gain, segp, invs = (r.hp, r.taps, r.offs, r.gain, r.segp, r.invs)
    normed, gate, gg, cin, tot, xs, ysum, ent = (r.normed, r.gate, r.gg, r.cin, r.tot, r.xs, r.ysum, r.ent)
    delta, run, runt, raw, sums, state = (r.delta, r.run, r.runt, r.raw, r.sums, r.state)
    gated, low_gate, gm, mgain, br, go, gw = (r.gated, r.low_gate, r.gm, r.mgain, r.br, r.go, r.gw)
    low_value, low_state, low_step, small, gheads, dtot, gpad = (r.low_value, r.low_state, r.low_step, r.small, r.gheads, r.dtot, r.gpad)
    gv, gs, gt, npart, sib_b, sib_n, sib_s, own_b, own_n = (r.gv, r.gs, r.gt, r.npart, r.sib_b, r.sib_n, r.sib_s, r.own_b, r.own_n)
    slot_b, slot_n, stage_b, stage_n = (r.slot_b, r.slot_n, r.stage_b, r.stage_n)
    slot_g, slot_o, slot_v, slot_t, slot_m, slot_s, stage_s, all_s, acc, slot_q = (r.slot_g, r.slot_o, r.slot_v, r.slot_t, r.slot_m, r.slot_s, r.stage_s, r.all_s, r.acc, r.slot_q)
    ps, pr, qs, qr, zs, zr, ds, dr, ss, sr, ms, mr, es, er = (r.ps, r.pr, r.qs, r.qr, r.zs, r.zr, r.ds, r.dr, r.ss, r.sr, r.ms, r.mr, r.es, r.er)
    az, bz, af, bf, ad, bd, aq, bq = (r.az, r.bz, r.af, r.bf, r.ad, r.bd, r.aq, r.bq)
    ai, bi, mo, mp = (r.ai, r.bi, r.mo, r.mp)
    own_ids, own_step = r.own_ids, r.own_step

    c, d, t = lax.axis_index("ctx"), lax.axis_index("dp"), lax.axis_index("tensor")
    nc, nd, nt = lax.axis_size("ctx"), lax.axis_size("dp"), lax.axis_size("tensor")
    total = nc * nt
    me = c * nt + t
    length = ids.shape[2]
    width = WG.shape[2]
    half = br.shape[2]
    wide = slot_o.shape[2]
    lags = cw.shape[0]
    pad = 8
    sib = {"tensor": 1 - t}
    barrier = pltpu.get_barrier_semaphore()

    def peer(k):
        q = rot(me, k, total)
        return q, {"ctx": q // nt, "tensor": lax.rem(q, nt)}

    for k in range(1, nd):
        greet(barrier, {"dp": rot(d, k, nd)})
    for k in range(1, total):
        greet(barrier, peer(k)[1])
    own_ids[...] = jnp.broadcast_to(seg[...].astype(f32), own_ids.shape)
    spots = sw.shape[0]
    pick = lax.broadcasted_iota(jnp.int32, (spots, own_step.shape[0]), 0) - c * heads
    line = lax.broadcasted_iota(jnp.int32, (spots, own_step.shape[0]), 1)
    pick = ((pick == line) & (line < heads)).astype(bf16)
    own_step[...] = dot(pick, sw[...], 0, 0).astype(bf16)
    pl.semaphore_wait(barrier, nd + total - 2)

    def line_of(a, own, to, parts):
        size = half // parts

        def one(n):
            rows = spot(t * parts + n, size)

            def at(block):
                return to.at[block, rows]

            def onward(block, w, s):
                ref = at(block)
                return remote(ref, ref, af.at[a, n, w, s], bf.at[a, n, w, s], sib)

            return Line(own.at[rows], at, az.at[a, n], bz.at[a, n], onward)

        return Several([one(n) for n in range(parts)])

    early_ids = []
    line_h, line_c = line_of(0, hid, H, PARTS), line_of(1, cot, CF, PARTS // 2)
    for k in range(1, nc):
        copy = remote(own_ids, ids.at[c], ai.at[k - 1], bi.at[k - 1], {"ctx": rot(c, k, nc)})
        copy.start()
        early_ids.append(copy)
    line_h.start()
    moves = (
        (wv.at[:, spot(c, width)], lambda q: WV.at[q]),
        (ws, lambda q: WS.at[q]),
        (own_step, lambda q: wst.at[:, spot(q, wide)]),
        (wg.at[:, spot(c, width)], lambda q: WG.at[q]),
        (wo.at[spot(c, width), :], lambda q: WO.at[:, spot(q, wide)]),
    )
    early = list(early_ids)

    def give(a):
        src, to = moves[a]
        for k in range(1, nd):
            early.append(remote(src, to(d), ad.at[a, k - 1], bd.at[a, k - 1], {"dp": rot(d, k, nd)}))
            early[-1].start()

    def given(a):
        for k in range(1, nd):
            q = rot(d, -k, nd)
            ref = moves[a][1](q)
            remote(ref, ref, ad.at[a, k - 1], bd.at[a, k - 1], {"dp": q}).wait_recv()

    for a in range(3):
        give(a)
    H[c] = hid[...]
    CF[c] = cot[...]
    ids[c] = own_ids[...]
    WV[d] = wv[:, spot(c, width)]
    WG[d] = wg[:, spot(c, width)]
    WS[d] = ws[...]
    wst[:, spot(d, wide)] = own_step[...]
    WO[:, spot(d, wide)] = wo[spot(c, width), :]
    first_chan = t * nc + c
    taps[:, :width] = cw[:, spot(first_chan, width)]
    taps[:, width:] = cw[:, inner:]
    for n in range(offs.shape[1] // 128):
        part = slice(n * 128, n * 128 + 128)
        own = n * 128 < width
        at = first_chan * (width // 128) + n if own else inner // 128 + n - width // 128
        offs[:, part] = cb[pl.ds(at, 1), :]
        if own:
            gain[:, part] = mg[pl.ds(at, 1), :]
    lane = lax.broadcasted_iota(jnp.int32, (1, hp.shape[1]), 1)
    for n, source in enumerate((r.bias1, r.decay1, r.skip1)):
        row = jnp.zeros(lane.shape, f32)
        for i in range(heads):
            value = source[first_chan * heads + i]
            row = jnp.where(lane == i, value, row)
        hp[n : n + 1, :] = jnp.where(lane < heads, -jnp.exp(row), 0.0) if n == 1 else row
    cin[:pad, :] = jnp.zeros((pad, cin.shape[1]), f32)
    for ref in (state, gpad, small, gheads, sums, mgain):
        ref[...] = jnp.zeros_like(ref)
    gain_row = r.gain_row
    for n in range(in_gain.shape[0]):
        gain_row[:, n * 128 : n * 128 + 128] = in_gain[n : n + 1, :]
    in_gain = gain_row
    for s in range(nc - 1):
        line_h.step(s)
        if s == max(nc - 3, 0):
            line_c.start()
            give(3)
            give(4)
    for k in range(1, nc):
        q = rot(c, -k, nc)
        remote(own_ids, ids.at[q], ai.at[k - 1], bi.at[k - 1], {"ctx": q}).wait_recv()
    segp[:pad, :] = jnp.full((pad, segp.shape[1]), -1.0, f32)
    for k in range(nc):
        segp[pad + k * length : pad + (k + 1) * length, :] = ids[k].T
    for a in range(3):
        given(a)
    line_h.arrived()
    WGr, WVr, WSr = (ref.reshape(ref.shape[0] * ref.shape[1], ref.shape[2]) for ref in (WG, WV, WS))
    for k in range(nc):
        scan_chunk(
            k, head, H, ids, WVr, WSr, wst, in_gain, hp,
            normed, cin, tot, xs, ysum, ent, delta, run, runt, raw, segp, taps, offs, invs, state,
        )
        if k < nc - 1:
            line_c.step(k)
    given(3)
    given(4)
    line_c.arrived()
    for k in range(nc):
        product_chunk(k, head, length, CF, WO, normed, WGr, hp, gain, tot, ysum, gate, gg, sums)
    slot_q[me] = sums[...]
    for k in range(1, total):
        early.append(remote(sums, slot_q.at[me], aq.at[k - 1], bq.at[k - 1], peer(k)[1]))
        early[-1].start()
    for k in range(1, total):
        q, device = peer(-k)
        remote(sums, slot_q.at[q], aq.at[k - 1], bq.at[k - 1], device).wait_recv()
    added = ranked(slot_q).T
    state[...] = jnp.zeros_like(state)
    sent = []

    def launch(copy):
        copy.start()
        sent.append(copy)

    def swap(a, k, src, dst):
        return remote(src.at[k, 1 - t], dst.at[k], ps.at[a, k], pr.at[a, k], sib)

    def scatter(a, src, slot):
        for k in range(1, nd):
            p = rot(d, k, nd)
            launch(remote(src(p), slot.at[d], ds.at[a, k - 1], dr.at[a, k - 1], {"dp": p}))

    def columns(ref):
        return lambda p: ref.at[:, spot(p, wide)]

    def collected(a, slot):
        for k in range(1, nd):
            r = rot(d, -k, nd)
            remote(slot.at[r], slot.at[r], ds.at[a, k - 1], dr.at[a, k - 1], {"dp": r}).wait_recv()
        return ranked(slot)

    def owned(a, src, other, own):
        for k in range(nc):
            swap(a, k, src, other).wait_recv()
            own[k] = src[k, t].astype(f32) + other[k].astype(f32)

    def place(a, ref, block):
        ref[c] = block.astype(bf16)
        line = Line(ref.at[c], lambda block: ref.at[block], zs.at[a], zr.at[a])
        line.start()
        return line

    for k in range(nc):
        gate_chunk(
            k, head, inner, length, added, hp, gain, tot, ysum, gate, gg, WO, gated, low_gate, gm, mgain, br
        )
        launch(swap(0, k, br, sib_b))
    gw[...] = dot(low_gate[...], normed[...], 0, 0).astype(bf16)
    scatter(0, columns(gw), slot_g)
    cfr = CF.reshape(nc * length, CF.shape[2])
    go[...] = dot(gated[...], cfr[...], 0, 0).astype(bf16)
    scatter(1, columns(go), slot_o)
    slot_g[d] = gw[:, spot(d, wide)]
    slot_o[d] = go[:, spot(d, wide)]

    def shed_of(a, own, slot, stage, parts):
        size = half // parts
        items = []
        for n in range(parts):
            rows = pl.ds(n * size, size)
            views = (own.at[:, rows], slot.at[:, :, rows], stage.at[:, :, rows])
            items.append(Shed(*views, qs.at[a, n], qr.at[a, n]))
            items[-1].rows = rows
        return Several(items)

    def shed_sum(shed):
        for item in shed.items:
            item.result(acc.at[item.rows])

    shed_b = shed_of(0, own_b, slot_b, stage_b, PARTS // 2)
    shed_n = shed_of(1, own_n, slot_n, stage_n, PARTS)
    lines = []

    def begin():
        owned(0, br, sib_b, own_b)
        shed_b.step(0)

    def settle():
        lines.append(place(0, dg, collected(0, slot_g).T))
        lines.append(place(1, do, collected(1, slot_o)))

    def onto(s):
        for item in lines:
            item.step(s)

    tasks = [partial(shed_b.step, 1), settle]
    tasks += [partial(shed_b.step, i) for i in range(2, nc - 1)] + [partial(onto, 0)]
    tasks += [partial(shed_b.step, i) for i in range(max(2, nc - 1), nc)]
    tasks += [partial(onto, i) for i in range(1, nc - 1)]

    def turn(count=1):
        for _ in range(count):
            if tasks:
                tasks.pop(0)()

    begin()
    for i in range(nc):
        backward_chunk(
            nc - 1 - i, head, gm, xs, ysum, tot, cin, segp, ids, taps, raw, hp, delta, run, runt, ent,
            low_value, low_state, low_step, small, gheads, state, dtot, gpad,
        )
        turn((0, 1, 2)[i] if i < 3 else 0)
    gs[...] = dot(low_state[...], normed[...], 0, 0).astype(bf16)
    side = wide // 2

    def cross(p):
        return remote(gs.at[:, spot(2 * p + 1 - t, side)], sib_s.at[p], ps.at[2, p], pr.at[2, p], sib)

    for p in range(nd):
        launch(cross(p))
    gv[...] = dot(low_value[...], normed[...], 0, 0).astype(bf16)
    scatter(2, columns(gv), slot_v)
    gt[...] = dot(low_step[...], normed[...], 0, 0).astype(bf16)
    scatter(3, columns(gt), slot_t)
    turn(1)
    slot_v[d] = gv[:, spot(d, wide)]
    slot_t[d] = gt[:, spot(d, wide)]
    for k in range(nc):
        rows = slice(k * length, (k + 1) * length)
        part = dot(low_gate[rows, :], WGr[...], 1, 1) + dot(low_value[rows, :], WVr[...], 1, 1)
        part = part + dot(low_state[rows, :], WSr[...], 1, 1) + dot(low_step[rows, :], wst[...])
        unit = H[k].astype(f32) * invs[rows, :]
        gained = jnp.sum(part * unit, axis=0, keepdims=True)
        for m in range(gained.shape[1] // small.shape[1]):
            at = lags + 2 + m
            small[at : at + 1, :] = small[at : at + 1, :] + gained[:, m * small.shape[1] : (m + 1) * small.shape[1]]
        part = part.astype(bf16)
        npart[k, 0] = part[:half]
        npart[k, 1] = part[half:]
        launch(swap(1, k, npart, sib_n))
        if k == nc // 2:
            for p in range(nd):
                cross(p).wait_recv()
                stage_s[p] = (gs[:, spot(2 * p + t, side)].astype(f32) + sib_s[p].astype(f32)).astype(bf16)
            for k in range(1, nd):
                p = rot(d, k, nd)
                launch(remote(stage_s.at[p], slot_s.at[d], ss.at[k - 1], sr.at[k - 1], {"dp": p}))
            slot_s[d] = stage_s[d]
    small[lags + 1 : lags + 2, :width] = mgain[...]
    small[small.shape[0] - 8 :, : raw.shape[1]] = gheads[...]
    scatter(4, lambda p: small, slot_m)
    slot_m[d] = small[...]
    owned(1, npart, sib_n, own_n)
    shed_n.step(0)
    late = place(2, dv, collected(2, slot_v).T)

    def cast(a, ref, block):
        ref[c] = block.astype(ref.dtype)
        casts.append(Cast(lambda block: ref.at[block], zs.at[a, 0], zr.at[a, 0]))
        casts[-1].start()

    casts = []
    cast(3, dst, collected(3, slot_t))
    for k in range(1, nd):
        r = rot(d, -k, nd)
        remote(slot_s.at[r], slot_s.at[r], ss.at[k - 1], sr.at[k - 1], {"dp": r}).wait_recv()
    cast(5, all_s, ranked(slot_s))
    smalls[c, t] = collected(4, slot_m)
    casts.append(Cast(lambda block: smalls.at[block, t], zs.at[4, 0], zr.at[4, 0]))
    casts[-1].start()
    ends = [(smalls.at[c, t], smalls.at[c, 1 - t], 3)]
    remote(smalls.at[c, t], smalls.at[c, t], es.at[3], er.at[3], sib).start()
    turn(2)

    def end(ref, e):
        ends.append((ref.at[t], ref.at[1 - t], e))
        remote(ref.at[t], ref.at[t], es.at[e], er.at[e], sib).start()

    rows = spot(t, half)
    base = hid[rows, :].astype(f32)
    for i in range(1, nc):
        shed_n.step(i)
        turn()
        late.step(i - 1)
    shed_sum(shed_b)
    out[t] = (base + acc[...]).astype(bf16)
    end(out, 1)
    shed_sum(shed_n)
    gn = acc[...]
    inv = lax.rsqrt(jnp.mean(base * base, axis=-1, keepdims=True) + epsilon)
    gsx = gn * in_gain[...]
    grad = inv * (gsx - base * (inv * inv) * jnp.mean(gsx * base, axis=-1, keepdims=True))
    gh[t] = cot[rows, :].astype(f32) + grad
    end(gh, 2)
    while tasks:
        turn()
    for item in casts:
        item.arrived()

    def hand(k, mine):
        block = rot(c, -k, nc)
        ref = smalls.at[block, t if mine else 1 - t]
        return remote(ref, ref, mo.at[k - 1], mp.at[k - 1], sib)

    for k in range(1, nc):
        hand(k, True).start()
    dstate[t] = ranked(all_s).T
    end(dstate, 0)
    for item in lines + casts + [late, shed_b, shed_n, line_h, line_c]:
        item.finish()
    for k in range(1, nc):
        hand(k, True).wait_send()
        hand(k, False).wait_recv()
    for copy in early:
        copy.wait_send()
    for copy in sent:
        copy.wait_send()
    for mine, theirs, e in ends:
        remote(mine, mine, es.at[e], er.at[e], sib).wait_send()
        remote(theirs, theirs, es.at[e], er.at[e], sib).wait_recv()


def finish_kernel(
    heads, out_in, gh_in, dg, dv, do, dst, dstate, smalls,
    out, gh, g_in, g_gate, g_value, g_state, g_step, g_conv, g_offs, g_gain, g_out, *g_heads,
):
    nc, nt = smalls.shape[0], smalls.shape[1]
    width = dg.shape[2]
    lags = g_conv.shape[0]
    inner = g_gain.shape[0] * 128
    half = out_in.shape[1]
    side = dstate.shape[1]
    hpad = dst.shape[1]
    headed_shape = (hpad, g_heads[0].shape[1])
    for m in range(2):
        out[m * half : (m + 1) * half, :] = out_in[m]
        gh[m * half : (m + 1) * half, :] = gh_in[m]
        g_state[m * side : (m + 1) * side, :] = dstate[m]
    shared, headed = None, jnp.zeros((8, g_heads[0].shape[1]), f32)
    for k in range(nc):
        part = slice(k * width, (k + 1) * width)
        g_gate[:, part] = dg[k].astype(f32)
        g_value[:, part] = dv[k].astype(f32)
        g_out[part, :] = do[k].astype(f32)
        g_step[k * heads : (k + 1) * heads, :] = dst[k, :, :].astype(f32)[:heads]
        for t in range(nt):
            mine = smalls[k, t]
            at = t * nc + k
            part = slice(at * width, (at + 1) * width)
            g_conv[:, part] = mine[:lags, :width]
            for n in range(width // 128):
                row = slice(at * (width // 128) + n, at * (width // 128) + n + 1)
                g_offs[row, :] = mine[lags : lags + 1, n * 128 : n * 128 + 128]
                g_gain[row, :] = mine[lags + 1 : lags + 2, n * 128 : n * 128 + 128]
            lane = lax.broadcasted_iota(jnp.int32, headed_shape, 1)
            line = lax.broadcasted_iota(jnp.int32, headed_shape, 0)
            pick = ((lane == line + at * heads) & (line < heads)).astype(f32)
            headed = headed + dot(mine[mine.shape[0] - 8 :, :hpad], pick, precision=highest)
            shared = mine if shared is None else shared + mine
    for n, ref in enumerate(g_heads):
        ref[...] = headed[n : n + 1]
    g_conv[:, inner:] = shared[:lags, width:]
    for n in range((shared.shape[1] - width) // 128):
        at = width + n * 128
        row = inner // 128 + n
        g_offs[row : row + 1, :] = shared[lags : lags + 1, at : at + 128]
    each = shared.shape[1] // 128
    for n in range(g_in.shape[0]):
        line = lags + 2 + n // each
        g_in[n : n + 1, :] = shared[line : line + 1, n % each * 128 : n % each * 128 + 128]


def sd(shape, kind):
    return jax.ShapeDtypeStruct(tuple(shape), kind)


def run_kernel(kernel, outs, args, scratch=(), name=None, ident=None):
    extra = {} if ident is None else dict(collective_id=ident, has_side_effects=True)
    return pl.pallas_call(
        kernel,
        out_shape=tuple(sd(s, k) for s, k in outs),
        in_specs=[VM] * len(args),
        out_specs=tuple([VM] * len(outs)),
        scratch_shapes=list(scratch),
        compiler_params=pltpu.CompilerParams(vmem_limit_bytes=LIMIT, **extra),
        name=name,
    )(*args)


def sems(*shape):
    return pltpu.SemaphoreType.DMA(shape)


def spread_body(
    hidden, segment_ids, cotangent, input_gain, gate_weight, value_weight, state_weight, step_weight,
    conv_weight, conv_bias, step_bias, decay_log, skip_gain, mixer_gain, out_weight,
):
    tokens, cot = hidden[0], cotangent[0]
    length, D = tokens.shape
    c, t = lax.axis_index("ctx"), lax.axis_index("tensor")
    nc, nd, nt = lax.axis_size("ctx"), lax.axis_size("dp"), lax.axis_size("tensor")
    width = gate_weight.shape[1] // nc
    inner = width * nc * nt
    heads_all = step_bias.shape[0]
    heads = heads_all // (nc * nt)
    hpad = 16 * ((heads + 15) // 16)
    head = width // heads
    states = state_weight.shape[1] // 2
    W = width + 2 * states
    T = length * nc
    rows = D // nd
    lags = conv_weight.shape[0]
    total = nc * nt
    half = length // 2
    shalf = rows // 2
    srows = 8 * ((2 * nc + 7) // 8)
    srow = 8 * ((lags + 2 + D // W + 7) // 8) + 8
    ins = dict(
        hid=tokens, cot=cot, seg=segment_ids, wg=gate_weight, wv=value_weight, ws=state_weight,
        sw=step_weight.T, wo=out_weight, in_gain=input_gain.reshape(-1, 128), cw=conv_weight,
        cb=conv_bias.reshape(-1, 128), mg=mixer_gain.reshape(-1, 128),
        bias1=step_bias, decay1=decay_log, skip1=skip_gain,
    )
    outs = dict(
        out=((2, half, D), bf16), gh=((2, half, D), f32), dg=((nc, rows, width), bf16),
        dv=((nc, rows, width), bf16), do=((nc, width, rows), bf16), dst=((nc, hpad, rows), bf16),
        dstate=((2, shalf, 2 * states), f32), smalls=((nc, nt, srow, W), f32),
    )
    rooms = dict(
        H=((nc, length, D), bf16), CF=((nc, length, D), bf16), IDS=((nc, 8, length), f32),
        WG=((nd, rows, width), bf16), WV=((nd, rows, width), bf16), WS=((nd, rows, 2 * states), bf16),
        WST=((hpad, D), bf16), WO=((width, D), bf16), own_ids=((8, length), f32),
        own_step=((hpad, rows), bf16), hp=((8, hpad), f32), taps=((lags, W), f32), offs=((1, W), f32),
        gain=((1, width), f32), gain_row=((1, D), f32), segp=((T + 8, 8), f32), invs=((T, 1), f32),
        normed=((T, D), bf16), gate=((T, width), f32), gg=((T, width), f32), cin=((T + 8, W), f32),
        tot=((T, W), f32), xs=((T, width), bf16), ysum=((T, width), f32),
        ent=((nc, width, states), bf16), delta=((T, hpad), f32), run=((T, hpad), f32),
        runt=((nc, hpad, length), f32), raw=((T, hpad), f32), sums=((srows, length), f32),
        state=((width, states), f32), gated=((T, width), bf16), low_gate=((T, width), bf16),
        gm=((T, width), bf16), mgain=((1, width), f32), br=((nc, 2, half, D), bf16),
        go=((width, D), bf16), gw=((width, D), bf16), low_value=((T, width), bf16),
        low_state=((T, 2 * states), bf16), low_step=((T, hpad), bf16), small=((srow, W), f32),
        gheads=((8, hpad), f32), dtot=((length, W), f32), gpad=((T + 8, W), f32),
        gv=((width, D), bf16), gs=((2 * states, D), bf16), gt=((hpad, D), bf16),
        npart=((nc, 2, half, D), bf16), sib_b=((nc, half, D), bf16), sib_n=((nc, half, D), bf16),
        sib_s=((nd, 2 * states, shalf), bf16), own_b=((nc, half, D), f32), own_n=((nc, half, D), f32),
        slot_b=((2, nc, half, D), bf16), slot_n=((2, nc, half, D), bf16),
        stage_b=((2, nc, half, D), bf16), stage_n=((2, nc, half, D), bf16),
        slot_g=((nd, width, rows), bf16), slot_o=((nd, width, rows), bf16),
        slot_v=((nd, width, rows), bf16), slot_t=((nd, hpad, rows), bf16), slot_m=((nd, srow, W), f32),
        slot_s=((nd, 2 * states, shalf), bf16), stage_s=((nd, 2 * states, shalf), bf16),
        all_s=((nc, 2 * states, shalf), bf16), acc=((half, D), f32), slot_q=((total, srows, length), f32),
    )
    most, hop = max(nc, nd), nc - 1
    flags = dict(
        ps=(3, most), pr=(3, most), qs=(2, PARTS, 2, nc), qr=(2, PARTS, 2, nc), zs=(6, 2, hop), zr=(6, 2, hop),
        ds=(5, nd - 1), dr=(5, nd - 1), ss=(nd - 1,), sr=(nd - 1,), ms=(2, hop), mr=(2, hop),
        es=(4,), er=(4,), az=(2, PARTS, 2, hop), bz=(2, PARTS, 2, hop), af=(2, PARTS, 2, hop), bf=(2, PARTS, 2, hop),
        ai=(hop,), bi=(hop,), mo=(hop,), mp=(hop,),
        ad=(5, nd - 1), bd=(5, nd - 1), aq=(total - 1,), bq=(total - 1,),
    )
    scalars = pl.BlockSpec(memory_space=pltpu.SMEM)
    names = tuple(ins) + tuple(outs) + tuple(rooms) + tuple(flags)
    made = pl.pallas_call(
        partial(whole_kernel, heads, head, inner, names),
        out_shape=tuple(sd(*v) for v in outs.values()),
        in_specs=[scalars if n.endswith("1") else VM for n in ins],
        out_specs=tuple([VM] * len(outs)),
        scratch_shapes=[pltpu.VMEM(*v) for v in rooms.values()] + [sems(*v) for v in flags.values()],
        compiler_params=pltpu.CompilerParams(vmem_limit_bytes=FULL, collective_id=0, has_side_effects=True),
        name="whole",
    )(*ins.values())
    outs = run_kernel(
        partial(finish_kernel, heads),
        (
            ((length, D), bf16), ((length, D), f32), ((D // 128, 128), f32), ((rows, nc * width), f32),
            ((rows, nc * width), f32), ((rows, 2 * states), f32), ((nc * heads, rows), f32),
            ((lags, inner + 2 * states), f32), (((inner + 2 * states) // 128, 128), f32),
            ((inner // 128, 128), f32), ((nc * width, rows), f32),
        )
        + (((1, heads_all), f32),) * 3,
        made,
        (),
        "finish",
    )
    out, gh, g_in, g_gate, g_value, g_state, g_step, g_conv, g_offs, g_gain, g_out, *g_heads = outs
    return (
        out[None], gh[None], g_in.reshape(-1), g_gate, g_value, g_state, g_step.T, g_conv, g_offs.reshape(-1),
        *(v.reshape(-1) for v in g_heads), g_gain.reshape(-1), g_out,
    )


def fits(mesh, args):
    nc, nd, nt = mesh.shape["ctx"], mesh.shape["dp"], mesh.shape["tensor"]
    hidden, gate_weight, state_weight, step_bias = args[0], args[4], args[6], args[10]
    seqs, tokens, D = hidden.shape
    inner, heads = gate_weight.shape[1], step_bias.shape[0]
    groups = nc * nt
    if nt != 2 or seqs != nd or heads % (2 * groups) or inner % (128 * groups):
        return False
    length = tokens // nc
    states = state_weight.shape[1]
    if D % (256 * nd) or D % (inner // groups + states) or nc % 2:
        return False
    return tokens * (D + inner // groups) <= 2 << 20 and length % 128 == 0


def solution(mesh):
    in_specs = (
        P("dp", "ctx", None),
        P("dp", "ctx"),
        P("dp", "ctx", None),
        P(),
        P("dp", "tensor"),
        P("dp", "tensor"),
        P("dp", None),
        P("dp", "tensor"),
        P(),
        P(),
        P(),
        P(),
        P(),
        P(),
        P("tensor", "dp"),
    )
    out_specs = (
        P("dp", "ctx", None),
        P("dp", "ctx", None),
        P(),
        P("dp", "tensor"),
        P("dp", "tensor"),
        P("dp", None),
        P("dp", "tensor"),
        P(),
        P(),
        P(),
        P(),
        P(),
        P(),
        P("tensor", "dp"),
    )

    def whole(*args):
        chosen = spread_body if fits(mesh, args) else body
        return jax.shard_map(chosen, mesh=mesh, in_specs=in_specs, out_specs=out_specs, check_vma=False)(*args)

    return whole
```

```python
from functools import partial
from types import SimpleNamespace

import jax
import jax.numpy as jnp
from jax import lax
from jax.experimental import pallas as pl
from jax.experimental.pallas import tpu as pltpu
from jax.sharding import PartitionSpec as P

epsilon = 1e-05
highest = lax.Precision.HIGHEST
f32, bf16 = jnp.float32, jnp.bfloat16
MESH = pl.DeviceIdType.MESH
VM = pl.BlockSpec(memory_space=pltpu.VMEM)
ANY = pl.BlockSpec(memory_space=pl.ANY)
LIMIT = 56 * 1024 * 1024
FULL = 60 * 1024 * 1024
PARTS = 4


def dot(a, b, ca=1, cb=0, precision=None):
    return lax.dot_general(
        a, b, (((ca,), (cb,)), ((), ())), precision=precision, preferred_element_type=f32
    )


def shifted(array, axis, by):
    size = lax.axis_size(axis)
    pairs = [(i, i + by) for i in range(size) if 0 <= i + by < size]
    return lax.ppermute(array, axis, pairs)


def chain_kernel(axis, by, chunks, local_ref, fade_ref, out_ref, landed, outgoing, send, recv):
    size = lax.axis_size(axis)
    me = lax.axis_index(axis)
    follower = lax.rem(me + by + size, size)
    leader = lax.rem(me - by + size, size)
    first, last = (0, size - 1) if by > 0 else (size - 1, 0)
    rows = local_ref.shape[0] // chunks
    barrier = pltpu.get_barrier_semaphore()

    @pl.when(me != first)
    def _():
        pl.semaphore_signal(barrier, inc=1, device_id={axis: leader}, device_id_type=MESH)

    @pl.when(me != last)
    def _():
        pl.semaphore_wait(barrier, 1)

    def copy(c):
        part = pl.ds(c * rows, rows)
        return pltpu.make_async_remote_copy(
            src_ref=outgoing.at[part],
            dst_ref=landed.at[part],
            send_sem=send.at[c],
            recv_sem=recv.at[c],
            device_id={axis: follower},
            device_id_type=MESH,
        )

    @pl.when(me == first)
    def _():
        landed[...] = jnp.zeros_like(landed)

    for c in range(chunks):
        part = pl.ds(c * rows, rows)

        @pl.when(me != first)
        def _():
            copy(c).wait_recv()

        @pl.when(me != last)
        def _():
            total = fade_ref[part, :] * landed[part, :].astype(f32) + local_ref[part, :].astype(f32)
            outgoing[part, :] = total.astype(outgoing.dtype)
            copy(c).start()

    out_ref[...] = landed[...]

    @pl.when(me != last)
    def _():
        for c in range(chunks):
            copy(c).wait_send()


def chain(local, fade, axis, by, ident, chunks=4):
    return pl.pallas_call(
        partial(chain_kernel, axis, by, chunks),
        out_shape=jax.ShapeDtypeStruct(local.shape, local.dtype),
        in_specs=[VM, VM],
        out_specs=VM,
        scratch_shapes=[
            pltpu.VMEM(local.shape, local.dtype),
            pltpu.VMEM(local.shape, local.dtype),
            pltpu.SemaphoreType.DMA((chunks,)),
            pltpu.SemaphoreType.DMA((chunks,)),
        ],
        compiler_params=pltpu.CompilerParams(collective_id=ident, has_side_effects=True),
        name="chain",
    )(local, fade)


def pair_kernel(axis, src_ref, out_ref, slots, send, recv):
    size = lax.axis_size(axis)
    me = lax.axis_index(axis)
    barrier = pltpu.get_barrier_semaphore()
    for k in range(1, size):
        pl.semaphore_signal(
            barrier, inc=1, device_id={axis: lax.rem(me + k, size)}, device_id_type=MESH
        )
    pl.semaphore_wait(barrier, size - 1)
    copies = []
    for k in range(1, size):
        copies.append(
            pltpu.make_async_remote_copy(
                src_ref=src_ref,
                dst_ref=slots.at[k - 1],
                send_sem=send.at[k - 1],
                recv_sem=recv.at[k - 1],
                device_id={axis: lax.rem(me + k, size)},
                device_id_type=MESH,
            )
        )
        copies[-1].start()
    for copy in copies:
        copy.wait()
    total = src_ref[...].astype(f32)
    for k in range(1, size):
        total = total + slots[k - 1].astype(f32)
    out_ref[...] = total


def pair_sum(array, axis, ident):
    size = lax.axis_size(axis)
    return pl.pallas_call(
        partial(pair_kernel, axis),
        out_shape=jax.ShapeDtypeStruct(array.shape, f32),
        in_specs=[VM],
        out_specs=VM,
        scratch_shapes=[
            pltpu.VMEM((size - 1,) + array.shape, array.dtype),
            pltpu.SemaphoreType.DMA((size - 1,)),
            pltpu.SemaphoreType.DMA((size - 1,)),
        ],
        compiler_params=pltpu.CompilerParams(
            collective_id=ident, has_side_effects=True, vmem_limit_bytes=LIMIT
        ),
        name="pair_sum",
    )(array)


def gather_kernel(axis, count, *refs):
    ins, outs = refs[:count], refs[count : 2 * count]
    local, send, recv = refs[2 * count :]
    me = lax.axis_index(axis)
    low, high = lax.rem(me, 2), me // 2
    side = high * 2 + (1 - low)
    other = (1 - high) * 2 + low
    corner = (1 - high) * 2 + (1 - low)
    barrier = pltpu.get_barrier_semaphore()
    for peer in (side, other):
        pl.semaphore_signal(barrier, inc=1, device_id={axis: peer}, device_id_type=MESH)
    own = []
    for a in range(count):
        own.append(pltpu.make_async_copy(ins[a], outs[a].at[me], local.at[a]))
        own[-1].start()
    pl.semaphore_wait(barrier, 2)

    def remote(a, src, dst, slot, peer):
        return pltpu.make_async_remote_copy(
            src_ref=src,
            dst_ref=dst,
            send_sem=send.at[a, slot],
            recv_sem=recv.at[a, slot],
            device_id={axis: peer},
            device_id_type=MESH,
        )

    direct = []
    for a in range(count):
        for slot, peer in ((0, side), (1, other)):
            direct.append(remote(a, ins[a], outs[a].at[me], slot, peer))
            direct[-1].start()
    relays = []
    for a in range(count):
        half = ins[a].shape[0] // 2
        lower, upper = pl.ds(0, half), pl.ds(half, half)
        remote(a, ins[a], outs[a].at[side], 0, side).wait_recv()
        relay = remote(a, outs[a].at[side, lower], outs[a].at[side, lower], 2, other)
        relay.start()
        relays.append(relay)
        remote(a, ins[a], outs[a].at[other], 1, other).wait_recv()
        relay = remote(a, outs[a].at[other, upper], outs[a].at[other, upper], 3, side)
        relay.start()
        relays.append(relay)
    for a in range(count):
        half = ins[a].shape[0] // 2
        lower, upper = pl.ds(0, half), pl.ds(half, half)
        remote(a, outs[a].at[corner, lower], outs[a].at[corner, lower], 2, other).wait_recv()
        remote(a, outs[a].at[corner, upper], outs[a].at[corner, upper], 3, side).wait_recv()
    for copy in direct + relays:
        copy.wait_send()
    for copy in own:
        copy.wait()


def gather(arrays, axis, ident):
    size = lax.axis_size(axis)
    if size != 4:
        return tuple(lax.all_gather(a, axis) for a in arrays)
    count = len(arrays)
    return pl.pallas_call(
        partial(gather_kernel, axis, count),
        out_shape=tuple(jax.ShapeDtypeStruct((size,) + a.shape, a.dtype) for a in arrays),
        in_specs=[VM] * count,
        out_specs=tuple([VM] * count),
        scratch_shapes=[
            pltpu.SemaphoreType.DMA((count,)),
            pltpu.SemaphoreType.DMA((count, 4)),
            pltpu.SemaphoreType.DMA((count, 4)),
        ],
        compiler_params=pltpu.CompilerParams(
            collective_id=ident, has_side_effects=True, vmem_limit_bytes=LIMIT
        ),
        name="gather",
    )(*arrays)


def sigmoid(v):
    return 1.0 / (1.0 + jnp.exp(-v))


def silu(v):
    return v / (1.0 + jnp.exp(-v))


def dsilu(v):
    s = sigmoid(v)
    return s * (1.0 + v * (1.0 - s))


def softplus(v):
    return jnp.maximum(v, 0.0) + jnp.log1p(jnp.exp(-jnp.abs(v)))


def spread_pair(first_lanes, table, pair):
    return jnp.where(first_lanes, table[:, 2 * pair : 2 * pair + 1], table[:, 2 * pair + 1 : 2 * pair + 2])


def lanes_first(length, head):
    return lax.broadcasted_iota(jnp.int32, (length, 2 * head), 1) < head


def negative_mask(segc, segr):
    length = segc.shape[0]
    row = lax.broadcasted_iota(jnp.int32, (length, length), 0)
    col = lax.broadcasted_iota(jnp.int32, (length, length), 1)
    return jnp.where((segc == segr) & (row >= col), 0.0, -1e30).astype(f32)


def tails(run, segc):
    length = segc.shape[0]
    return jnp.exp(run[length - 1 : length, :] - run) * (segc == segc[length - 1 : length]).astype(f32)


def local_kernel(
    width, head, cin, same, taps, offs, raw, bias, rate, segc, segr,
    tot, intra, xs, final, delta_out, run_out, runt_out, wide,
):
    length = segc.shape[0]
    total_width = cin.shape[1]
    states = (total_width - width) // 2
    wide[...] = cin[...].astype(f32)
    lags = taps.shape[0]
    pad = cin.shape[0] - length
    for c in range(total_width // 128):
        part = slice(c * 128, c * 128 + 128)
        acc = jnp.broadcast_to(offs[:, part], (length, 128))
        for j in range(lags):
            acc = acc + taps[j : j + 1, part] * (wide[pad - j : pad - j + length, part] * same[:, j : j + 1])
        tot[:, part] = acc
    delta = softplus(raw[...] + bias[...])
    delta_out[...] = delta
    row = lax.broadcasted_iota(jnp.int32, (length, length), 0)
    col = lax.broadcasted_iota(jnp.int32, (length, length), 1)
    below = (row >= col).astype(f32)
    decay = delta * rate[...]
    run = dot(below, decay, precision=highest)
    run_out[...] = run
    runt = run.T
    runt_out[...] = runt
    b = silu(tot[:, width : width + states]).astype(bf16)
    c = silu(tot[:, width + states :]).astype(bf16)
    scores = dot(c, b, 1, 1)
    negative = negative_mask(segc[...], segr[...])
    first = lanes_first(length, head)
    tail = tails(run, segc[...])
    for pair in range(width // (2 * head)):
        part = slice(pair * 2 * head, (pair + 1) * 2 * head)
        x = (silu(tot[:, part]) * spread_pair(first, delta, pair)).astype(bf16)
        xs[:, part] = x
        x32 = x.astype(f32)
        faded = (x32 * spread_pair(first, tail, pair)).astype(bf16)
        final[part, :] = dot(faded, b, 0, 0).astype(bf16)
        total = None
        for k in range(2):
            h = 2 * pair + k
            w = (jnp.exp(run[:, h : h + 1] - runt[h : h + 1, :] + negative) * scores).astype(bf16)
            xk = jnp.where(first if k == 0 else ~first, x32, 0.0).astype(bf16)
            term = dot(w, xk)
            total = term if total is None else total + term
        intra[:, part] = total


def entries(run, segc, before):
    return jnp.exp(run) * (segc == before).astype(f32)


def product_kernel(
    width, head, inner, ctot_ref, tot, intra, entering, run, segc, before, gate, gg, gain, skip, ysum, sums,
):
    length = segc.shape[0]
    first = lanes_first(length, head)
    c = silu(ctot_ref[...]).astype(bf16)
    entry = entries(run[...], segc[...], before[...])
    squares = jnp.zeros((length, 1), f32)
    project = jnp.zeros((length, 1), f32)
    for pair in range(width // (2 * head)):
        part = slice(pair * 2 * head, (pair + 1) * 2 * head)
        y = intra[:, part] + dot(c, entering[part, :], 1, 1) * spread_pair(first, entry, pair)
        ysum[:, part] = y
        mixed = y + spread_pair(first[:1], skip[...], pair) * silu(tot[:, part])
        product = mixed * silu(gate[:, part])
        squares = squares + jnp.sum(product * product, axis=1, keepdims=True)
        project = project + jnp.sum(gg[:, part] * gain[:, part] * product, axis=1, keepdims=True)
    lane = lax.broadcasted_iota(jnp.int32, sums.shape, 1)
    sums[...] = jnp.where(lane == 0, squares, jnp.where(lane == 1, project, 0.0))


def norm_kernel(
    width, head, inner, ctot_ref, tot, ysum, run, segc, before, gate, gg, gain, skip, sums,
    gated, low_gate, gm, grad_entering, grad_gain,
):
    length = segc.shape[0]
    first = lanes_first(length, head)
    c = silu(ctot_ref[...]).astype(bf16)
    entry = entries(run[...], segc[...], before[...])
    scale = lax.rsqrt(sums[:, 0:1] / inner + epsilon)
    project = scale * sums[:, 1:2] / inner
    for pair in range(width // (2 * head)):
        part = slice(pair * 2 * head, (pair + 1) * 2 * head)
        mixed = ysum[:, part] + spread_pair(first[:1], skip[...], pair) * silu(tot[:, part])
        z = gate[:, part]
        sg = sigmoid(z)
        act = z * sg
        unit = mixed * act * scale
        gated[:, part] = (unit * gain[:, part]).astype(bf16)
        g = gg[:, part]
        grad_gain[:, part] = jnp.sum(g * unit, axis=0, keepdims=True)
        gp = scale * (g * gain[:, part] - unit * project)
        gmix = gp * act
        low_gate[:, part] = (gp * mixed * sg * (1.0 + z * (1.0 - sg))).astype(bf16)
        gmb = gmix.astype(bf16)
        gm[:, part] = gmb
        scaled = (gmb.astype(f32) * spread_pair(first, entry, pair)).astype(bf16)
        grad_entering[part, :] = dot(scaled, c, 0, 0).astype(bf16)


def back_kernel(
    width, head, gm, xs, ysum, tot, cin, same, taps, raw, bias, rate, skip, delta_in, run_in, runt_in,
    segc, segr, before, entering, leaving,
    gpad, gtaps, goffs, graw, gheads, dtot, wide,
):
    length = segc.shape[0]
    heads = width // head
    total_width = tot.shape[1]
    states = (total_width - width) // 2
    first = lanes_first(length, head)
    run, runt, delta = run_in[...], runt_in[...], delta_in[...]
    negative = negative_mask(segc[...], segr[...])
    b = silu(tot[:, width : width + states]).astype(bf16)
    c = silu(tot[:, width + states :]).astype(bf16)
    scores = dot(c, b, 1, 1)
    tail = tails(run, segc[...])
    entry = entries(run, segc[...], before[...])
    dscores = jnp.zeros((length, length), f32)
    u = jnp.zeros((length, heads), f32)
    q = jnp.zeros((1, heads), f32)
    vdx = jnp.zeros((length, heads), f32)
    gv = jnp.zeros((1, heads), f32)
    ge = jnp.zeros((1, heads), f32)
    db = jnp.zeros((length, states), f32)
    dc = jnp.zeros((length, states), f32)
    chan = lax.broadcasted_iota(jnp.int32, (2 * head, heads), 0)
    which = lax.broadcasted_iota(jnp.int32, (2 * head, heads), 1)
    for pair in range(heads // 2):
        part = slice(pair * 2 * head, (pair + 1) * 2 * head)
        pick = (which == 2 * pair + (chan >= head).astype(jnp.int32)).astype(f32)
        x = xs[:, part]
        x32 = x.astype(f32)
        g = gm[:, part]
        g32 = g.astype(f32)
        tl = spread_pair(first, tail, pair)
        grad_f = leaving[part, :]
        late = dot(b, grad_f, 1, 1) * tl
        dx = late
        for k in range(2):
            h = 2 * pair + k
            lanes = first if k == 0 else ~first
            gk = jnp.where(lanes, g32, 0.0).astype(bf16)
            decay = jnp.exp(run[:, h : h + 1] - runt[h : h + 1, :] + negative)
            w = (decay * scores).astype(bf16)
            dscores = dscores + decay * dot(gk, x, 1, 1)
            dx = dx + dot(w, gk, 0, 0)
        raw_v = tot[:, part]
        sg = sigmoid(raw_v)
        v = raw_v * sg
        u = u + dot(g32 * ysum[:, part] - x32 * dx, pick, precision=highest)
        q = q + jnp.sum(dot(x32 * late, pick, precision=highest), axis=0, keepdims=True)
        vdx = vdx + dot(v * dx, pick, precision=highest)
        gv = gv + dot(jnp.sum(g32 * v, axis=0, keepdims=True), pick, precision=highest)
        per_row = jnp.sum(grad_f.astype(f32) * entering[part, :].astype(f32), axis=1, keepdims=True)
        ge = ge + jnp.sum(per_row * pick, axis=0, keepdims=True)
        dv = spread_pair(first, delta, pair) * dx + spread_pair(first[:1], skip[...], pair) * g32
        dtot[:, part] = dv * (sg * (1.0 + raw_v * (1.0 - sg)))
        db = db + dot((x32 * tl).astype(bf16), grad_f)
        dc = dc + dot((g32 * spread_pair(first, entry, pair)).astype(bf16), entering[part, :])
    dsb = dscores.astype(bf16)
    dc = dc + dot(dsb, b)
    db = db + dot(dsb, c, 0, 0)
    dtot[:, width : width + states] = db * dsilu(tot[:, width : width + states])
    dtot[:, width + states :] = dc * dsilu(tot[:, width + states :])
    row = lax.broadcasted_iota(jnp.int32, (length, length), 0)
    col = lax.broadcasted_iota(jnp.int32, (length, length), 1)
    above = (row <= col).astype(f32)
    last = slice(length - 1, length)
    dld = dot(above, u, precision=highest) + (q + entry[last, :] * ge)
    ddelta = dld * rate[...] + vdx
    gr = ddelta * sigmoid(raw[...] + bias[...])
    graw[...] = gr
    gheads[...] = jnp.zeros_like(gheads)
    gheads[0:1, :] = jnp.sum(gr, axis=0, keepdims=True)
    gheads[1:2, :] = jnp.sum(dld * delta, axis=0, keepdims=True) * rate[...]
    gheads[2:3, :] = gv
    wide[...] = cin[...].astype(f32)
    gpad[...] = jnp.zeros_like(gpad)
    lags = taps.shape[0]
    pad = cin.shape[0] - length
    for n in range(total_width // 128):
        part = slice(n * 128, n * 128 + 128)
        d = dtot[:, part]
        goffs[:, part] = jnp.sum(d, axis=0, keepdims=True)
        for j in range(lags):
            ds = d * same[:, j : j + 1]
            window = slice(pad - j, pad - j + length)
            gtaps[j : j + 1, part] = jnp.sum(ds * wide[window, part], axis=0, keepdims=True)
            gpad[window, part] = gpad[window, part] + ds * taps[j : j + 1, part]


def call(kernel, outs, args, scratch=(), name=None):
    return pl.pallas_call(
        kernel,
        out_shape=tuple(jax.ShapeDtypeStruct(s, d) for s, d in outs),
        in_specs=[VM] * len(args),
        out_specs=tuple([VM] * len(outs)),
        scratch_shapes=list(scratch),
        compiler_params=pltpu.CompilerParams(vmem_limit_bytes=LIMIT),
        name=name,
    )(*args)


def body(
    hidden,
    segment_ids,
    cotangent,
    input_gain,
    gate_weight,
    value_weight,
    state_weight,
    step_weight,
    conv_weight,
    conv_bias,
    step_bias,
    decay_log,
    skip_gain,
    mixer_gain,
    out_weight,
):
    tokens = hidden[0]
    wrapped = segment_ids[0] % 128
    cot = cotangent[0]
    length, width_in = tokens.shape
    shard = lax.axis_index("tensor")
    shards = lax.axis_size("tensor")
    lags = conv_weight.shape[0]
    reach = lags - 1
    dp = lax.axis_size("dp")
    width = gate_weight.shape[1]
    local_heads = step_weight.shape[1]
    head = width // local_heads
    inner = width * shards
    states = state_weight.shape[1] // 2
    ids_col = jnp.broadcast_to(wrapped[length - reach :].astype(bf16)[:, None], (reach, 128))
    edge = shifted(jnp.concatenate([tokens[length - reach :], ids_col], 1), "ctx", 1)
    narrow = jnp.concatenate(
        [state_weight, step_weight, jnp.zeros((state_weight.shape[0], 128 - local_heads), bf16)], 1
    )
    g_gate, g_value, g_narrow, g_out = gather(
        (gate_weight, value_weight, narrow, out_weight), "dp", 0
    )
    full_gate = g_gate.reshape(width_in, width)
    full_value = g_value.reshape(width_in, width)
    full_narrow = g_narrow.reshape(width_in, narrow.shape[1])
    full_out = jnp.concatenate([g_out[k] for k in range(dp)], 1)
    pad = 8
    base_ext = jnp.concatenate(
        [jnp.zeros((pad - reach, width_in), bf16), edge[:, :width_in], tokens], 0
    ).astype(f32)
    inv_ext = lax.rsqrt(jnp.mean(base_ext * base_ext, axis=-1, keepdims=True) + epsilon)
    normed_ext = (base_ext * inv_ext * input_gain).astype(bf16)
    normed = normed_ext[pad:]
    base = tokens.astype(f32)
    inv = inv_ext[pad:]
    gate = jnp.dot(normed, full_gate, preferred_element_type=f32)
    value_pre = jnp.dot(normed_ext, full_value, preferred_element_type=f32)
    rest_pre = jnp.dot(normed_ext, full_narrow, preferred_element_type=f32)
    cin = jnp.concatenate([value_pre.astype(bf16), rest_pre[:, : 2 * states].astype(bf16)], 1)
    raw_step = rest_pre[pad:, 2 * states : 2 * states + local_heads]
    grad_gated = jnp.dot(cot, full_out.T, preferred_element_type=f32)

    padded_ids = jnp.concatenate([edge[:, width_in].astype(jnp.int32), wrapped])
    before = padded_ids[reach - 1].astype(f32).reshape(1, 1)
    same = jnp.stack(
        [
            (padded_ids[reach - j : reach - j + length] == wrapped).astype(f32)
            for j in range(lags)
        ],
        1,
    )
    segc = wrapped.astype(f32)[:, None]
    segr = wrapped.astype(f32)[None, :]

    def local(array, size):
        return lax.dynamic_slice_in_dim(array, shard * size, size, array.ndim - 1)

    taps = jnp.concatenate([local(conv_weight, width), conv_weight[:, inner:]], 1)
    offs = jnp.concatenate([local(conv_bias, width), conv_bias[inner:]], 0)[None]
    bias = local(step_bias, local_heads)[None]
    rate = -jnp.exp(local(decay_log, local_heads))[None]
    skip = local(skip_gain, local_heads)[None]
    gain = local(mixer_gain, width)[None]
    total_width = width + 2 * states

    tot, intra, xs, final, delta, run, runt = call(
        partial(local_kernel, width, head),
        (
            ((length, total_width), f32),
            ((length, width), f32),
            ((length, width), bf16),
            ((width, states), bf16),
            ((length, local_heads), f32),
            ((length, local_heads), f32),
            ((local_heads, length), f32),
        ),
        (cin, same, taps, offs, raw_step, bias, rate, segc, segr),
        (pltpu.VMEM((length + pad, total_width), f32),),
        "mixer_local",
    )
    through = jnp.exp(run[length - 1]) * (segc[length - 1] == before[0]).astype(f32)
    fade = jnp.broadcast_to(jnp.repeat(through, head)[:, None], (width, 128))
    entering = chain(final, fade, "ctx", 1, 1)
    ctot = tot[:, width + states :]
    ysum, sums = call(
        partial(product_kernel, width, head, inner),
        (((length, width), f32), ((length, 128), f32)),
        (ctot, tot, intra, entering, run, segc, before, gate, grad_gated, gain, skip),
        (),
        "mixer_product",
    )
    sums = pair_sum(sums, "tensor", 2)
    gated, low_gate, gm, grad_entering, grad_mgain = call(
        partial(norm_kernel, width, head, inner),
        (
            ((length, width), bf16),
            ((length, width), bf16),
            ((length, width), bf16),
            ((width, states), bf16),
            ((1, width), f32),
        ),
        (ctot, tot, ysum, run, segc, before, gate, grad_gated, gain, skip, sums),
        (),
        "mixer_norm",
    )
    grad_out = jnp.dot(gated.T, cot, preferred_element_type=f32).astype(bf16)
    grad_gate_w = jnp.dot(normed.T, low_gate, preferred_element_type=f32).astype(bf16)
    out_piece = lax.psum_scatter(grad_out, "dp", scatter_dimension=1, tiled=True)
    gate_piece = lax.psum_scatter(grad_gate_w, "dp", scatter_dimension=0, tiled=True)
    leaving = chain(grad_entering, fade, "ctx", -1, 3)
    gpad, gtaps, goffs, graw, gheads = call(
        partial(back_kernel, width, head),
        (
            ((length + pad, total_width), f32),
            ((lags, total_width), f32),
            ((1, total_width), f32),
            ((length, local_heads), f32),
            ((8, local_heads), f32),
        ),
        (
            gm, xs, ysum, tot, cin, same, taps, raw_step, bias, rate, skip, delta, run, runt,
            segc, segr, before, entering, leaving,
        ),
        (pltpu.VMEM((length, total_width), f32), pltpu.VMEM((length + pad, total_width), f32)),
        "mixer_back",
    )
    edge_grad = shifted(gpad[pad - reach : pad], "ctx", -1)
    grad_input = jnp.concatenate(
        [gpad[pad : pad + length - 8], gpad[pad + length - 8 :] + jnp.pad(edge_grad, ((8 - reach, 0), (0, 0)))], 0
    )
    low_value = grad_input[:, :width].astype(bf16)
    low_rest = jnp.concatenate(
        [
            grad_input[:, width:].astype(bf16),
            graw.astype(bf16),
            jnp.zeros((length, 128 - local_heads), bf16),
        ],
        1,
    )
    low_tail = jnp.concatenate([low_value, low_rest], 1)
    grad_tail_w = jnp.dot(normed.T, low_tail, preferred_element_type=f32).astype(bf16)
    tail_piece = lax.psum_scatter(grad_tail_w, "dp", scatter_dimension=0, tiled=True)
    branch_out = jnp.dot(gated, full_out, preferred_element_type=f32).astype(bf16)
    normed_part = (
        jnp.dot(low_gate, full_gate.T, preferred_element_type=f32)
        + jnp.dot(low_value, full_value.T, preferred_element_type=f32)
        + jnp.dot(low_rest, full_narrow.T, preferred_element_type=f32)
    ).astype(bf16)
    both = pair_sum(jnp.concatenate([branch_out, normed_part], 0), "tensor", 4)
    result = (base + both[:length]).astype(bf16)
    gn = both[length:]
    grad_gain = jnp.sum(gn * base * inv, axis=0)
    gs = gn * input_gain
    grad_base = inv * (gs - base * (inv * inv) * jnp.mean(gs * base, axis=-1, keepdims=True))
    grad_tokens = cot.astype(f32) + grad_base

    out_sum = lax.psum(out_piece, "ctx").astype(f32)
    gate_sum = lax.psum(gate_piece, "ctx").astype(f32)
    tail_sum = lax.psum(tail_piece, "ctx")
    state_sum = pair_sum(tail_sum[:, width : width + 2 * states], "tensor", 5)

    mine = (shard == 0).astype(f32)

    def placed(array, size):
        spots = [jnp.where(shard == k, array, 0.0) for k in range(shards)]
        return jnp.concatenate(spots, -1)

    small = jnp.concatenate(
        [
            (grad_gain * mine)[None],
            jnp.concatenate([placed(gtaps[:, :width], width), gtaps[:, width:]], 1).reshape(1, -1),
            jnp.concatenate([placed(goffs[:, :width], width), goffs[:, width:]], 1),
            placed(grad_mgain, width),
            placed(gheads[0:1], local_heads),
            placed(gheads[1:2], local_heads),
            placed(gheads[2:3], local_heads),
        ],
        1,
    )
    sizes = [width_in, lags * (inner + 2 * states), inner + 2 * states, inner]
    sizes = sizes + [local_heads * shards] * 3
    totals = lax.psum(small, ("dp", "ctx", "tensor"))[0]
    parts, at = [], 0
    for size in sizes:
        parts.append(totals[at : at + size])
        at += size
    return (
        result[None],
        grad_tokens[None],
        parts[0],
        gate_sum,
        tail_sum[:, :width].astype(f32),
        state_sum,
        tail_sum[:, width + 2 * states : width + 2 * states + local_heads].astype(f32),
        parts[1].reshape(lags, inner + 2 * states),
        parts[2],
        parts[4],
        parts[5],
        parts[6],
        parts[3],
        out_sum,
    )


def rot(me, k, size):
    return lax.rem(me + k + size, size)


def remote(src, dst, send, recv, device):
    return pltpu.make_async_remote_copy(
        src_ref=src, dst_ref=dst, send_sem=send, recv_sem=recv, device_id=device, device_id_type=MESH
    )


def greet(barrier, device):
    pl.semaphore_signal(barrier, inc=1, device_id=device, device_id_type=MESH)


def spot(index, size):
    return pl.ds(pl.multiple_of(index * size, size), size)


def inside(index, size):
    return (index >= 0) & (index < size)


class Line:
    def __init__(self, own, at, send, recv, onward=None):
        self.own, self.at, self.send, self.recv, self.onward = own, at, send, recv, onward
        self.me, self.size = lax.axis_index("ctx"), lax.axis_size("ctx")

    def hop(self, w, s):
        way = (1, -1)[w]
        block = self.me - way * s
        src = self.own if s == 0 else self.at(block)
        return remote(src, self.at(block), self.send.at[w, s], self.recv.at[w, s], {"ctx": self.me + way})

    def start(self):
        for w, way in enumerate((1, -1)):
            @pl.when(inside(self.me + way, self.size))
            def _(w=w):
                self.hop(w, 0).start()

    def step(self, s):
        for w, way in enumerate((1, -1)):
            block = self.me - way * (s + 1)

            @pl.when(inside(block, self.size))
            def _(w=w, way=way, block=block):
                ref = self.at(block)
                remote(ref, ref, self.send.at[w, s], self.recv.at[w, s], {"ctx": self.me - way}).wait_recv()
                if s + 1 < self.size - 1:
                    @pl.when(inside(self.me + way, self.size))
                    def _():
                        self.hop(w, s + 1).start()
                if self.onward is not None:
                    self.onward(block, w, s).start()

    def finish(self):
        for s in range(self.size - 1):
            for w, way in enumerate((1, -1)):
                @pl.when(inside(self.me + way, self.size) & inside(self.me - way * s, self.size))
                def _(w=w, s=s):
                    self.hop(w, s).wait_send()

    def arrived(self):
        for s in range(self.size - 1):
            for w, way in enumerate((1, -1)):
                block = self.me - way * (s + 1)

                @pl.when(inside(block, self.size))
                def _(w=w, s=s, block=block):
                    self.onward(block, w, s).wait()


def greet_line(barrier):
    c, nc = lax.axis_index("ctx"), lax.axis_size("ctx")
    for way in (1, -1):
        @pl.when(inside(c + way, nc))
        def _(way=way):
            greet(barrier, {"ctx": c + way})


class Cast:
    def __init__(self, ref, send, recv):
        self.ref, self.send, self.recv = ref, send, recv
        self.me, self.size = lax.axis_index("ctx"), lax.axis_size("ctx")

    def copy(self, block, k):
        ref = self.ref(block)
        return remote(ref, ref, self.send.at[k - 1], self.recv.at[k - 1], {"ctx": rot(self.me, k, self.size)})

    def start(self):
        for k in range(1, self.size):
            self.copy(self.me, k).start()

    def arrived(self):
        for k in range(1, self.size):
            self.copy(rot(self.me, -k, self.size), k).wait_recv()

    def finish(self):
        for k in range(1, self.size):
            self.copy(self.me, k).wait_send()


class Several:
    def __init__(self, items):
        self.items = items

    def start(self):
        for item in self.items:
            item.start()

    def step(self, i):
        for item in self.items:
            item.step(i)

    def finish(self):
        for item in self.items:
            item.finish()

    def arrived(self):
        for item in self.items:
            item.arrived()


def line_peers():
    c, nc = lax.axis_index("ctx"), lax.axis_size("ctx")
    return (c > 0).astype(jnp.int32) + (c < nc - 1).astype(jnp.int32)


def chunk_masks(segp, at, length, lags):
    segc = segp[at : at + length, 0:1]
    return segc, [(segp[at - j : at - j + length, 0:1] == segc).astype(f32) for j in range(lags)]


def fades(through, pair, head, rows):
    low = lax.broadcasted_iota(jnp.int32, (rows, 1), 0) < head
    return jnp.where(low, through[:, 2 * pair : 2 * pair + 1], through[:, 2 * pair + 1 : 2 * pair + 2])


def scan_chunk(
    k, head, hid, ids, wv, ws, wst, in_gain, hp,
    normed, cin, tot, xs, ysum, ent, delta, run, runt, raw, segp, taps, offs, invs, state,
):
    length = ids.shape[2]
    width = wv.shape[1]
    states = ws.shape[1] // 2
    lags = taps.shape[0]
    pad = 8
    row = lax.broadcasted_iota(jnp.int32, (length, length), 0)
    col = lax.broadcasted_iota(jnp.int32, (length, length), 1)
    below = (row >= col).astype(f32)
    first = lanes_first(length, head)
    bias, rate = hp[0:1, :], hp[1:2, :]
    rows = slice(k * length, (k + 1) * length)
    at = pad + k * length
    base = hid[k].astype(f32)
    inv = lax.rsqrt(jnp.mean(base * base, axis=-1, keepdims=True) + epsilon)
    invs[rows, :] = inv
    nb = (base * inv * in_gain[...]).astype(bf16)
    normed[rows, :] = nb
    cin[at : at + length, :width] = dot(nb, wv[...]).astype(bf16).astype(f32)
    cin[at : at + length, width:] = dot(nb, ws[...]).astype(bf16).astype(f32)
    rawk = dot(nb, wst[...], 1, 1)
    raw[rows, :] = rawk
    segc, same = chunk_masks(segp, at, length, lags)
    segr = ids[k, 0:1, :]
    before = segp[at - 1 : at, 0:1]
    for n in range(cin.shape[1] // 128):
        part = slice(n * 128, n * 128 + 128)
        acc = jnp.broadcast_to(offs[:, part], (length, 128))
        for j in range(lags):
            acc = acc + taps[j : j + 1, part] * (cin[at - j : at - j + length, part] * same[j])
        tot[rows, part] = acc
    dk = softplus(rawk + bias)
    delta[rows, :] = dk
    rk = dot(below, dk * rate, precision=highest)
    run[rows, :] = rk
    rkt = rk.T
    runt[k] = rkt
    b = silu(tot[rows, width : width + states]).astype(bf16)
    cc = silu(tot[rows, width + states :]).astype(bf16)
    scores = dot(cc, b, 1, 1)
    negative = negative_mask(segc, segr)
    tail = tails(rk, segc)
    entry = entries(rk, segc, before)
    through = entry[length - 1 : length, :]
    for pair in range(width // (2 * head)):
        part = slice(pair * 2 * head, (pair + 1) * 2 * head)
        values = silu(tot[rows, part])
        x = (values * spread_pair(first, dk, pair)).astype(bf16)
        xs[rows, part] = x
        x32 = x.astype(f32)
        faded = (x32 * spread_pair(first, tail, pair)).astype(bf16)
        old = state[part, :]
        entering = old.astype(bf16)
        ent[k, part, :] = entering
        state[part, :] = fades(through, pair, head, 2 * head) * old + dot(faded, b, 0, 0)
        y = dot(cc, entering, 1, 1) * spread_pair(first, entry, pair)
        for m in range(2):
            h = 2 * pair + m
            w = (jnp.exp(rk[:, h : h + 1] - rkt[h : h + 1, :] + negative) * scores).astype(bf16)
            xk = jnp.where(first if m == 0 else ~first, x32, 0.0).astype(bf16)
            y = y + dot(w, xk)
        ysum[rows, part] = y


def product_chunk(k, head, length, cf, wo, normed, wg, hp, gain, tot, ysum, gate, gg, sums):
    first = lanes_first(length, head)
    skip = hp[2:3, :]
    rows = slice(k * length, (k + 1) * length)
    gate[rows, :] = dot(normed[rows, :], wg[...])
    gg[rows, :] = dot(cf[k], wo[...], 1, 1)
    squares = jnp.zeros((length, 1), f32)
    project = jnp.zeros((length, 1), f32)
    for pair in range(gate.shape[1] // (2 * head)):
        part = slice(pair * 2 * head, (pair + 1) * 2 * head)
        mixed = ysum[rows, part] + spread_pair(first[:1], skip, pair) * silu(tot[rows, part])
        product = mixed * silu(gate[rows, part])
        squares = squares + jnp.sum(product * product, axis=1, keepdims=True)
        project = project + jnp.sum(gg[rows, part] * gain[:, part] * product, axis=1, keepdims=True)
    lane = lax.broadcasted_iota(jnp.int32, (length, 128), 1)
    both = jnp.where(lane == 0, squares, jnp.where(lane == 1, project, 0.0))
    sums[2 * k : 2 * k + 2, :] = both.T[0:2, :]


def gate_chunk(k, head, inner, length, added, hp, gain, tot, ysum, gate, gg, wo, gated, low_gate, gm, mgain, br):
    first = lanes_first(length, head)
    skip = hp[2:3, :]
    rows = slice(k * length, (k + 1) * length)
    scale = lax.rsqrt(added[:, 2 * k : 2 * k + 1] / inner + epsilon)
    project = scale * added[:, 2 * k + 1 : 2 * k + 2] / inner
    for pair in range(gate.shape[1] // (2 * head)):
        part = slice(pair * 2 * head, (pair + 1) * 2 * head)
        mixed = ysum[rows, part] + spread_pair(first[:1], skip, pair) * silu(tot[rows, part])
        z = gate[rows, part]
        sg = sigmoid(z)
        act = z * sg
        unit = mixed * act * scale
        gated[rows, part] = (unit * gain[:, part]).astype(bf16)
        g = gg[rows, part]
        mgain[:, part] = mgain[:, part] + jnp.sum(g * unit, axis=0, keepdims=True)
        gp = scale * (g * gain[:, part] - unit * project)
        low_gate[rows, part] = (gp * mixed * sg * (1.0 + z * (1.0 - sg))).astype(bf16)
        gm[rows, part] = (gp * act).astype(bf16)
    branch = dot(gated[rows, :], wo[...]).astype(bf16)
    half = length // 2
    br[k, 0] = branch[:half]
    br[k, 1] = branch[half:]


def backward_chunk(
    k, head, gm, xs, ysum, tot, cin, segp, ids, taps, raw, hp, delta_in, run_in, runt_in, ent,
    low_value, low_state, low_step, small, gheads, state, dtot, gpad,
):
    length = ids.shape[2]
    width = gm.shape[1]
    heads = raw.shape[1]
    total_width = tot.shape[1]
    states = (total_width - width) // 2
    lags = taps.shape[0]
    pad = cin.shape[0] - tot.shape[0]
    first = lanes_first(length, head)
    bias, rate, skip = hp[0:1, :], hp[1:2, :], hp[2:3, :]
    chan = lax.broadcasted_iota(jnp.int32, (2 * head, heads), 0)
    which = lax.broadcasted_iota(jnp.int32, (2 * head, heads), 1)
    row = lax.broadcasted_iota(jnp.int32, (length, length), 0)
    col = lax.broadcasted_iota(jnp.int32, (length, length), 1)
    above = (row <= col).astype(f32)
    rows = slice(k * length, (k + 1) * length)
    at = pad + k * length
    segc, same = chunk_masks(segp, at, length, lags)
    segr = ids[k, 0:1, :]
    before = segp[at - 1 : at, 0:1]
    run, runt, delta = run_in[rows, :], runt_in[k], delta_in[rows, :]
    negative = negative_mask(segc, segr)
    b = silu(tot[rows, width : width + states]).astype(bf16)
    c = silu(tot[rows, width + states :]).astype(bf16)
    scores = dot(c, b, 1, 1)
    tail = tails(run, segc)
    entry = entries(run, segc, before)
    through = entry[length - 1 : length, :]
    dscores = jnp.zeros((length, length), f32)
    u = jnp.zeros((length, heads), f32)
    q = jnp.zeros((1, heads), f32)
    vdx = jnp.zeros((length, heads), f32)
    gv = jnp.zeros((1, heads), f32)
    ge = jnp.zeros((1, heads), f32)
    db = jnp.zeros((length, states), f32)
    dc = jnp.zeros((length, states), f32)
    for pair in range(width // (2 * head)):
        part = slice(pair * 2 * head, (pair + 1) * 2 * head)
        pick = (which == 2 * pair + (chan >= head).astype(jnp.int32)).astype(f32)
        x = xs[rows, part]
        x32 = x.astype(f32)
        g32 = gm[rows, part].astype(f32)
        tl = spread_pair(first, tail, pair)
        grad_f32 = state[part, :]
        grad_f = grad_f32.astype(bf16)
        entering = ent[k, part, :]
        late = dot(b, grad_f, 1, 1) * tl
        dx = late
        for m in range(2):
            h = 2 * pair + m
            lanes = first if m == 0 else ~first
            gk = jnp.where(lanes, g32, 0.0).astype(bf16)
            decay = jnp.exp(run[:, h : h + 1] - runt[h : h + 1, :] + negative)
            w = (decay * scores).astype(bf16)
            dscores = dscores + decay * dot(gk, x, 1, 1)
            dx = dx + dot(w, gk, 0, 0)
        raw_v = tot[rows, part]
        sg = sigmoid(raw_v)
        v = raw_v * sg
        u = u + dot(g32 * ysum[rows, part] - x32 * dx, pick, precision=highest)
        q = q + dot(jnp.sum(x32 * late, axis=0, keepdims=True), pick, precision=highest)
        vdx = vdx + dot(v * dx, pick, precision=highest)
        gv = gv + dot(jnp.sum(g32 * v, axis=0, keepdims=True), pick, precision=highest)
        per_row = jnp.sum(grad_f32 * entering.astype(f32), axis=1, keepdims=True)
        ge = ge + jnp.sum(per_row * pick, axis=0, keepdims=True)
        dv = spread_pair(first, delta, pair) * dx + spread_pair(first[:1], skip, pair) * g32
        dtot[:, part] = dv * (sg * (1.0 + raw_v * (1.0 - sg)))
        db = db + dot((x32 * tl).astype(bf16), grad_f)
        scaled = (g32 * spread_pair(first, entry, pair)).astype(bf16)
        dc = dc + dot(scaled, entering)
        state[part, :] = fades(through, pair, head, 2 * head) * grad_f32 + dot(scaled, c, 0, 0)
    dsb = dscores.astype(bf16)
    dc = dc + dot(dsb, b)
    db = db + dot(dsb, c, 0, 0)
    dtot[:, width : width + states] = db * dsilu(tot[rows, width : width + states])
    dtot[:, width + states :] = dc * dsilu(tot[rows, width + states :])
    dld = dot(above, u, precision=highest) + (q + through * ge)
    ddelta = dld * rate + vdx
    gr = ddelta * sigmoid(raw[rows, :] + bias)
    low_step[rows, :] = gr.astype(bf16)
    gheads[0:1, :] = gheads[0:1, :] + jnp.sum(gr, axis=0, keepdims=True)
    gheads[1:2, :] = gheads[1:2, :] + jnp.sum(dld * delta, axis=0, keepdims=True) * rate
    gheads[2:3, :] = gheads[2:3, :] + gv
    for n in range(total_width // 128):
        part = slice(n * 128, n * 128 + 128)
        d = dtot[:, part]
        small[lags : lags + 1, part] = small[lags : lags + 1, part] + jnp.sum(d, axis=0, keepdims=True)
        for j in range(lags):
            ds = d * same[j]
            window = slice(at - j, at - j + length)
            small[j : j + 1, part] = small[j : j + 1, part] + jnp.sum(ds * cin[window, part], axis=0, keepdims=True)
            gpad[window, part] = gpad[window, part] + ds * taps[j : j + 1, part]
    low_value[rows, :] = gpad[at : at + length, :width].astype(bf16)
    low_state[rows, :] = gpad[at : at + length, width:].astype(bf16)


def ranked(slots):
    total = slots[0].astype(f32)
    for r in range(1, slots.shape[0]):
        total = total + slots[r].astype(f32)
    return total


class Shed:
    def __init__(self, own, slot, stage, send, recv):
        self.own, self.slot, self.stage, self.send, self.recv = own, slot, stage, send, recv
        self.me, self.size = lax.axis_index("ctx"), lax.axis_size("ctx")

    def hop(self, w, b):
        way = (1, -1)[w]
        return remote(
            self.stage.at[w, b], self.slot.at[w, b], self.send.at[w, b], self.recv.at[w, b], {"ctx": self.me + way}
        )

    def step(self, i):
        far = self.size - 1 - i
        for w, way in enumerate((1, -1)):
            b = self.me + way * far
            fed = inside(self.me - way, self.size) & inside(b, self.size)

            @pl.when(fed)
            def _(w=w, b=b, way=way):
                ref = self.slot.at[w, b]
                remote(ref, ref, self.send.at[w, b], self.recv.at[w, b], {"ctx": self.me - way}).wait_recv()
                if far:
                    self.stage[w, b] = (self.own[b] + self.slot[w, b].astype(f32)).astype(bf16)
                    self.hop(w, b).start()

            if far:
                @pl.when(jnp.logical_not(inside(self.me - way, self.size)) & inside(b, self.size))
                def _(w=w, b=b):
                    self.stage[w, b] = self.own[b].astype(bf16)
                    self.hop(w, b).start()

    def result(self, ref):
        ref[...] = self.own[self.me]
        for w, way in enumerate((1, -1)):
            @pl.when(inside(self.me - way, self.size))
            def _(w=w):
                ref[...] = ref[...] + self.slot[w, self.me].astype(f32)

    def finish(self):
        for b in range(self.size):
            for w, way in enumerate((1, -1)):
                @pl.when((b - self.me) * way > 0)
                def _(w=w, b=b):
                    self.hop(w, b).wait_send()


def whole_kernel(heads, head, inner, names, *refs):
    r = SimpleNamespace(**dict(zip(names, refs)))
    hid, cot, seg, wg, wv, ws, sw, wo = (r.hid, r.cot, r.seg, r.wg, r.wv, r.ws, r.sw, r.wo)
    H, CF, ids, WG, WV, WS, wst, WO = (r.H, r.CF, r.IDS, r.WG, r.WV, r.WS, r.WST, r.WO)
    in_gain, cw, cb, mg = (r.in_gain, r.cw, r.cb, r.mg)
    out, gh, dg, dv, do, dst, dstate, smalls = (r.out, r.gh, r.dg, r.dv, r.do, r.dst, r.dstate, r.smalls)
    hp, taps, offs, gain, segp, invs = (r.hp, r.taps, r.offs, r.gain, r.segp, r.invs)
    normed, gate, gg, cin, tot, xs, ysum, ent = (r.normed, r.gate, r.gg, r.cin, r.tot, r.xs, r.ysum, r.ent)
    delta, run, runt, raw, sums, state = (r.delta, r.run, r.runt, r.raw, r.sums, r.state)
    gated, low_gate, gm, mgain, br, go, gw = (r.gated, r.low_gate, r.gm, r.mgain, r.br, r.go, r.gw)
    low_value, low_state, low_step, small, gheads, dtot, gpad = (r.low_value, r.low_state, r.low_step, r.small, r.gheads, r.dtot, r.gpad)
    gv, gs, gt, npart, sib_b, sib_n, sib_s, own_b, own_n = (r.gv, r.gs, r.gt, r.npart, r.sib_b, r.sib_n, r.sib_s, r.own_b, r.own_n)
    slot_b, slot_n, stage_b, stage_n = (r.slot_b, r.slot_n, r.stage_b, r.stage_n)
    slot_g, slot_o, slot_v, slot_t, slot_m, slot_s, stage_s, all_s, acc, slot_q = (r.slot_g, r.slot_o, r.slot_v, r.slot_t, r.slot_m, r.slot_s, r.stage_s, r.all_s, r.acc, r.slot_q)
    ps, pr, qs, qr, zs, zr, ds, dr, ss, sr, ms, mr, es, er = (r.ps, r.pr, r.qs, r.qr, r.zs, r.zr, r.ds, r.dr, r.ss, r.sr, r.ms, r.mr, r.es, r.er)
    az, bz, af, bf, ad, bd, aq, bq = (r.az, r.bz, r.af, r.bf, r.ad, r.bd, r.aq, r.bq)
    ai, bi, mo, mp = (r.ai, r.bi, r.mo, r.mp)
    own_ids, own_step = r.own_ids, r.own_step

    c, d, t = lax.axis_index("ctx"), lax.axis_index("dp"), lax.axis_index("tensor")
    nc, nd, nt = lax.axis_size("ctx"), lax.axis_size("dp"), lax.axis_size("tensor")
    total = nc * nt
    me = c * nt + t
    length = ids.shape[2]
    width = WG.shape[2]
    half = br.shape[2]
    wide = slot_o.shape[2]
    lags = cw.shape[0]
    pad = 8
    sib = {"tensor": 1 - t}
    barrier = pltpu.get_barrier_semaphore()

    def peer(k):
        q = rot(me, k, total)
        return q, {"ctx": q // nt, "tensor": lax.rem(q, nt)}

    for k in range(1, nd):
        greet(barrier, {"dp": rot(d, k, nd)})
    for k in range(1, total):
        greet(barrier, peer(k)[1])
    own_ids[...] = jnp.broadcast_to(seg[...].astype(f32), own_ids.shape)
    spots = sw.shape[0]
    pick = lax.broadcasted_iota(jnp.int32, (spots, own_step.shape[0]), 0) - c * heads
    line = lax.broadcasted_iota(jnp.int32, (spots, own_step.shape[0]), 1)
    pick = ((pick == line) & (line < heads)).astype(bf16)
    own_step[...] = dot(pick, sw[...], 0, 0).astype(bf16)
    pl.semaphore_wait(barrier, nd + total - 2)

    def line_of(a, own, to, parts):
        size = half // parts

        def one(n):
            rows = spot(t * parts + n, size)

            def at(block):
                return to.at[block, rows]

            def onward(block, w, s):
                ref = at(block)
                return remote(ref, ref, af.at[a, n, w, s], bf.at[a, n, w, s], sib)

            return Line(own.at[rows], at, az.at[a, n], bz.at[a, n], onward)

        return Several([one(n) for n in range(parts)])

    early_ids = []
    line_h, line_c = line_of(0, hid, H, PARTS), line_of(1, cot, CF, PARTS // 2)
    for k in range(1, nc):
        copy = remote(own_ids, ids.at[c], ai.at[k - 1], bi.at[k - 1], {"ctx": rot(c, k, nc)})
        copy.start()
        early_ids.append(copy)
    line_h.start()
    moves = (
        (wv.at[:, spot(c, width)], lambda q: WV.at[q]),
        (ws, lambda q: WS.at[q]),
        (own_step, lambda q: wst.at[:, spot(q, wide)]),
        (wg.at[:, spot(c, width)], lambda q: WG.at[q]),
        (wo.at[spot(c, width), :], lambda q: WO.at[:, spot(q, wide)]),
    )
    early = list(early_ids)

    def give(a):
        src, to = moves[a]
        for k in range(1, nd):
            early.append(remote(src, to(d), ad.at[a, k - 1], bd.at[a, k - 1], {"dp": rot(d, k, nd)}))
            early[-1].start()

    def given(a):
        for k in range(1, nd):
            q = rot(d, -k, nd)
            ref = moves[a][1](q)
            remote(ref, ref, ad.at[a, k - 1], bd.at[a, k - 1], {"dp": q}).wait_recv()

    for a in range(3):
        give(a)
    H[c] = hid[...]
    CF[c] = cot[...]
    ids[c] = own_ids[...]
    WV[d] = wv[:, spot(c, width)]
    WG[d] = wg[:, spot(c, width)]
    WS[d] = ws[...]
    wst[:, spot(d, wide)] = own_step[...]
    WO[:, spot(d, wide)] = wo[spot(c, width), :]
    first_chan = t * nc + c
    taps[:, :width] = cw[:, spot(first_chan, width)]
    taps[:, width:] = cw[:, inner:]
    for n in range(offs.shape[1] // 128):
        part = slice(n * 128, n * 128 + 128)
        own = n * 128 < width
        at = first_chan * (width // 128) + n if own else inner // 128 + n - width // 128
        offs[:, part] = cb[pl.ds(at, 1), :]
        if own:
            gain[:, part] = mg[pl.ds(at, 1), :]
    lane = lax.broadcasted_iota(jnp.int32, (1, hp.shape[1]), 1)
    for n, source in enumerate((r.bias1, r.decay1, r.skip1)):
        row = jnp.zeros(lane.shape, f32)
        for i in range(heads):
            value = source[first_chan * heads + i]
            row = jnp.where(lane == i, value, row)
        hp[n : n + 1, :] = jnp.where(lane < heads, -jnp.exp(row), 0.0) if n == 1 else row
    cin[:pad, :] = jnp.zeros((pad, cin.shape[1]), f32)
    for ref in (state, gpad, small, gheads, sums, mgain):
        ref[...] = jnp.zeros_like(ref)
    gain_row = r.gain_row
    for n in range(in_gain.shape[0]):
        gain_row[:, n * 128 : n * 128 + 128] = in_gain[n : n + 1, :]
    in_gain = gain_row
    for s in range(nc - 1):
        line_h.step(s)
        if s == max(nc - 3, 0):
            line_c.start()
            give(3)
            give(4)
    for k in range(1, nc):
        q = rot(c, -k, nc)
        remote(own_ids, ids.at[q], ai.at[k - 1], bi.at[k - 1], {"ctx": q}).wait_recv()
    segp[:pad, :] = jnp.full((pad, segp.shape[1]), -1.0, f32)
    for k in range(nc):
        segp[pad + k * length : pad + (k + 1) * length, :] = ids[k].T
    for a in range(3):
        given(a)
    line_h.arrived()
    WGr, WVr, WSr = (ref.reshape(ref.shape[0] * ref.shape[1], ref.shape[2]) for ref in (WG, WV, WS))
    for k in range(nc):
        scan_chunk(
            k, head, H, ids, WVr, WSr, wst, in_gain, hp,
            normed, cin, tot, xs, ysum, ent, delta, run, runt, raw, segp, taps, offs, invs, state,
        )
        if k < nc - 1:
            line_c.step(k)
    given(3)
    given(4)
    line_c.arrived()
    for k in range(nc):
        product_chunk(k, head, length, CF, WO, normed, WGr, hp, gain, tot, ysum, gate, gg, sums)
    slot_q[me] = sums[...]
    for k in range(1, total):
        early.append(remote(sums, slot_q.at[me], aq.at[k - 1], bq.at[k - 1], peer(k)[1]))
        early[-1].start()
    for k in range(1, total):
        q, device = peer(-k)
        remote(sums, slot_q.at[q], aq.at[k - 1], bq.at[k - 1], device).wait_recv()
    added = ranked(slot_q).T
    state[...] = jnp.zeros_like(state)
    sent = []

    def launch(copy):
        copy.start()
        sent.append(copy)

    def swap(a, k, src, dst):
        return remote(src.at[k, 1 - t], dst.at[k], ps.at[a, k], pr.at[a, k], sib)

    def scatter(a, src, slot):
        for k in range(1, nd):
            p = rot(d, k, nd)
            launch(remote(src(p), slot.at[d], ds.at[a, k - 1], dr.at[a, k - 1], {"dp": p}))

    def columns(ref):
        return lambda p: ref.at[:, spot(p, wide)]

    def collected(a, slot):
        for k in range(1, nd):
            r = rot(d, -k, nd)
            remote(slot.at[r], slot.at[r], ds.at[a, k - 1], dr.at[a, k - 1], {"dp": r}).wait_recv()
        return ranked(slot)

    def owned(a, src, other, own):
        for k in range(nc):
            swap(a, k, src, other).wait_recv()
            own[k] = src[k, t].astype(f32) + other[k].astype(f32)

    def place(a, ref, block):
        ref[c] = block.astype(bf16)
        line = Line(ref.at[c], lambda block: ref.at[block], zs.at[a], zr.at[a])
        line.start()
        return line

    for k in range(nc):
        gate_chunk(
            k, head, inner, length, added, hp, gain, tot, ysum, gate, gg, WO, gated, low_gate, gm, mgain, br
        )
        launch(swap(0, k, br, sib_b))
    gw[...] = dot(low_gate[...], normed[...], 0, 0).astype(bf16)
    scatter(0, columns(gw), slot_g)
    cfr = CF.reshape(nc * length, CF.shape[2])
    go[...] = dot(gated[...], cfr[...], 0, 0).astype(bf16)
    scatter(1, columns(go), slot_o)
    slot_g[d] = gw[:, spot(d, wide)]
    slot_o[d] = go[:, spot(d, wide)]

    def shed_of(a, own, slot, stage, parts):
        size = half // parts
        items = []
        for n in range(parts):
            rows = pl.ds(n * size, size)
            views = (own.at[:, rows], slot.at[:, :, rows], stage.at[:, :, rows])
            items.append(Shed(*views, qs.at[a, n], qr.at[a, n]))
            items[-1].rows = rows
        return Several(items)

    def shed_sum(shed):
        for item in shed.items:
            item.result(acc.at[item.rows])

    shed_b = shed_of(0, own_b, slot_b, stage_b, PARTS // 2)
    shed_n = shed_of(1, own_n, slot_n, stage_n, PARTS)
    lines = []

    def begin():
        owned(0, br, sib_b, own_b)
        shed_b.step(0)

    def settle():
        lines.append(place(0, dg, collected(0, slot_g).T))
        lines.append(place(1, do, collected(1, slot_o)))

    def onto(s):
        for item in lines:
            item.step(s)

    tasks = [partial(shed_b.step, 1), settle]
    tasks += [partial(shed_b.step, i) for i in range(2, nc - 1)] + [partial(onto, 0)]
    tasks += [partial(shed_b.step, i) for i in range(max(2, nc - 1), nc)]
    tasks += [partial(onto, i) for i in range(1, nc - 1)]

    def turn(count=1):
        for _ in range(count):
            if tasks:
                tasks.pop(0)()

    begin()
    for i in range(nc):
        backward_chunk(
            nc - 1 - i, head, gm, xs, ysum, tot, cin, segp, ids, taps, raw, hp, delta, run, runt, ent,
            low_value, low_state, low_step, small, gheads, state, dtot, gpad,
        )
        turn((0, 1, 2)[i] if i < 3 else 0)
    gs[...] = dot(low_state[...], normed[...], 0, 0).astype(bf16)
    side = wide // 2

    def cross(p):
        return remote(gs.at[:, spot(2 * p + 1 - t, side)], sib_s.at[p], ps.at[2, p], pr.at[2, p], sib)

    for p in range(nd):
        launch(cross(p))
    gv[...] = dot(low_value[...], normed[...], 0, 0).astype(bf16)
    scatter(2, columns(gv), slot_v)
    gt[...] = dot(low_step[...], normed[...], 0, 0).astype(bf16)
    scatter(3, columns(gt), slot_t)
    turn(1)
    slot_v[d] = gv[:, spot(d, wide)]
    slot_t[d] = gt[:, spot(d, wide)]
    for k in range(nc):
        rows = slice(k * length, (k + 1) * length)
        part = dot(low_gate[rows, :], WGr[...], 1, 1) + dot(low_value[rows, :], WVr[...], 1, 1)
        part = part + dot(low_state[rows, :], WSr[...], 1, 1) + dot(low_step[rows, :], wst[...])
        unit = H[k].astype(f32) * invs[rows, :]
        gained = jnp.sum(part * unit, axis=0, keepdims=True)
        for m in range(gained.shape[1] // small.shape[1]):
            at = lags + 2 + m
            small[at : at + 1, :] = small[at : at + 1, :] + gained[:, m * small.shape[1] : (m + 1) * small.shape[1]]
        part = part.astype(bf16)
        npart[k, 0] = part[:half]
        npart[k, 1] = part[half:]
        launch(swap(1, k, npart, sib_n))
        if k == nc // 2:
            for p in range(nd):
                cross(p).wait_recv()
                stage_s[p] = (gs[:, spot(2 * p + t, side)].astype(f32) + sib_s[p].astype(f32)).astype(bf16)
            for k in range(1, nd):
                p = rot(d, k, nd)
                launch(remote(stage_s.at[p], slot_s.at[d], ss.at[k - 1], sr.at[k - 1], {"dp": p}))
            slot_s[d] = stage_s[d]
    small[lags + 1 : lags + 2, :width] = mgain[...]
    small[small.shape[0] - 8 :, : raw.shape[1]] = gheads[...]
    scatter(4, lambda p: small, slot_m)
    slot_m[d] = small[...]
    late = place(2, dv, collected(2, slot_v).T)
    owned(1, npart, sib_n, own_n)
    shed_n.step(0)

    def cast(a, ref, block):
        ref[c] = block.astype(ref.dtype)
        casts.append(Cast(lambda block: ref.at[block], zs.at[a, 0], zr.at[a, 0]))
        casts[-1].start()

    casts = []
    cast(3, dst, collected(3, slot_t))
    for k in range(1, nd):
        r = rot(d, -k, nd)
        remote(slot_s.at[r], slot_s.at[r], ss.at[k - 1], sr.at[k - 1], {"dp": r}).wait_recv()
    cast(5, all_s, ranked(slot_s))
    smalls[c, t] = collected(4, slot_m)
    casts.append(Cast(lambda block: smalls.at[block, t], zs.at[4, 0], zr.at[4, 0]))
    casts[-1].start()
    ends = [(smalls.at[c, t], smalls.at[c, 1 - t], 3)]
    remote(smalls.at[c, t], smalls.at[c, t], es.at[3], er.at[3], sib).start()
    turn(2)

    def end(ref, e):
        ends.append((ref.at[t], ref.at[1 - t], e))
        remote(ref.at[t], ref.at[t], es.at[e], er.at[e], sib).start()

    rows = spot(t, half)
    base = hid[rows, :].astype(f32)
    for i in range(1, nc):
        shed_n.step(i)
        turn()
        late.step(i - 1)
    shed_sum(shed_b)
    out[t] = (base + acc[...]).astype(bf16)
    end(out, 1)
    shed_sum(shed_n)
    gn = acc[...]
    inv = lax.rsqrt(jnp.mean(base * base, axis=-1, keepdims=True) + epsilon)
    gsx = gn * in_gain[...]
    grad = inv * (gsx - base * (inv * inv) * jnp.mean(gsx * base, axis=-1, keepdims=True))
    gh[t] = cot[rows, :].astype(f32) + grad
    end(gh, 2)
    while tasks:
        turn()
    for item in casts:
        item.arrived()

    def hand(k, mine):
        block = rot(c, -k, nc)
        ref = smalls.at[block, t if mine else 1 - t]
        return remote(ref, ref, mo.at[k - 1], mp.at[k - 1], sib)

    for k in range(1, nc):
        hand(k, True).start()
    dstate[t] = ranked(all_s).T
    end(dstate, 0)
    for item in lines + casts + [late, shed_b, shed_n, line_h, line_c]:
        item.finish()
    for k in range(1, nc):
        hand(k, True).wait_send()
        hand(k, False).wait_recv()
    for copy in early:
        copy.wait_send()
    for copy in sent:
        copy.wait_send()
    for mine, theirs, e in ends:
        remote(mine, mine, es.at[e], er.at[e], sib).wait_send()
        remote(theirs, theirs, es.at[e], er.at[e], sib).wait_recv()


def finish_kernel(
    heads, out_in, gh_in, dg, dv, do, dst, dstate, smalls,
    out, gh, g_in, g_gate, g_value, g_state, g_step, g_conv, g_offs, g_gain, g_out, *g_heads,
):
    nc, nt = smalls.shape[0], smalls.shape[1]
    width = dg.shape[2]
    lags = g_conv.shape[0]
    inner = g_gain.shape[0] * 128
    half = out_in.shape[1]
    side = dstate.shape[1]
    hpad = dst.shape[1]
    headed_shape = (hpad, g_heads[0].shape[1])
    for m in range(2):
        out[m * half : (m + 1) * half, :] = out_in[m]
        gh[m * half : (m + 1) * half, :] = gh_in[m]
        g_state[m * side : (m + 1) * side, :] = dstate[m]
    shared, headed = None, jnp.zeros((8, g_heads[0].shape[1]), f32)
    for k in range(nc):
        part = slice(k * width, (k + 1) * width)
        g_gate[:, part] = dg[k].astype(f32)
        g_value[:, part] = dv[k].astype(f32)
        g_out[part, :] = do[k].astype(f32)
        g_step[k * heads : (k + 1) * heads, :] = dst[k, :, :].astype(f32)[:heads]
        for t in range(nt):
            mine = smalls[k, t]
            at = t * nc + k
            part = slice(at * width, (at + 1) * width)
            g_conv[:, part] = mine[:lags, :width]
            for n in range(width // 128):
                row = slice(at * (width // 128) + n, at * (width // 128) + n + 1)
                g_offs[row, :] = mine[lags : lags + 1, n * 128 : n * 128 + 128]
                g_gain[row, :] = mine[lags + 1 : lags + 2, n * 128 : n * 128 + 128]
            lane = lax.broadcasted_iota(jnp.int32, headed_shape, 1)
            line = lax.broadcasted_iota(jnp.int32, headed_shape, 0)
            pick = ((lane == line + at * heads) & (line < heads)).astype(f32)
            headed = headed + dot(mine[mine.shape[0] - 8 :, :hpad], pick, precision=highest)
            shared = mine if shared is None else shared + mine
    for n, ref in enumerate(g_heads):
        ref[...] = headed[n : n + 1]
    g_conv[:, inner:] = shared[:lags, width:]
    for n in range((shared.shape[1] - width) // 128):
        at = width + n * 128
        row = inner // 128 + n
        g_offs[row : row + 1, :] = shared[lags : lags + 1, at : at + 128]
    each = shared.shape[1] // 128
    for n in range(g_in.shape[0]):
        line = lags + 2 + n // each
        g_in[n : n + 1, :] = shared[line : line + 1, n % each * 128 : n % each * 128 + 128]


def sd(shape, kind):
    return jax.ShapeDtypeStruct(tuple(shape), kind)


def run_kernel(kernel, outs, args, scratch=(), name=None, ident=None):
    extra = {} if ident is None else dict(collective_id=ident, has_side_effects=True)
    return pl.pallas_call(
        kernel,
        out_shape=tuple(sd(s, k) for s, k in outs),
        in_specs=[VM] * len(args),
        out_specs=tuple([VM] * len(outs)),
        scratch_shapes=list(scratch),
        compiler_params=pltpu.CompilerParams(vmem_limit_bytes=LIMIT, **extra),
        name=name,
    )(*args)


def sems(*shape):
    return pltpu.SemaphoreType.DMA(shape)


def spread_body(
    hidden, segment_ids, cotangent, input_gain, gate_weight, value_weight, state_weight, step_weight,
    conv_weight, conv_bias, step_bias, decay_log, skip_gain, mixer_gain, out_weight,
):
    tokens, cot = hidden[0], cotangent[0]
    length, D = tokens.shape
    c, t = lax.axis_index("ctx"), lax.axis_index("tensor")
    nc, nd, nt = lax.axis_size("ctx"), lax.axis_size("dp"), lax.axis_size("tensor")
    width = gate_weight.shape[1] // nc
    inner = width * nc * nt
    heads_all = step_bias.shape[0]
    heads = heads_all // (nc * nt)
    hpad = 16 * ((heads + 15) // 16)
    head = width // heads
    states = state_weight.shape[1] // 2
    W = width + 2 * states
    T = length * nc
    rows = D // nd
    lags = conv_weight.shape[0]
    total = nc * nt
    half = length // 2
    shalf = rows // 2
    srows = 8 * ((2 * nc + 7) // 8)
    srow = 8 * ((lags + 2 + D // W + 7) // 8) + 8
    ins = dict(
        hid=tokens, cot=cot, seg=segment_ids, wg=gate_weight, wv=value_weight, ws=state_weight,
        sw=step_weight.T, wo=out_weight, in_gain=input_gain.reshape(-1, 128), cw=conv_weight,
        cb=conv_bias.reshape(-1, 128), mg=mixer_gain.reshape(-1, 128),
        bias1=step_bias, decay1=decay_log, skip1=skip_gain,
    )
    outs = dict(
        out=((2, half, D), bf16), gh=((2, half, D), f32), dg=((nc, rows, width), bf16),
        dv=((nc, rows, width), bf16), do=((nc, width, rows), bf16), dst=((nc, hpad, rows), bf16),
        dstate=((2, shalf, 2 * states), f32), smalls=((nc, nt, srow, W), f32),
    )
    rooms = dict(
        H=((nc, length, D), bf16), CF=((nc, length, D), bf16), IDS=((nc, 8, length), f32),
        WG=((nd, rows, width), bf16), WV=((nd, rows, width), bf16), WS=((nd, rows, 2 * states), bf16),
        WST=((hpad, D), bf16), WO=((width, D), bf16), own_ids=((8, length), f32),
        own_step=((hpad, rows), bf16), hp=((8, hpad), f32), taps=((lags, W), f32), offs=((1, W), f32),
        gain=((1, width), f32), gain_row=((1, D), f32), segp=((T + 8, 8), f32), invs=((T, 1), f32),
        normed=((T, D), bf16), gate=((T, width), f32), gg=((T, width), f32), cin=((T + 8, W), f32),
        tot=((T, W), f32), xs=((T, width), bf16), ysum=((T, width), f32),
        ent=((nc, width, states), bf16), delta=((T, hpad), f32), run=((T, hpad), f32),
        runt=((nc, hpad, length), f32), raw=((T, hpad), f32), sums=((srows, length), f32),
        state=((width, states), f32), gated=((T, width), bf16), low_gate=((T, width), bf16),
        gm=((T, width), bf16), mgain=((1, width), f32), br=((nc, 2, half, D), bf16),
        go=((width, D), bf16), gw=((width, D), bf16), low_value=((T, width), bf16),
        low_state=((T, 2 * states), bf16), low_step=((T, hpad), bf16), small=((srow, W), f32),
        gheads=((8, hpad), f32), dtot=((length, W), f32), gpad=((T + 8, W), f32),
        gv=((width, D), bf16), gs=((2 * states, D), bf16), gt=((hpad, D), bf16),
        npart=((nc, 2, half, D), bf16), sib_b=((nc, half, D), bf16), sib_n=((nc, half, D), bf16),
        sib_s=((nd, 2 * states, shalf), bf16), own_b=((nc, half, D), f32), own_n=((nc, half, D), f32),
        slot_b=((2, nc, half, D), bf16), slot_n=((2, nc, half, D), bf16),
        stage_b=((2, nc, half, D), bf16), stage_n=((2, nc, half, D), bf16),
        slot_g=((nd, width, rows), bf16), slot_o=((nd, width, rows), bf16),
        slot_v=((nd, width, rows), bf16), slot_t=((nd, hpad, rows), bf16), slot_m=((nd, srow, W), f32),
        slot_s=((nd, 2 * states, shalf), bf16), stage_s=((nd, 2 * states, shalf), bf16),
        all_s=((nc, 2 * states, shalf), bf16), acc=((half, D), f32), slot_q=((total, srows, length), f32),
    )
    most, hop = max(nc, nd), nc - 1
    flags = dict(
        ps=(3, most), pr=(3, most), qs=(2, PARTS, 2, nc), qr=(2, PARTS, 2, nc), zs=(6, 2, hop), zr=(6, 2, hop),
        ds=(5, nd - 1), dr=(5, nd - 1), ss=(nd - 1,), sr=(nd - 1,), ms=(2, hop), mr=(2, hop),
        es=(4,), er=(4,), az=(2, PARTS, 2, hop), bz=(2, PARTS, 2, hop), af=(2, PARTS, 2, hop), bf=(2, PARTS, 2, hop),
        ai=(hop,), bi=(hop,), mo=(hop,), mp=(hop,),
        ad=(5, nd - 1), bd=(5, nd - 1), aq=(total - 1,), bq=(total - 1,),
    )
    scalars = pl.BlockSpec(memory_space=pltpu.SMEM)
    names = tuple(ins) + tuple(outs) + tuple(rooms) + tuple(flags)
    made = pl.pallas_call(
        partial(whole_kernel, heads, head, inner, names),
        out_shape=tuple(sd(*v) for v in outs.values()),
        in_specs=[scalars if n.endswith("1") else VM for n in ins],
        out_specs=tuple([VM] * len(outs)),
        scratch_shapes=[pltpu.VMEM(*v) for v in rooms.values()] + [sems(*v) for v in flags.values()],
        compiler_params=pltpu.CompilerParams(vmem_limit_bytes=FULL, collective_id=0, has_side_effects=True),
        name="whole",
    )(*ins.values())
    outs = run_kernel(
        partial(finish_kernel, heads),
        (
            ((length, D), bf16), ((length, D), f32), ((D // 128, 128), f32), ((rows, nc * width), f32),
            ((rows, nc * width), f32), ((rows, 2 * states), f32), ((nc * heads, rows), f32),
            ((lags, inner + 2 * states), f32), (((inner + 2 * states) // 128, 128), f32),
            ((inner // 128, 128), f32), ((nc * width, rows), f32),
        )
        + (((1, heads_all), f32),) * 3,
        made,
        (),
        "finish",
    )
    out, gh, g_in, g_gate, g_value, g_state, g_step, g_conv, g_offs, g_gain, g_out, *g_heads = outs
    return (
        out[None], gh[None], g_in.reshape(-1), g_gate, g_value, g_state, g_step.T, g_conv, g_offs.reshape(-1),
        *(v.reshape(-1) for v in g_heads), g_gain.reshape(-1), g_out,
    )


def fits(mesh, args):
    nc, nd, nt = mesh.shape["ctx"], mesh.shape["dp"], mesh.shape["tensor"]
    hidden, gate_weight, state_weight, step_bias = args[0], args[4], args[6], args[10]
    seqs, tokens, D = hidden.shape
    inner, heads = gate_weight.shape[1], step_bias.shape[0]
    groups = nc * nt
    if nt != 2 or seqs != nd or heads % (2 * groups) or inner % (128 * groups):
        return False
    length = tokens // nc
    states = state_weight.shape[1]
    if D % (256 * nd) or D % (inner // groups + states) or nc % 2:
        return False
    return tokens * (D + inner // groups) <= 2 << 20 and length % 128 == 0


def solution(mesh):
    in_specs = (
        P("dp", "ctx", None),
        P("dp", "ctx"),
        P("dp", "ctx", None),
        P(),
        P("dp", "tensor"),
        P("dp", "tensor"),
        P("dp", None),
        P("dp", "tensor"),
        P(),
        P(),
        P(),
        P(),
        P(),
        P(),
        P("tensor", "dp"),
    )
    out_specs = (
        P("dp", "ctx", None),
        P("dp", "ctx", None),
        P(),
        P("dp", "tensor"),
        P("dp", "tensor"),
        P("dp", None),
        P("dp", "tensor"),
        P(),
        P(),
        P(),
        P(),
        P(),
        P(),
        P("tensor", "dp"),
    )

    def whole(*args):
        chosen = spread_body if fits(mesh, args) else body
        return jax.shard_map(chosen, mesh=mesh, in_specs=in_specs, out_specs=out_specs, check_vma=False)(*args)

    return whole
```
